32 devices in a mesh: group: 2 (over x), frame: 4 (over y, core), strip: 4 (over z).
Axes of the slice: x: 2, y: 2, z: 4, core: 2. Of those that a mesh axis runs over, the one named last changes fastest.
Arguments:
- spatial_queries: bfloat16 [32, 1024, 576], P(('group', 'frame'), 'strip'), parts along dimension 0, may hold values from -6 to 6
- spatial_keys: bfloat16 [32, 1024, 576], P(('group', 'frame'), 'strip'), parts along dimension 0, may hold values from -6 to 6
- spatial_values: bfloat16 [32, 1024, 576], P(('group', 'frame'), 'strip'), parts along dimension 0, may hold values from -6 to 6
- hidden: bfloat16 [32, 1024, 1152], P(('group', 'frame'), 'strip'), parts along dimension 0, may hold values from -6 to 6
- spatial_out_weight: bfloat16 [576, 1152], replicated, may hold values from -0.25 to 0.25
- spatial_gain: float32 [1152], replicated, may hold values from 0.5 to 1.5
- temporal_qkv_weight: bfloat16 [1152, 1728], replicated, may hold values from -0.1875 to 0.1875
- temporal_out_weight: bfloat16 [576, 1152], replicated, may hold values from -0.25 to 0.25
- temporal_gain: float32 [1152], replicated, may hold values from 0.5 to 1.5
- tile_list: int32 [32, 8, 3], P(('group', 'frame'), 'strip'), parts along dimension 0, may hold values from 0 to 7, as said below
- tile_count: int32 [32, 8], P(('group', 'frame'), 'strip'), parts along dimension 0, may hold values from 1 to 3, as said below
Outputs:
- block_out: bfloat16 [32, 1024, 1152], P(('group', 'frame'), 'strip'), parts along dimension 0
The draws below stay inside these ranges and needn't reach their ends.
There are 2 independent parts, one for each index of `group`. The reference program is written for one: setup_inputs(seed, part) draws one part's arguments, and reference() takes and returns one part's arrays. A program takes and returns all parts, laid end to end along the dimension named above; an argument that names none is the same for every part. Nothing has to cross between parts.
Inputs may be any that keep to these rules, and one draw needn't show every extreme that they name: `tile_list`: entry 0 of a query tile's row is the query tile itself; the 3 entries of a row are distinct tiles, each in the query tile's own strip of 2 tiles or the nearest tile of an adjacent strip of the same frame. In frame 0, the first tile of every strip but the first attends the tile just below it, and the last tile of every strip but the last attends the tile just above it. `tile_count`: some query tile has 3 in every draw.
All inputs are finite; a program needn't handle non-finite values.
Results may differ from the reference program's by a relative error of at most 0.0083.
Values may be sent and summed in bfloat16 or wider, within the bound.
No kernel may reach another device: no remote copies, remote signals or barrier semaphores. Data moves between devices by JAX's collectives and lax.ppermute only.
A program may use at most 128 MiB of HBM per device.

```python
import jax
import jax.numpy as jnp
from jax import lax

D = 1152
HEAD_DIM = 72
HEADS = 8
TILE = 128
TILES_DEV = 2
MAXT = 3
HD = 576
P_SIZE = 1024
PT = 8
FRAMES = 16


def tile_plan(key):
    base_key = jax.random.fold_in(key, 4242)
    level_key, forced_key, count_key, ranking_key = jax.random.split(base_key, 4)
    strips = PT // TILES_DEV
    forced = jax.random.randint(forced_key, (), 0, strips)
    busy_strip = (jax.random.randint(level_key, (strips,), 0, 4) == 0) | (jnp.arange(strips) == forced)
    tile_strip = jnp.arange(PT) // TILES_DEV
    busy_tile = busy_strip[tile_strip]
    coin_flip = jax.random.randint(count_key, (FRAMES, PT), 0, 2)
    counts = jnp.where(busy_tile[None, :], MAXT - 1 + coin_flip, 1)
    span = TILES_DEV + 2
    own_tile = jnp.arange(PT)
    candidates = tile_strip[:, None] * TILES_DEV - 1 + jnp.arange(span)[None, :]
    usable = (candidates >= 0) & (candidates < PT) & (candidates != own_tile[:, None])
    ranks = jax.random.randint(ranking_key, (FRAMES, PT, span), 0, 1024) * span + jnp.arange(span)
    ranks = ranks + jnp.where(usable[None, :, :], 0, 1 << 24)
    ranking = jnp.argsort(ranks, axis=-1, stable=True)
    broad = jnp.broadcast_to(candidates[None, :, :], (FRAMES, PT, span))
    chosen = jnp.take_along_axis(broad, ranking[:, :, :MAXT - 1], axis=-1)
    position = own_tile % TILES_DEV
    lower_edge = (position == 0) & (own_tile > 0)
    upper_edge = (position == TILES_DEV - 1) & (own_tile < PT - 1)
    edge_tile = lower_edge | upper_edge
    wanted = jnp.where(lower_edge, own_tile - 1, own_tile + 1)
    old_first = chosen[0, :, 0]
    new_first = jnp.where(edge_tile, wanted, old_first)
    frame_rows = [new_first[:, None]]
    if MAXT > 2:
        old_second = chosen[0, :, 1]
        new_second = jnp.where(edge_tile & (old_first != wanted), old_first, old_second)
        frame_rows.append(new_second[:, None])
        if MAXT > 3:
            frame_rows.append(chosen[0, :, 2:])
    frame_zero = jnp.concatenate(frame_rows, axis=-1)
    chosen = chosen.at[0].set(frame_zero)
    counts = counts.at[0].set(jnp.where(edge_tile, jnp.maximum(counts[0], 2), counts[0]))
    counts = counts.at[0, forced * TILES_DEV].set(MAXT)
    first = jnp.broadcast_to(own_tile[None, :, None], (FRAMES, PT, 1))
    tile_rows = jnp.concatenate([first, chosen], axis=-1)
    return (tile_rows.astype(jnp.int32), counts.astype(jnp.int32))


def draw_tile_list(key, part):
    return tile_plan(key)[0]


def draw_tile_count(key, part):
    return tile_plan(key)[1]


def shard_levels(own_key, extent, pieces, smallest, largest):
    def one(dim, blocks):
        heights = jax.random.uniform(jax.random.fold_in(jax.random.fold_in(own_key, 6), dim), (blocks,), jnp.float32, smallest / len(pieces), largest / len(pieces))
        return jnp.repeat(jnp.exp(heights), extent[dim] // blocks).reshape((-1,) + (1,) * (len(extent) - dim - 1))

    level = one(*pieces[0])
    for cut in pieces[1:]:
        level = level * one(*cut)
    return level


def scatter_about(rng, shape, width, reach, pieces=(), dtype=jnp.bfloat16):
    level = shard_levels(rng, shape, pieces, -0.22, 0.18) if pieces else 1.0
    values = jax.random.normal(rng, shape, jnp.float32) * width * level
    return jnp.minimum(jnp.maximum(values, -reach), reach).astype(dtype)


def setup_inputs(seed: int = 0, part: int = 0) -> dict:
    seeds = jax.random.split(jax.random.key(seed), 12)
    part_splits = jax.random.split(jax.random.fold_in(seeds[11], part), 12)
    spatial_queries = scatter_about(part_splits[0], (FRAMES, P_SIZE, HD), 1.0, 6.0, ((0, 4), (1, 4)))
    spatial_keys = scatter_about(part_splits[1], (FRAMES, P_SIZE, HD), 1.0, 6.0, ((0, 4), (1, 4)))
    spatial_values = scatter_about(part_splits[2], (FRAMES, P_SIZE, HD), 1.0, 6.0, ((0, 4), (1, 4)))
    hidden = scatter_about(part_splits[3], (FRAMES, P_SIZE, D), 1.0, 6.0, ((0, 4), (1, 4)))
    spatial_out_weight = scatter_about(seeds[4], (HD, D), HD ** -0.5, 0.25)
    spatial_gain = jnp.clip(1.0 + 0.1 * jax.random.normal(seeds[5], (D,), jnp.float32), 0.5, 1.5)
    temporal_qkv_weight = scatter_about(seeds[6], (D, 3 * HD), D ** -0.5, 0.1875)
    temporal_out_weight = scatter_about(seeds[7], (HD, D), HD ** -0.5, 0.25)
    temporal_gain = jnp.clip(1.0 + 0.1 * jax.random.normal(seeds[8], (D,), jnp.float32), 0.5, 1.5)
    tile_list = draw_tile_list(jax.random.fold_in(jax.random.fold_in(seeds[11], part), 71), part)
    tile_count = draw_tile_count(jax.random.fold_in(jax.random.fold_in(seeds[11], part), 71), part)
    return dict(spatial_queries=spatial_queries, spatial_keys=spatial_keys, spatial_values=spatial_values, hidden=hidden, spatial_out_weight=spatial_out_weight, spatial_gain=spatial_gain, temporal_qkv_weight=temporal_qkv_weight, temporal_out_weight=temporal_out_weight, temporal_gain=temporal_gain, tile_list=tile_list, tile_count=tile_count)


epsilon = 1e-06

def head_norm(values):
    return values * lax.rsqrt(lax.optimization_barrier(jnp.mean(values * values, axis=-1, keepdims=True)) + epsilon)

def row_norm(values, gain):
    return values * lax.rsqrt(lax.optimization_barrier(jnp.mean(values * values, axis=-1, keepdims=True)) + epsilon) * gain

def spatial_frame(operands):
    query_frame, key_frame, value_frame, list_frame, count_frame = operands
    scale = HEAD_DIM ** (-0.5)
    query_tiles = head_norm(query_frame.astype(jnp.float32).reshape(PT, TILE, HEADS, HEAD_DIM)).astype(jnp.bfloat16)
    key_tiles = head_norm(key_frame.astype(jnp.float32).reshape(PT, TILE, HEADS, HEAD_DIM)).astype(jnp.bfloat16)
    value_tiles = value_frame.reshape(PT, TILE, HEADS, HEAD_DIM)
    picked_keys = key_tiles[list_frame]
    picked_values = value_tiles[list_frame]
    scores = jnp.einsum('tqhd,tjkhd->thqjk', query_tiles.astype(jnp.float32), picked_keys.astype(jnp.float32)) * scale
    usable = (jnp.arange(MAXT)[None, :] < count_frame[:, None]).astype(jnp.float32)
    expo = jnp.exp(scores) * usable[:, None, None, :, None]
    total = lax.optimization_barrier(jnp.sum(expo, axis=(3, 4)))
    rounded = expo.astype(jnp.bfloat16)
    numer = jnp.einsum('thqjk,tjkhd->tqhd', rounded.astype(jnp.float32), picked_values.astype(jnp.float32))
    result = numer / jnp.transpose(total, (0, 2, 1))[..., None]
    return result.astype(jnp.bfloat16).reshape(P_SIZE, HD)

def reference(spatial_queries, spatial_keys, spatial_values, hidden, spatial_out_weight, spatial_gain, temporal_qkv_weight, temporal_out_weight, temporal_gain, tile_list, tile_count):
    scale = HEAD_DIM ** (-0.5)
    attended = lax.map(spatial_frame, (spatial_queries, spatial_keys, spatial_values, tile_list, tile_count))
    projected = jnp.dot(attended.reshape(FRAMES * P_SIZE, HD), spatial_out_weight, preferred_element_type=jnp.float32)
    mixed = (hidden.reshape(FRAMES * P_SIZE, D).astype(jnp.float32) + row_norm(projected, spatial_gain)).astype(jnp.bfloat16)
    qkv_rows = jnp.dot(mixed, temporal_qkv_weight, preferred_element_type=jnp.float32)
    temporal_queries = head_norm(qkv_rows[:, :HD].reshape(FRAMES, P_SIZE, HEADS, HEAD_DIM)).astype(jnp.bfloat16)
    temporal_keys = head_norm(qkv_rows[:, HD:2 * HD].reshape(FRAMES, P_SIZE, HEADS, HEAD_DIM)).astype(jnp.bfloat16)
    temporal_values = qkv_rows[:, 2 * HD:].reshape(FRAMES, P_SIZE, HEADS, HEAD_DIM).astype(jnp.bfloat16)
    scores = jnp.einsum('fphd,gphd->phfg', temporal_queries.astype(jnp.float32), temporal_keys.astype(jnp.float32)) * scale
    expo = jnp.exp(scores)
    total = lax.optimization_barrier(jnp.sum(expo, axis=-1))
    rounded = expo.astype(jnp.bfloat16)
    numer = jnp.einsum('phfg,gphd->fphd', rounded.astype(jnp.float32), temporal_values.astype(jnp.float32))
    temporal_attended = (numer / jnp.transpose(total, (2, 0, 1))[..., None]).astype(jnp.bfloat16)
    out_rows = jnp.dot(temporal_attended.reshape(FRAMES * P_SIZE, HD), temporal_out_weight, preferred_element_type=jnp.float32)
    block_out = (mixed.astype(jnp.float32) + row_norm(out_rows, temporal_gain)).astype(jnp.bfloat16)
    return block_out.reshape(FRAMES, P_SIZE, D)
```

```python
import functools
import math

import jax
import jax.numpy as jnp
from jax import lax
from jax.experimental import pallas as pl
from jax.experimental.pallas import tpu as pltpu
from jax.sharding import PartitionSpec as P

HEAD_DIM = 72
HEADS = 8
TILE = 128
MAXT = 3
SUB = 16
EPS = 1e-06
EXP2_SCALE = HEAD_DIM ** -0.5 * math.log2(math.e)

BF = jnp.bfloat16
F32 = jnp.float32


def peer(i, j, n):
    return i ^ j if n & (n - 1) == 0 else (i + j) % n


def vmem(limit):
    return pltpu.CompilerParams(vmem_limit_bytes=limit << 20)


def whole(shape):
    return pl.BlockSpec(shape, lambda *_: (0,) * len(shape))


def contract(a, b, da, db):
    return lax.dot_general(a, b, (((da,), (db,)), ((), ())), preferred_element_type=F32)


def head_scale(x):
    return lax.rsqrt(jnp.mean(x * x, axis=0, keepdims=True) + EPS)


def head(h, base=0):
    return slice(base + h * HEAD_DIM, base + (h + 1) * HEAD_DIM)


def prep_kernel(info, k_ref, v_ref, a_ref, b_ref, scratch):
    width = k_ref.shape[1]
    for h in range(width // HEAD_DIM):
        x = k_ref[0, head(h), :].astype(F32)
        scratch[head(h), :] = (x * head_scale(x)).astype(BF)
    even = info[1] % 2 == 0

    def fill(first, second):
        first[:width, :] = scratch[:, :TILE]
        first[width:, :] = v_ref[0, :, :TILE]
        second[:width, :] = scratch[:, TILE:]
        second[width:, :] = v_ref[0, :, TILE:]

    @pl.when(even)
    def _():
        fill(b_ref, a_ref)

    @pl.when(jnp.logical_not(even))
    def _():
        fill(a_ref, b_ref)


def spatial_kernel(frame, n_groups, info, q_ref, a_ref, b_ref, ra_ref, rb_ref, h_ref, w_ref, g_ref, *rest):
    outs, (kv, att, mix) = rest[:n_groups], rest[n_groups:]
    width, tokens = q_ref.shape[1], q_ref.shape[2]
    tiles = tokens // TILE
    share = tokens // n_groups
    for i, ref in enumerate((a_ref, b_ref, ra_ref, rb_ref)):
        kv[:, i * TILE:(i + 1) * TILE] = ref[...]
    strip = info[1]
    odd = strip % 2
    first = strip * tiles
    places = (first + 1 - odd, first + odd, first + 2 - 3 * odd, first - 1 + 3 * odd)
    frames = info_frames(info, tiles)
    base = 2 + frames * tiles
    masks = []
    for t in range(tiles):
        row = frame * tiles + t
        live = info[2 + row]
        cells = []
        for place in places:
            hit = jnp.bool_(False)
            for j in range(MAXT):
                hit = hit | ((info[base + row * MAXT + j] == place) & (j < live))
            cells.append(jnp.where(hit, 1.0, 0.0).astype(F32))
        masks.append(cells)
    for h in range(width // HEAD_DIM):
        q = q_ref[0, head(h), :].astype(F32)
        qn = (q * (head_scale(q) * EXP2_SCALE)).astype(BF)
        s = contract(kv[head(h), :], qn, 0, 0)
        p = jnp.exp2(s)
        p = jnp.concatenate(
            [
                jnp.concatenate(
                    [
                        p[i * TILE:(i + 1) * TILE, t * TILE:(t + 1) * TILE] * masks[t][i]
                        for t in range(tiles)
                    ],
                    axis=1,
                )
                for i in range(4)
            ],
            axis=0,
        )
        total = jnp.sum(p, axis=0, keepdims=True)
        o = contract(kv[head(h, width), :], p.astype(BF), 1, 0)
        att[head(h), :] = (o / total).astype(BF)
    proj = contract(att[...], w_ref[...], 0, 0)
    scale = lax.rsqrt(jnp.mean(proj * proj, axis=-1, keepdims=True) + EPS)
    mix[...] = (h_ref[0].astype(F32) + proj * scale * g_ref[...]).astype(BF)
    for j, out in enumerate(outs):
        group = peer(info[0], j, n_groups)
        out[...] = mix[pl.ds(pl.multiple_of(group * share, SUB), share), :]


def info_frames(info, tiles):
    return (info.shape[0] - 2) // (tiles * (1 + MAXT))


def rel_order(c, n_groups):
    return [j ^ (c & 1) for j in range(n_groups)] if n_groups % 2 == 0 else list(range(n_groups))


def temporal_kernel(n_groups, frames, *refs):
    n_in = n_groups * frames
    pieces, w_ref = refs[:n_in], refs[n_in]
    outs = refs[n_in + 1:n_in + 1 + n_groups]
    x, qkv, att = refs[n_in + 1 + n_groups:]
    chunks = pieces[0].shape[0] // SUB
    rows = n_in * SUB
    width = w_ref.shape[0] // 3
    row_pos = lax.broadcasted_iota(jnp.int32, (rows, rows), 0) % SUB
    col_pos = lax.broadcasted_iota(jnp.int32, (rows, rows), 1) % SUB
    same = jnp.where(row_pos == col_pos, 1.0, 0.0).astype(F32)
    for c in range(chunks):
        order = rel_order(c, n_groups)
        for slot, j in enumerate(order):
            for f in range(frames):
                at = (slot * frames + f) * SUB
                x[c, at:at + SUB, :] = pieces[j * frames + f][c * SUB:(c + 1) * SUB, :]
        qkv[c] = contract(w_ref[...], x[c], 1, 1)
        for h in range(width // HEAD_DIM):
            q = qkv[c, head(h), :]
            k = qkv[c, head(h, width), :]
            v = qkv[c, head(h, 2 * width), :].astype(BF)
            qn = (q * (head_scale(q) * EXP2_SCALE)).astype(BF)
            kn = (k * head_scale(k)).astype(BF)
            p = jnp.exp2(contract(kn, qn, 0, 0)) * same
            total = jnp.sum(p, axis=0, keepdims=True)
            o = contract(v, p.astype(BF), 1, 0)
            att[c, head(h), :] = (o / total).astype(BF)
    lanes = frames * SUB
    if chunks == 2 and n_groups % 2 == 0:
        low = lax.broadcasted_iota(jnp.int32, (width, 2 * lanes), 1) < lanes
        for m in range(n_groups // 2):
            one = att[0, :, 2 * lanes * m:2 * lanes * (m + 1)]
            two = att[1, :, 2 * lanes * m:2 * lanes * (m + 1)]
            outs[2 * m][...] = jnp.where(low, one, two)
            outs[2 * m + 1][...] = jnp.where(low, two, one)
    else:
        for c in range(chunks):
            for slot, j in enumerate(rel_order(c, n_groups)):
                outs[j][:, c * lanes:(c + 1) * lanes] = att[c, :, slot * lanes:(slot + 1) * lanes]


def output_kernel(n_groups, frames, half, halves, aliased, info, *refs):
    n_in = n_groups * frames
    atts, pieces = refs[:n_groups], refs[n_groups:n_groups + n_in]
    w_ref, g_ref = refs[n_groups + n_in:n_groups + n_in + 2]
    rest = refs[n_groups + n_in + 2 + aliased:]
    out, buf, sems = rest
    rows = pieces[0].shape[0]
    chunks = rows // SUB
    merged = chunks == 2 and n_groups % 2 == 0
    copies = []
    for j in range(n_groups):
        proj = contract(atts[j][...], w_ref[...], 0, 0)
        scale = lax.rsqrt(jnp.mean(proj * proj, axis=-1, keepdims=True) + EPS)
        res = proj * scale * g_ref[...]
        for slot in range(chunks):
            c = slot ^ (j & 1) if merged else slot
            for f in range(frames):
                at = (slot * frames + f) * SUB
                mine = pieces[j * frames + f][c * SUB:(c + 1) * SUB, :].astype(F32)
                buf[j, f, c * SUB:(c + 1) * SUB, :] = (mine + res[at:at + SUB, :]).astype(BF)
        group = peer(info[0], j, n_groups)
        start = pl.multiple_of((group * halves + half) * rows, SUB)
        copy = pltpu.make_async_copy(buf.at[j], out.at[:, pl.ds(start, rows), :], sems.at[j])
        copy.start()
        copies.append(copy)
    for copy in copies:
        copy.wait()


def shards(
    spatial_queries,
    spatial_keys,
    spatial_values,
    hidden,
    spatial_out_weight,
    spatial_gain,
    temporal_qkv_weight,
    temporal_out_weight,
    temporal_gain,
    tile_list,
    tile_count,
):
    frames, tokens, width = spatial_queries.shape
    model = hidden.shape[2]
    groups = lax.axis_size("frame")
    strips = lax.axis_size("strip")
    share = tokens // groups
    halves = 2 if share % (4 * SUB) == 0 else 1
    rows = share // halves
    queries = jnp.transpose(spatial_queries, (0, 2, 1))
    keys = jnp.transpose(spatial_keys, (0, 2, 1))
    values = jnp.transpose(spatial_values, (0, 2, 1))
    qkv_weight = temporal_qkv_weight.T
    gain_one = spatial_gain.reshape(1, model)
    gain_two = temporal_gain.reshape(1, model)
    me, strip = lax.axis_index("frame"), lax.axis_index("strip")
    info = jnp.concatenate(
        [jnp.stack([me, strip]).astype(jnp.int32), tile_count.reshape(-1), tile_list.reshape(-1)]
    )
    near = [(i, i ^ 1) for i in range(strips) if i ^ 1 < strips]
    far = [e for i in range(1, strips - 1, 2) for e in ((i, i + 1), (i + 1, i))]
    edge = jax.ShapeDtypeStruct((2 * width, TILE), BF)

    tiles_out, halos = [], []
    for f in range(frames):
        frame_block = pl.BlockSpec((1, width, tokens), lambda i, _, f=f: (f, 0, 0))
        a, b = pl.pallas_call(
            prep_kernel,
            grid_spec=pltpu.PrefetchScalarGridSpec(
                num_scalar_prefetch=1,
                grid=(1,),
                in_specs=[frame_block, frame_block],
                out_specs=[whole(edge.shape)] * 2,
                scratch_shapes=[pltpu.VMEM((width, tokens), BF)],
            ),
            out_shape=[edge, edge],
            compiler_params=vmem(16),
            name="prep",
        )(info, keys, values)
        tiles_out.append((a, b))
        halos.append((lax.ppermute(a, "strip", near), lax.ppermute(b, "strip", far)))

    mixed = [[None] * frames for _ in range(groups)]
    there = [[None] * frames for _ in range(groups)]
    for f in range(frames):
        frame_block = pl.BlockSpec((1, width, tokens), lambda i, _, f=f: (f, 0, 0))
        row_block = pl.BlockSpec((1, tokens, model), lambda i, _, f=f: (f, 0, 0))
        parts = pl.pallas_call(
            functools.partial(spatial_kernel, f, groups),
            grid_spec=pltpu.PrefetchScalarGridSpec(
                num_scalar_prefetch=1,
                grid=(1,),
                in_specs=[frame_block]
                + [whole(edge.shape)] * 4
                + [row_block, whole((width, model)), whole((1, model))],
                out_specs=[whole((share, model))] * groups,
                scratch_shapes=[
                    pltpu.VMEM((2 * width, 4 * TILE), BF),
                    pltpu.VMEM((width, tokens), BF),
                    pltpu.VMEM((tokens, model), BF),
                ],
            ),
            out_shape=[jax.ShapeDtypeStruct((share, model), BF)] * groups,
            compiler_params=vmem(32),
            name="spatial",
        )(info, queries, *tiles_out[f], *halos[f], hidden, spatial_out_weight, gain_one)
        for j in range(groups):
            mixed[j][f] = parts[j]
            pairs = [(i, peer(i, j, groups)) for i in range(groups)]
            there[j][f] = parts[j] if j == 0 else lax.ppermute(parts[j], "frame", pairs)

    out = None
    returned = []
    chunks = rows // SUB
    lanes = frames * SUB
    block = groups * frames * SUB
    here = [there[j][f] for j in range(groups) for f in range(frames)]
    mine = [mixed[j][f] for j in range(groups) for f in range(frames)]
    for half in range(halves):
        piece = pl.BlockSpec((rows, model), lambda *_, half=half: (half, 0))
        back = pl.pallas_call(
            functools.partial(temporal_kernel, groups, frames),
            grid=(1,),
            in_specs=[piece] * len(here) + [whole((3 * width, model))],
            out_specs=[whole((width, chunks * lanes))] * groups,
            out_shape=[jax.ShapeDtypeStruct((width, chunks * lanes), BF)] * groups,
            scratch_shapes=[
                pltpu.VMEM((chunks, block, model), BF),
                pltpu.VMEM((chunks, 3 * width, block), F32),
                pltpu.VMEM((chunks, width, block), BF),
            ],
            compiler_params=vmem(48),
            name="temporal",
        )(*here, qkv_weight)
        got = []
        for j in range(groups):
            pairs = [(peer(i, j, groups), i) for i in range(groups)]
            got.append(back[j] if j == 0 else lax.ppermute(back[j], "frame", pairs))
        returned.append(got)
    for half in range(halves):
        piece = pl.BlockSpec((rows, model), lambda *_, half=half: (half, 0))
        extra = [] if out is None else [out]
        any_spec = pl.BlockSpec(memory_space=pl.ANY)
        out = pl.pallas_call(
            functools.partial(output_kernel, groups, frames, half, halves, len(extra)),
            grid_spec=pltpu.PrefetchScalarGridSpec(
                num_scalar_prefetch=1,
                grid=(1,),
                in_specs=[whole((width, chunks * lanes))] * groups
                + [piece] * len(mine)
                + [whole((width, model)), whole((1, model))]
                + [any_spec] * len(extra),
                out_specs=any_spec,
                scratch_shapes=[
                    pltpu.VMEM((groups, frames, rows, model), BF),
                    pltpu.SemaphoreType.DMA((groups,)),
                ],
            ),
            out_shape=jax.ShapeDtypeStruct((frames, tokens, model), BF),
            input_output_aliases={1 + groups + len(mine) + 2: 0} if extra else {},
            compiler_params=vmem(32),
            name="output",
        )(info, *returned[half], *mine, temporal_out_weight, gain_two, *extra)
    return out


def solution(mesh):
    rows = P(("group", "frame"), "strip", None)
    placed = (rows, rows, rows, rows, P(), P(), P(), P(), P(), rows, P(("group", "frame"), "strip"))
    return jax.shard_map(shards, mesh=mesh, in_specs=placed, out_specs=rows, check_vma=False)
```

```python
import functools
import math

import jax
import jax.numpy as jnp
from jax import lax
from jax.experimental import pallas as pl
from jax.experimental.pallas import tpu as pltpu
from jax.sharding import PartitionSpec as P

HEAD_DIM = 72
HEADS = 8
TILE = 128
MAXT = 3
SUB = 16
EPS = 1e-06
EXP2_SCALE = HEAD_DIM ** -0.5 * math.log2(math.e)

BF = jnp.bfloat16
F32 = jnp.float32


def peer(i, j, n):
    return i ^ j if n & (n - 1) == 0 else (i + j) % n


def vmem(limit):
    return pltpu.CompilerParams(vmem_limit_bytes=limit << 20)


def whole(shape):
    return pl.BlockSpec(shape, lambda *_: (0,) * len(shape))


def contract(a, b, da, db):
    return lax.dot_general(a, b, (((da,), (db,)), ((), ())), preferred_element_type=F32)


def head_scale(x):
    return lax.rsqrt(jnp.mean(x * x, axis=0, keepdims=True) + EPS)


def head(h, base=0):
    return slice(base + h * HEAD_DIM, base + (h + 1) * HEAD_DIM)


def prep_kernel(place, *refs):
    n = len(refs) // 4
    width = refs[0].shape[1]
    even = place[1] % 2 == 0
    for f in range(n):
        k_ref, v_ref = refs[2 * f:2 * f + 2]
        a_ref, b_ref = refs[2 * n + 2 * f:2 * n + 2 * f + 2]

        def fill(first, second):
            for h in range(width // HEAD_DIM):
                x = k_ref[0, head(h), :].astype(F32)
                y = (x * head_scale(x)).astype(BF)
                first[head(h), :] = y[:, :TILE]
                second[head(h), :] = y[:, TILE:]
            first[width:, :] = v_ref[0, :, :TILE]
            second[width:, :] = v_ref[0, :, TILE:]

        pl.when(even)(functools.partial(fill, b_ref, a_ref))
        pl.when(jnp.logical_not(even))(functools.partial(fill, a_ref, b_ref))


def spatial_kernel(frame, n_groups, place, counts, lists, q_ref, a_ref, b_ref, ra_ref, rb_ref, h_ref, w_ref, g_ref, *rest):
    outs, (att, mix) = rest[:n_groups], rest[n_groups:]
    width, tokens = q_ref.shape[1], q_ref.shape[2]
    tiles = tokens // TILE
    share = tokens // n_groups
    keys = ((a_ref, b_ref), (ra_ref, rb_ref))
    strip = place[1]
    odd = strip % 2
    first = strip * tiles
    places = (first + 1 - odd, first + odd, first + 2 - 3 * odd, first - 1 + 3 * odd)
    masks = []
    for t in range(tiles):
        live = counts[t, frame]
        cells = []
        for spot in places:
            hit = jnp.bool_(False)
            for j in range(MAXT):
                hit = hit | ((lists[j, t, frame] == spot) & (j < live))
            cells.append(jnp.where(hit, 1.0, 0.0).astype(F32))
        masks.append(cells)

    def weigh(s, i):
        return jnp.concatenate(
            [
                jnp.concatenate(
                    [
                        jnp.exp2(s[u * TILE:(u + 1) * TILE, t * TILE:(t + 1) * TILE] * EXP2_SCALE)
                        * masks[t][2 * i + u]
                        for t in range(tiles)
                    ],
                    axis=1,
                )
                for u in range(2)
            ],
            axis=0,
        )

    def side(i, rows):
        return jnp.concatenate([r[rows, :] for r in keys[i]], axis=1)

    for h in range(width // HEAD_DIM):
        q = q_ref[0, head(h), :].astype(F32)
        qn = (q * head_scale(q)).astype(BF)
        s = [contract(side(i, head(h)), qn, 0, 0) for i in range(2)]
        p = [weigh(s[i], i) for i in range(2)]
        total = sum(jnp.sum(x, axis=0, keepdims=True) for x in p)
        o = sum(contract(side(i, head(h, width)), p[i].astype(BF), 1, 0) for i in range(2))
        att[head(h), :] = (o / total).astype(BF)
    proj = contract(att[...], w_ref[...], 0, 0)
    scale = lax.rsqrt(jnp.mean(proj * proj, axis=-1, keepdims=True) + EPS)
    mix[...] = (h_ref[0].astype(F32) + proj * scale * g_ref[...]).astype(BF)
    for j, out in enumerate(outs):
        group = peer(place[0], j, n_groups)
        out[...] = mix[pl.ds(pl.multiple_of(group * share, SUB), share), :]


def paired(chunks, lanes, frames):
    return chunks % 2 == 0 and frames % 2 == 0 and 2 * lanes == TILE


def project_kernel(frame, frames, *refs):
    pieces, w_ref, out, x = refs[:-3], refs[-3], refs[-2], refs[-1]
    n_groups = len(pieces)
    chunks = pieces[0].shape[0] // SUB
    swap = frame & 1 if paired(chunks, n_groups * SUB, frames) else 0
    for c in range(chunks):
        for j, piece in enumerate(pieces):
            at = ((c ^ swap) * n_groups + j) * SUB
            x[at:at + SUB, :] = piece[c * SUB:(c + 1) * SUB, :]
    width = w_ref.shape[0] // 3
    cut = w_ref.shape[0] // 2
    heads = width // HEAD_DIM
    parts = [contract(w_ref[i * cut:(i + 1) * cut, :], x[...], 1, 1) for i in range(2)]
    for h in range(3 * heads):
        i, at = divmod(h * HEAD_DIM, cut)
        y = parts[i][at:at + HEAD_DIM, :]
        if h < 2 * heads:
            y = y * head_scale(y)
        out[head(h), :] = y.astype(BF)


def temporal_kernel(n_groups, *refs):
    frames = len(refs) - n_groups - 1
    ins, outs, att = refs[:frames], refs[frames:frames + n_groups], refs[-1]
    lanes = n_groups * SUB
    chunks = ins[0].shape[1] // lanes
    width = ins[0].shape[0] // 3
    rows = frames * lanes
    pair = paired(chunks, lanes, frames)
    row_pos = lax.broadcasted_iota(jnp.int32, (rows, rows), 0) % SUB
    col_pos = lax.broadcasted_iota(jnp.int32, (rows, rows), 1) % SUB
    same = jnp.where(row_pos == col_pos, 1.0, 0.0).astype(F32)
    low = lax.broadcasted_iota(jnp.int32, (HEAD_DIM, TILE), 1) < lanes

    def take(c, where):
        if not pair:
            return jnp.concatenate([r[where, c * lanes:(c + 1) * lanes] for r in ins], axis=1)
        tile = slice(c // 2 * TILE, (c // 2 + 1) * TILE)
        got = [r[where, tile] for r in ins]
        return jnp.concatenate(
            [
                jnp.where(low, got[m + (c & 1)], got[m + 1 - (c & 1)])
                for m in range(0, frames, 2)
            ],
            axis=1,
        )

    for c in range(chunks):
        heads = range(width // HEAD_DIM)
        for h0 in heads[::2]:
            two = heads[h0:h0 + 2]
            s = [contract(take(c, head(h, width)), take(c, head(h)), 0, 0) for h in two]
            p = [jnp.exp2(x * EXP2_SCALE) * same for x in s]
            o = [contract(take(c, head(h, 2 * width)), x.astype(BF), 1, 0) for h, x in zip(two, p)]
            for h, x, y in zip(two, p, o):
                att[c, head(h), :] = y / jnp.sum(x, axis=0, keepdims=True)
    turned = [att[c].T.astype(BF) for c in range(chunks)]
    for j, out in enumerate(outs):
        for c in range(chunks):
            for f in range(frames):
                slot = f ^ (c & 1) if pair else f
                at = slot * lanes + j * SUB
                out[c * SUB:(c + 1) * SUB, f * width:(f + 1) * width] = turned[c][at:at + SUB, :]


def output_kernel(n_groups, frames, half, halves, aliased, place, *refs):
    n_in = n_groups * frames
    atts, pieces = refs[:n_groups], refs[n_groups:n_groups + n_in]
    w_ref, g_ref = refs[n_groups + n_in:n_groups + n_in + 2]
    out, buf, sems = refs[n_groups + n_in + 2 + aliased:]
    rows = pieces[0].shape[0]
    width = w_ref.shape[0]
    copies = []
    for j in range(n_groups):
        x = jnp.concatenate([atts[j][:, f * width:(f + 1) * width] for f in range(frames)], axis=0)
        proj = contract(x, w_ref[...], 1, 0)
        scale = lax.rsqrt(jnp.mean(proj * proj, axis=-1, keepdims=True) + EPS)
        res = proj * scale * g_ref[...]
        for f in range(frames):
            mine = pieces[j * frames + f][...].astype(F32)
            buf[j, f] = (mine + res[f * rows:(f + 1) * rows, :]).astype(BF)
        group = peer(place[0], j, n_groups)
        start = pl.multiple_of((group * halves + half) * rows, SUB)
        copy = pltpu.make_async_copy(buf.at[j], out.at[:, pl.ds(start, rows), :], sems.at[j])
        copy.start()
        copies.append(copy)
    for copy in copies:
        copy.wait()


def shards(
    spatial_queries,
    spatial_keys,
    spatial_values,
    hidden,
    spatial_out_weight,
    spatial_gain,
    temporal_qkv_weight,
    temporal_out_weight,
    temporal_gain,
    tile_list,
    tile_count,
):
    frames, tokens, width = spatial_queries.shape
    model = hidden.shape[2]
    groups = lax.axis_size("frame")
    strips = lax.axis_size("strip")
    share = tokens // groups
    halves = 2 if share % (4 * SUB) == 0 else 1
    rows = share // halves
    queries = jnp.transpose(spatial_queries, (0, 2, 1))
    keys = pltpu.with_memory_space_constraint(jnp.transpose(spatial_keys, (0, 2, 1)), pltpu.HBM)
    values = pltpu.with_memory_space_constraint(jnp.transpose(spatial_values, (0, 2, 1)), pltpu.HBM)
    lists = jnp.transpose(tile_list, (2, 1, 0))
    counts = tile_count.T
    qkv_weight = temporal_qkv_weight.T
    gain_one = spatial_gain.reshape(1, model)
    gain_two = temporal_gain.reshape(1, model)
    place = jnp.stack([lax.axis_index("frame"), lax.axis_index("strip")]).astype(jnp.int32)
    near = [(i, i ^ 1) for i in range(strips) if i ^ 1 < strips]
    far = [e for i in range(1, strips - 1, 2) for e in ((i, i + 1), (i + 1, i))]
    edge = jax.ShapeDtypeStruct((2 * width, TILE), BF)
    smem = pl.BlockSpec(memory_space=pltpu.SMEM)

    def call(kernel, name, in_specs, out_specs, out_shape, scratch=(), limit=32, prefetch=0, alias=None):
        return pl.pallas_call(
            kernel,
            grid_spec=pltpu.PrefetchScalarGridSpec(
                num_scalar_prefetch=prefetch,
                grid=(1,),
                in_specs=in_specs,
                out_specs=out_specs,
                scratch_shapes=list(scratch),
            ),
            out_shape=out_shape,
            input_output_aliases=alias or {},
            compiler_params=vmem(limit),
            name=name,
        )

    def frame_block(f):
        return pl.BlockSpec((1, width, tokens), lambda *_: (f, 0, 0))

    edges, halos = [], []
    for some in [[0], list(range(1, frames))]:
        got = call(
            prep_kernel,
            "prep",
            [smem] + [frame_block(f) for f in some for _ in range(2)],
            [whole(edge.shape)] * (2 * len(some)),
            [edge] * (2 * len(some)),
            limit=16,
        )(place, *[keys, values] * len(some))
        edges += [got[2 * i:2 * i + 2] for i in range(len(some))]
    for a, b in edges:
        halos.append((lax.ppermute(a, "strip", near), lax.ppermute(b, "strip", far)))

    mixed = [[None] * frames for _ in range(groups)]
    projected = []
    for f in range(frames):
        parts = call(
            functools.partial(spatial_kernel, f, groups),
            "spatial",
            [smem, smem, smem, frame_block(f)]
            + [whole(edge.shape)] * 4
            + [
                pl.BlockSpec((1, tokens, model), lambda *_, f=f: (f, 0, 0)),
                whole((width, model)),
                whole((1, model)),
            ],
            [whole((share, model))] * groups,
            [jax.ShapeDtypeStruct((share, model), BF)] * groups,
            [pltpu.VMEM((width, tokens), BF), pltpu.VMEM((tokens, model), BF)],
        )(place, counts, lists, queries, *edges[f], *halos[f], hidden, spatial_out_weight, gain_one)
        arrived = []
        for j in range(groups):
            mixed[j][f] = parts[j]
            pairs = [(i, peer(i, j, groups)) for i in range(groups)]
            arrived.append(parts[j] if j == 0 else lax.ppermute(parts[j], "frame", pairs))
        projected.append(
            call(
                functools.partial(project_kernel, f, frames),
                "project",
                [whole((share, model))] * groups + [whole((3 * width, model))],
                whole((3 * width, tokens)),
                jax.ShapeDtypeStruct((3 * width, tokens), BF),
                [pltpu.VMEM((tokens, model), BF)],
            )(*arrived, qkv_weight)
        )

    returned = []
    back_shape = (rows, frames * width)
    for half in range(halves):
        part = pl.BlockSpec((3 * width, tokens // halves), lambda *_, half=half: (0, half))
        back = call(
            functools.partial(temporal_kernel, groups),
            "temporal",
            [part] * frames,
            [whole(back_shape)] * groups,
            [jax.ShapeDtypeStruct(back_shape, BF)] * groups,
            [pltpu.VMEM((rows // SUB, width, groups * frames * SUB), F32)],
        )(*projected)
        got = []
        for j in range(groups):
            pairs = [(peer(i, j, groups), i) for i in range(groups)]
            got.append(back[j] if j == 0 else lax.ppermute(back[j], "frame", pairs))
        returned.append(got)

    out = None
    mine = [mixed[j][f] for j in range(groups) for f in range(frames)]
    any_spec = pl.BlockSpec(memory_space=pl.ANY)
    for half in range(halves):
        piece = pl.BlockSpec((rows, model), lambda *_, half=half: (half, 0))
        extra = [] if out is None else [out]
        out = call(
            functools.partial(output_kernel, groups, frames, half, halves, len(extra)),
            "output",
            [smem]
            + [whole(back_shape)] * groups
            + [piece] * len(mine)
            + [whole((width, model)), whole((1, model))]
            + [any_spec] * len(extra),
            any_spec,
            jax.ShapeDtypeStruct((frames, tokens, model), BF),
            [
                pltpu.VMEM((groups, frames, rows, model), BF),
                pltpu.SemaphoreType.DMA((groups,)),
            ],
            alias={1 + groups + len(mine) + 2: 0} if extra else None,
        )(place, *returned[half], *mine, temporal_out_weight, gain_two, *extra)
    return out


def solution(mesh):
    rows = P(("group", "frame"), "strip", None)
    placed = (rows, rows, rows, rows, P(), P(), P(), P(), P(), rows, P(("group", "frame"), "strip"))
    return jax.shard_map(shards, mesh=mesh, in_specs=placed, out_specs=rows, check_vma=False)
```

```python
import functools
import math

import jax
import jax.numpy as jnp
from jax import lax
from jax.experimental import pallas as pl
from jax.experimental.pallas import tpu as pltpu
from jax.sharding import PartitionSpec as P


HEAD_DIM = 72
TILE = 128
MAXT = 3
SUB = 16
EPS = 1e-06
EXP2_SCALE = HEAD_DIM ** -0.5 * math.log2(math.e)

BF = jnp.bfloat16
F32 = jnp.float32


def peer(i, j, n):
    return i ^ j if n & (n - 1) == 0 else (i + j) % n


def vmem(limit):
    return pltpu.CompilerParams(vmem_limit_bytes=limit << 20)


def whole(shape):
    return pl.BlockSpec(shape, lambda *_: (0,) * len(shape))


def contract(a, b, da, db):
    return lax.dot_general(a, b, (((da,), (db,)), ((), ())), preferred_element_type=F32)


def head_scale(x):
    return lax.rsqrt(jnp.mean(x * x, axis=0, keepdims=True) + EPS)


def head(h, base=0):
    return slice(base + h * HEAD_DIM, base + (h + 1) * HEAD_DIM)


def pipeline(steps, scores, weigh, gather):
    ahead, behind = scores(*steps[0]), None
    for n, step in enumerate(steps):
        now = ahead
        if n + 1 < len(steps):
            ahead = scores(*steps[n + 1])
        weighed = weigh(now)
        if behind is not None:
            gather(*steps[n - 1], *behind)
        behind = weighed
    gather(*steps[-1], *behind)


def prep_kernel(place, *refs):
    n = len(refs) // 4
    width = refs[0].shape[1]
    even = place[1] % 2 == 0
    for f in range(n):
        k_ref, v_ref = refs[2 * f:2 * f + 2]
        a_ref, b_ref = refs[2 * n + 2 * f:2 * n + 2 * f + 2]

        def fill(first, second):
            for h in range(width // HEAD_DIM):
                x = k_ref[0, head(h), :].astype(F32)
                y = (x * head_scale(x)).astype(BF)
                first[head(h), :] = y[:, :TILE]
                second[head(h), :] = y[:, TILE:]
            first[width:, :] = v_ref[0, :, :TILE]
            second[width:, :] = v_ref[0, :, TILE:]

        pl.when(even)(functools.partial(fill, b_ref, a_ref))
        pl.when(jnp.logical_not(even))(functools.partial(fill, a_ref, b_ref))


def spatial_kernel(frame, n_groups, place, counts, lists, q_ref, a_ref, b_ref, ra_ref, rb_ref, h_ref, w_ref, g_ref, *rest):
    outs, (att, mix) = rest[:n_groups], rest[n_groups:]
    width, tokens = q_ref.shape[1], q_ref.shape[2]
    tiles = tokens // TILE
    share = tokens // n_groups
    keys = ((a_ref, b_ref), (ra_ref, rb_ref))
    strip = place[1]
    odd = strip % 2
    first = strip * tiles
    places = (first + 1 - odd, first + odd, first + 2 - 3 * odd, first - 1 + 3 * odd)
    masks = []
    for t in range(tiles):
        live = counts[t, frame]
        cells = []
        for spot in places:
            hit = jnp.bool_(False)
            for j in range(MAXT):
                hit = hit | ((lists[j, t, frame] == spot) & (j < live))
            cells.append(jnp.where(hit, 1.0, 0.0).astype(F32))
        masks.append(cells)

    def scores(h):
        q = q_ref[0, head(h), :].astype(F32)
        qn = (q * head_scale(q)).astype(BF)
        return [[contract(keys[i][u][head(h), :], qn, 0, 0) for u in range(2)] for i in range(2)]

    def weigh(pair):
        partial, halves = [], []
        for i in range(2):
            packed = []
            for u in range(2):
                p = jnp.exp2(pair[i][u] * EXP2_SCALE)
                p = jnp.concatenate(
                    [p[:, t * TILE:(t + 1) * TILE] * masks[t][2 * i + u] for t in range(tiles)], axis=1
                )
                partial.append(jnp.sum(p.reshape(TILE // 8, 8, tokens), axis=0))
                packed.append(p.astype(BF))
            halves.append(jnp.concatenate(packed, axis=0))
        return jnp.sum(sum(partial), axis=0, keepdims=True), halves

    def gather(h, total, halves):
        o = 0
        for i in range(2):
            v = jnp.concatenate([r[head(h, width), :] for r in keys[i]], axis=1)
            o += contract(v, halves[i], 1, 0)
        att[head(h), :] = (o / total).astype(BF)

    pipeline([(h,) for h in range(width // HEAD_DIM)], scores, weigh, gather)
    proj = contract(att[...], w_ref[...], 0, 0)
    scale = lax.rsqrt(jnp.mean(proj * proj, axis=-1, keepdims=True) + EPS)
    mix[...] = (h_ref[0].astype(F32) + proj * scale * g_ref[...]).astype(BF)
    for j, out in enumerate(outs):
        group = peer(place[0], j, n_groups)
        out[...] = mix[pl.ds(pl.multiple_of(group * share, SUB), share), :]


def paired(chunks, lanes, frames):
    return chunks % 2 == 0 and frames % 2 == 0 and 2 * lanes == TILE


def project_kernel(frame, frames, *refs):
    pieces, w_ref, out, x = refs[:-3], refs[-3], refs[-2], refs[-1]
    n_groups = len(pieces)
    chunks = pieces[0].shape[0] // SUB
    swap = frame & 1 if paired(chunks, n_groups * SUB, frames) else 0
    for c in range(chunks):
        for j, piece in enumerate(pieces):
            at = ((c ^ swap) * n_groups + j) * SUB
            x[at:at + SUB, :] = piece[c * SUB:(c + 1) * SUB, :]
    width = w_ref.shape[0] // 3
    cut = w_ref.shape[0] // 2
    heads = width // HEAD_DIM
    parts = [contract(w_ref[i * cut:(i + 1) * cut, :], x[...], 1, 1) for i in range(2)]
    for h in range(3 * heads):
        i, at = divmod(h * HEAD_DIM, cut)
        y = parts[i][at:at + HEAD_DIM, :]
        if h < 2 * heads:
            y = y * head_scale(y)
        out[head(h), :] = y.astype(BF)


def temporal_kernel(n_groups, *refs):
    frames = len(refs) - n_groups - 1
    ins, outs, att = refs[:frames], refs[frames:frames + n_groups], refs[-1]
    lanes = n_groups * SUB
    chunks = ins[0].shape[1] // lanes
    width = ins[0].shape[0] // 3
    rows = frames * lanes
    pair = paired(chunks, lanes, frames)
    row_pos = lax.broadcasted_iota(jnp.int32, (rows, rows), 0) % SUB
    col_pos = lax.broadcasted_iota(jnp.int32, (rows, rows), 1) % SUB
    same = jnp.where(row_pos == col_pos, 1.0, 0.0).astype(F32)
    low = lax.broadcasted_iota(jnp.int32, (HEAD_DIM, TILE), 1) < lanes

    def take(c, where):
        if not pair:
            return jnp.concatenate([r[where, c * lanes:(c + 1) * lanes] for r in ins], axis=1)
        tile = slice(c // 2 * TILE, (c // 2 + 1) * TILE)
        got = [r[where, tile] for r in ins]
        return jnp.concatenate(
            [
                jnp.where(low, got[m + (c & 1)], got[m + 1 - (c & 1)])
                for m in range(0, frames, 2)
            ],
            axis=1,
        )

    def scores(c, h):
        return contract(take(c, head(h, width)), take(c, head(h)), 0, 0)

    def weigh(s):
        p = jnp.exp2(s * EXP2_SCALE) * same
        return jnp.sum(p, axis=0, keepdims=True), p.astype(BF)

    def gather(c, h, total, p):
        att[c, head(h), :] = contract(take(c, head(h, 2 * width)), p, 1, 0) / total

    steps = [(c, h) for c in range(chunks) for h in range(width // HEAD_DIM)]
    pipeline(steps, scores, weigh, gather)
    turned = [att[c].T.astype(BF) for c in range(chunks)]
    for j, out in enumerate(outs):
        for c in range(chunks):
            for f in range(frames):
                slot = f ^ (c & 1) if pair else f
                at = slot * lanes + j * SUB
                out[c * SUB:(c + 1) * SUB, f * width:(f + 1) * width] = turned[c][at:at + SUB, :]


def output_kernel(n_groups, frames, half, halves, aliased, place, *refs):
    n_in = n_groups * frames
    atts, pieces = refs[:n_groups], refs[n_groups:n_groups + n_in]
    w_ref, g_ref = refs[n_groups + n_in:n_groups + n_in + 2]
    out, buf, sems = refs[n_groups + n_in + 2 + aliased:]
    rows = pieces[0].shape[0]
    width = w_ref.shape[0]
    copies = []
    for j in range(n_groups):
        x = jnp.concatenate([atts[j][:, f * width:(f + 1) * width] for f in range(frames)], axis=0)
        proj = contract(x, w_ref[...], 1, 0)
        scale = lax.rsqrt(jnp.mean(proj * proj, axis=-1, keepdims=True) + EPS)
        res = proj * scale * g_ref[...]
        for f in range(frames):
            mine = pieces[j * frames + f][...].astype(F32)
            buf[j, f] = (mine + res[f * rows:(f + 1) * rows, :]).astype(BF)
        group = peer(place[0], j, n_groups)
        start = pl.multiple_of((group * halves + half) * rows, SUB)
        copy = pltpu.make_async_copy(buf.at[j], out.at[:, pl.ds(start, rows), :], sems.at[j])
        copy.start()
        copies.append(copy)
    for copy in copies:
        copy.wait()


def shards(
    spatial_queries,
    spatial_keys,
    spatial_values,
    hidden,
    spatial_out_weight,
    spatial_gain,
    temporal_qkv_weight,
    temporal_out_weight,
    temporal_gain,
    tile_list,
    tile_count,
):
    frames, tokens, width = spatial_queries.shape
    model = hidden.shape[2]
    groups = lax.axis_size("frame")
    strips = lax.axis_size("strip")
    share = tokens // groups
    halves = 2 if share % (4 * SUB) == 0 else 1
    rows = share // halves
    queries = jnp.transpose(spatial_queries, (0, 2, 1))
    keys = pltpu.with_memory_space_constraint(jnp.transpose(spatial_keys, (0, 2, 1)), pltpu.HBM)
    values = pltpu.with_memory_space_constraint(jnp.transpose(spatial_values, (0, 2, 1)), pltpu.HBM)
    lists = jnp.transpose(tile_list, (2, 1, 0))
    counts = tile_count.T
    qkv_weight = temporal_qkv_weight.T
    gain_one = spatial_gain.reshape(1, model)
    gain_two = temporal_gain.reshape(1, model)
    place = jnp.stack([lax.axis_index("frame"), lax.axis_index("strip")]).astype(jnp.int32)
    near = [(i, i ^ 1) for i in range(strips) if i ^ 1 < strips]
    far = [e for i in range(1, strips - 1, 2) for e in ((i, i + 1), (i + 1, i))]
    edge = jax.ShapeDtypeStruct((2 * width, TILE), BF)
    smem = pl.BlockSpec(memory_space=pltpu.SMEM)

    def call(kernel, in_specs, out_specs, out_shape, scratch=(), limit=32, prefetch=0, alias=None):
        return pl.pallas_call(
            kernel,
            grid_spec=pltpu.PrefetchScalarGridSpec(
                num_scalar_prefetch=prefetch,
                grid=(1,),
                in_specs=in_specs,
                out_specs=out_specs,
                scratch_shapes=list(scratch),
            ),
            out_shape=out_shape,
            input_output_aliases=alias or {},
            compiler_params=vmem(limit),
        )

    def frame_block(f):
        return pl.BlockSpec((1, width, tokens), lambda *_: (f, 0, 0))

    edges, halos = [], []
    for some in [[0], list(range(1, frames))]:
        got = call(
            prep_kernel,
            [smem] + [frame_block(f) for f in some for _ in range(2)],
            [whole(edge.shape)] * (2 * len(some)),
            [edge] * (2 * len(some)),
            limit=16,
        )(place, *[keys, values] * len(some))
        edges += [got[2 * i:2 * i + 2] for i in range(len(some))]
    for a, b in edges:
        halos.append((lax.ppermute(a, "strip", near), lax.ppermute(b, "strip", far)))

    mixed = [[None] * frames for _ in range(groups)]
    projected = []
    for f in range(frames):
        parts = call(
            functools.partial(spatial_kernel, f, groups),
            [smem, smem, smem, frame_block(f)]
            + [whole(edge.shape)] * 4
            + [
                pl.BlockSpec((1, tokens, model), lambda *_, f=f: (f, 0, 0)),
                whole((width, model)),
                whole((1, model)),
            ],
            [whole((share, model))] * groups,
            [jax.ShapeDtypeStruct((share, model), BF)] * groups,
            [pltpu.VMEM((width, tokens), BF), pltpu.VMEM((tokens, model), BF)],
        )(place, counts, lists, queries, *edges[f], *halos[f], hidden, spatial_out_weight, gain_one)
        arrived = []
        for j in range(groups):
            mixed[j][f] = parts[j]
            pairs = [(i, peer(i, j, groups)) for i in range(groups)]
            arrived.append(parts[j] if j == 0 else lax.ppermute(parts[j], "frame", pairs))
        projected.append(
            call(
                functools.partial(project_kernel, f, frames),
                [whole((share, model))] * groups + [whole((3 * width, model))],
                whole((3 * width, tokens)),
                jax.ShapeDtypeStruct((3 * width, tokens), BF),
                [pltpu.VMEM((tokens, model), BF)],
            )(*arrived, qkv_weight)
        )

    returned = []
    back_shape = (rows, frames * width)
    for half in range(halves):
        part = pl.BlockSpec((3 * width, tokens // halves), lambda *_, half=half: (0, half))
        back = call(
            functools.partial(temporal_kernel, groups),
            [part] * frames,
            [whole(back_shape)] * groups,
            [jax.ShapeDtypeStruct(back_shape, BF)] * groups,
            [pltpu.VMEM((rows // SUB, width, groups * frames * SUB), F32)],
        )(*projected)
        got = []
        for j in range(groups):
            pairs = [(peer(i, j, groups), i) for i in range(groups)]
            got.append(back[j] if j == 0 else lax.ppermute(back[j], "frame", pairs))
        returned.append(got)

    out = None
    mine = [mixed[j][f] for j in range(groups) for f in range(frames)]
    any_spec = pl.BlockSpec(memory_space=pl.ANY)
    for half in range(halves):
        piece = pl.BlockSpec((rows, model), lambda *_, half=half: (half, 0))
        extra = [] if out is None else [out]
        out = call(
            functools.partial(output_kernel, groups, frames, half, halves, len(extra)),
            [smem]
            + [whole(back_shape)] * groups
            + [piece] * len(mine)
            + [whole((width, model)), whole((1, model))]
            + [any_spec] * len(extra),
            any_spec,
            jax.ShapeDtypeStruct((frames, tokens, model), BF),
            [
                pltpu.VMEM((groups, frames, rows, model), BF),
                pltpu.SemaphoreType.DMA((groups,)),
            ],
            alias={1 + groups + len(mine) + 2: 0} if extra else None,
        )(place, *returned[half], *mine, temporal_out_weight, gain_two, *extra)
    return out


def solution(mesh):
    rows = P(("group", "frame"), "strip", None)
    placed = (rows, rows, rows, rows, P(), P(), P(), P(), P(), rows, P(("group", "frame"), "strip"))

    return jax.shard_map(shards, mesh=mesh, in_specs=placed, out_specs=rows, check_vma=False)
```

```python
import functools
import math

import jax
import jax.numpy as jnp
from jax import lax
from jax.experimental import pallas as pl
from jax.experimental.pallas import tpu as pltpu
from jax.sharding import PartitionSpec as P


HEAD_DIM = 72
TILE = 128
MAXT = 3
SUB = 16
EPS = 1e-06
EXP2_SCALE = HEAD_DIM ** -0.5 * math.log2(math.e)

BF = jnp.bfloat16
F32 = jnp.float32


def peer(i, j, n):
    return i ^ j if n & (n - 1) == 0 else (i + j) % n


def vmem(limit):
    return pltpu.CompilerParams(vmem_limit_bytes=limit << 20)


def whole(shape):
    return pl.BlockSpec(shape, lambda *_: (0,) * len(shape))


def contract(a, b, da, db):
    return lax.dot_general(a, b, (((da,), (db,)), ((), ())), preferred_element_type=F32)


def head_scale(x):
    return lax.rsqrt(jnp.mean(x * x, axis=0, keepdims=True) + EPS)


def head(h, base=0):
    return slice(base + h * HEAD_DIM, base + (h + 1) * HEAD_DIM)


def pipeline(steps, scores, weigh, gather):
    ahead, behind = scores(*steps[0]), None
    for n, step in enumerate(steps):
        now = ahead
        if n + 1 < len(steps):
            ahead = scores(*steps[n + 1])
        weighed = weigh(now)
        if behind is not None:
            gather(*steps[n - 1], *behind)
        behind = weighed
    gather(*steps[-1], *behind)


def prep_kernel(place, k_ref, v_ref, a_ref, b_ref):
    n, width, _ = k_ref.shape
    even = place[1] % 2 == 0

    def fill(first, second):
        for f in range(n):
            for h in range(width // HEAD_DIM):
                x = k_ref[f, head(h), :].astype(F32)
                y = (x * head_scale(x)).astype(BF)
                first[f, head(h), :] = y[:, :TILE]
                second[f, head(h), :] = y[:, TILE:]
            first[f, width:, :] = v_ref[f, :, :TILE]
            second[f, width:, :] = v_ref[f, :, TILE:]

    pl.when(even)(functools.partial(fill, b_ref, a_ref))
    pl.when(jnp.logical_not(even))(functools.partial(fill, a_ref, b_ref))


def split_kernel(place, *refs):
    n = len(refs) // 2
    for src, dst in zip(refs[:n], refs[n:]):
        dst[...] = src[...]


def attend(frame, place, counts, lists, q_ref, keys, att):
    n, width, tokens = q_ref.shape
    tiles = tokens // TILE
    strip = place[1]
    odd = strip % 2
    first = strip * tiles
    places = (first + 1 - odd, first + odd, first + 2 - 3 * odd, first - 1 + 3 * odd)
    masks = []
    for f in range(n):
        table = []
        for t in range(tiles):
            live = counts[t, frame + f]
            cells = []
            for spot in places:
                hit = jnp.bool_(False)
                for j in range(MAXT):
                    hit = hit | ((lists[j, t, frame + f] == spot) & (j < live))
                cells.append(jnp.where(hit, 1.0, 0.0).astype(F32))
            table.append(cells)
        masks.append(table)

    def scores(f, h):
        q = q_ref[f, head(h), :].astype(F32)
        qn = (q * head_scale(q)).astype(BF)
        return f, [contract(ref[f, head(h), :], qn, 0, 0) for ref in keys]

    def weigh(scored):
        f, s = scored
        partial, packed = [], []
        for i, x in enumerate(s):
            p = jnp.exp2(x * EXP2_SCALE)
            p = jnp.concatenate(
                [p[:, t * TILE:(t + 1) * TILE] * masks[f][t][i] for t in range(tiles)], axis=1
            )
            partial.append(jnp.sum(p.reshape(TILE // 8, 8, tokens), axis=0))
            packed.append(p.astype(BF))
        halves = [jnp.concatenate(packed[i:i + 2], axis=0) for i in (0, 2)]
        return jnp.sum(sum(partial), axis=0, keepdims=True), halves

    def gather(f, h, total, halves):
        o = 0
        for i in range(2):
            v = jnp.concatenate([r[f, head(h, width), :] for r in keys[2 * i:2 * i + 2]], axis=1)
            o += contract(v, halves[i], 1, 0)
        att[f, head(h), :] = (o / total).astype(att.dtype)

    pipeline([(f, h) for f in range(n) for h in range(width // HEAD_DIM)], scores, weigh, gather)


def add_normed(base, proj, gain):
    scale = lax.rsqrt(jnp.mean(proj * proj, axis=-1, keepdims=True) + EPS)
    return (base.astype(F32) + proj * scale * gain).astype(BF)


def spatial_kernel(frame, n_groups, place, counts, lists, q_ref, a_ref, b_ref, ra_ref, rb_ref, h_ref, w_ref, g_ref, *rest):
    outs, (att, mix) = rest[:n_groups], rest[n_groups:]
    attend(frame, place, counts, lists, q_ref, (a_ref, b_ref, ra_ref, rb_ref), att)
    mix[...] = add_normed(h_ref[0], contract(att[0], w_ref[...], 0, 0), g_ref[...])
    share = mix.shape[0] // n_groups
    for j, out in enumerate(outs):
        group = peer(place[0], j, n_groups)
        out[...] = mix[pl.ds(pl.multiple_of(group * share, SUB), share), :]


def late_kernel(frame, n_groups, halves, place, counts, lists, q_ref, a_ref, b_ref, ra_ref, rb_ref, *rest):
    outs, (att, rows) = rest[:n_groups * halves], rest[n_groups * halves:]
    n, width, tokens = q_ref.shape
    attend(frame, place, counts, lists, q_ref, (a_ref, b_ref, ra_ref, rb_ref), att)
    for f in range(n):
        rows[:, f * width:(f + 1) * width] = att[f].T.astype(BF)
    size = tokens // n_groups // halves
    for half in range(halves):
        for j in range(n_groups):
            start = (peer(place[0], j, n_groups) * halves + half) * size
            outs[half * n_groups + j][...] = rows[pl.ds(pl.multiple_of(start, SUB), size), :]


def mix_kernel(*refs):
    atts, hids = refs[:len(refs) // 2 - 1], refs[len(refs) // 2 - 1:-3]
    w_ref, g_ref, out = refs[-3:]
    width = w_ref.shape[0]
    n, rows, _ = hids[0].shape
    for j, (att, hid) in enumerate(zip(atts, hids)):
        x = jnp.concatenate([att[:, f * width:(f + 1) * width] for f in range(n)], axis=0)
        proj = contract(x, w_ref[...], 1, 0)
        for f in range(n):
            out[j, f] = add_normed(hid[f], proj[f * rows:(f + 1) * rows, :], g_ref[...])


def paired(chunks, lanes, frames):
    return chunks % 2 == 0 and frames % 2 == 0 and 2 * lanes == TILE


def slot(c, frame, chunks, n_groups, frames):
    return c ^ (frame & 1) if paired(chunks, n_groups * SUB, frames) else c


def project(w_ref, x, out):
    width = w_ref.shape[0] // 3
    cut = w_ref.shape[0] // 2
    heads = width // HEAD_DIM
    parts = [contract(w_ref[i * cut:(i + 1) * cut, :], x[...], 1, 1) for i in range(2)]
    for h in range(3 * heads):
        i, at = divmod(h * HEAD_DIM, cut)
        y = parts[i][at:at + HEAD_DIM, :]
        if h < 2 * heads:
            y = y * head_scale(y)
        out[head(h), :] = y.astype(BF)


def project_kernel(frame, frames, *refs):
    pieces, w_ref, out, x = refs[:-3], refs[-3], refs[-2], refs[-1]
    n_groups = len(pieces)
    chunks = pieces[0].shape[0] // SUB
    for c in range(chunks):
        for j, piece in enumerate(pieces):
            at = (slot(c, frame, chunks, n_groups, frames) * n_groups + j) * SUB
            x[at:at + SUB, :] = piece[c * SUB:(c + 1) * SUB, :]
    project(w_ref, x, out)


def late_project_kernel(frame, frames, *refs):
    n_groups = (len(refs) - 7) // 2
    atts, hids = refs[:n_groups], refs[n_groups:2 * n_groups]
    w_ref, g_ref, qkv_ref, out, a, b, x = refs[2 * n_groups:]
    width = w_ref.shape[0]
    n, rows, _ = hids[0].shape
    chunks = rows // SUB
    for f in range(n):
        for c in range(chunks):
            for j in range(n_groups):
                at = ((f * chunks + slot(c, frame + f, chunks, n_groups, frames)) * n_groups + j) * SUB
                piece = slice(c * SUB, (c + 1) * SUB)
                a[at:at + SUB, :] = atts[j][piece, f * width:(f + 1) * width]
                b[at:at + SUB, :] = hids[j][f, piece, :]
    x[...] = add_normed(b[...], contract(a[...], w_ref[...], 1, 0), g_ref[...])
    project(qkv_ref, x, out)


def temporal_kernel(n_groups, *refs):
    frames = len(refs) - n_groups - 1
    ins, outs, att = refs[:frames], refs[frames:frames + n_groups], refs[-1]
    lanes = n_groups * SUB
    chunks = ins[0].shape[1] // lanes
    width = ins[0].shape[0] // 3
    rows = frames * lanes
    pair = paired(chunks, lanes, frames)
    row_pos = lax.broadcasted_iota(jnp.int32, (rows, rows), 0) % SUB
    col_pos = lax.broadcasted_iota(jnp.int32, (rows, rows), 1) % SUB
    same = jnp.where(row_pos == col_pos, 1.0, 0.0).astype(F32)
    low = lax.broadcasted_iota(jnp.int32, (HEAD_DIM, TILE), 1) < lanes

    def take(c, where):
        if not pair:
            return jnp.concatenate([r[where, c * lanes:(c + 1) * lanes] for r in ins], axis=1)
        tile = slice(c // 2 * TILE, (c // 2 + 1) * TILE)
        got = [r[where, tile] for r in ins]
        return jnp.concatenate(
            [
                jnp.where(low, got[m + (c & 1)], got[m + 1 - (c & 1)])
                for m in range(0, frames, 2)
            ],
            axis=1,
        )

    def scores(c, h):
        return contract(take(c, head(h, width)), take(c, head(h)), 0, 0)

    def weigh(s):
        p = jnp.exp2(s * EXP2_SCALE) * same
        return jnp.sum(p, axis=0, keepdims=True), p.astype(BF)

    def gather(c, h, total, p):
        att[c, head(h), :] = contract(take(c, head(h, 2 * width)), p, 1, 0) / total

    steps = [(c, h) for c in range(chunks) for h in range(width // HEAD_DIM)]
    pipeline(steps, scores, weigh, gather)
    turned = [att[c].T.astype(BF) for c in range(chunks)]
    for j, out in enumerate(outs):
        for c in range(chunks):
            for f in range(frames):
                at = (f ^ (c & 1) if pair else f) * lanes + j * SUB
                out[c * SUB:(c + 1) * SUB, f * width:(f + 1) * width] = turned[c][at:at + SUB, :]


def output_kernel(n_groups, js, early, half, halves, aliased, place, *refs):
    n = len(js)
    atts, pieces = refs[:n], refs[n:n * (1 + early)]
    late_ref, w_ref, g_ref = refs[n * (1 + early):n * (1 + early) + 3]
    out, buf, sems = refs[n * (1 + early) + 3 + aliased:]
    _, late, rows, _ = late_ref.shape
    width = w_ref.shape[0]
    frames = early + late
    copies = []
    for i, j in enumerate(js):
        x = jnp.concatenate([atts[i][:, f * width:(f + 1) * width] for f in range(frames)], axis=0)
        proj = contract(x, w_ref[...], 1, 0)
        for f in range(frames):
            mine = pieces[i * early + f][...] if f < early else late_ref[j, f - early]
            buf[i, f] = add_normed(mine, proj[f * rows:(f + 1) * rows, :], g_ref[...])
        group = peer(place[0], j, n_groups)
        start = pl.multiple_of((group * halves + half) * rows, SUB)
        copy = pltpu.make_async_copy(buf.at[i], out.at[:, pl.ds(start, rows), :], sems.at[i])
        copy.start()
        copies.append(copy)
    for copy in copies:
        copy.wait()


def shards(
    spatial_queries,
    spatial_keys,
    spatial_values,
    hidden,
    spatial_out_weight,
    spatial_gain,
    temporal_qkv_weight,
    temporal_out_weight,
    temporal_gain,
    tile_list,
    tile_count,
):
    frames, tokens, width = spatial_queries.shape
    model = hidden.shape[2]
    groups = lax.axis_size("frame")
    strips = lax.axis_size("strip")
    share = tokens // groups
    halves = 2 if share % (4 * SUB) == 0 else 1
    rows = share // halves
    queries = jnp.transpose(spatial_queries, (0, 2, 1))
    keys = pltpu.with_memory_space_constraint(jnp.transpose(spatial_keys, (0, 2, 1)), pltpu.HBM)
    values = pltpu.with_memory_space_constraint(jnp.transpose(spatial_values, (0, 2, 1)), pltpu.HBM)
    hidden_far = pltpu.with_memory_space_constraint(hidden, pltpu.HBM)
    lists = jnp.transpose(tile_list, (2, 1, 0))
    counts = tile_count.T
    qkv_weight = temporal_qkv_weight.T
    gain_one = spatial_gain.reshape(1, model)
    gain_two = temporal_gain.reshape(1, model)
    place = jnp.stack([lax.axis_index("frame"), lax.axis_index("strip")]).astype(jnp.int32)
    near = [(i, i ^ 1) for i in range(strips) if i ^ 1 < strips]
    far = [e for i in range(1, strips - 1, 2) for e in ((i, i + 1), (i + 1, i))]
    edge = jax.ShapeDtypeStruct((2 * width, TILE), BF)
    smem = pl.BlockSpec(memory_space=pltpu.SMEM)

    def call(kernel, in_specs, out_specs, out_shape, scratch=(), limit=32, prefetch=0, alias=None):
        return pl.pallas_call(
            kernel,
            grid_spec=pltpu.PrefetchScalarGridSpec(
                num_scalar_prefetch=prefetch,
                grid=(1,),
                in_specs=in_specs,
                out_specs=out_specs,
                scratch_shapes=list(scratch),
            ),
            out_shape=out_shape,
            input_output_aliases=alias or {},
            compiler_params=vmem(limit),
        )

    def frame_block(f):
        return pl.BlockSpec((1, width, tokens), lambda *_: (f, 0, 0))

    late = frames // 2
    early = frames - late

    halos = []
    for some in range(2):
        block = pl.BlockSpec((late, width, tokens), lambda *_, some=some: (some, 0, 0))
        a, b = call(
            prep_kernel,
            [smem, block, block],
            [whole((late,) + edge.shape)] * 2,
            [jax.ShapeDtypeStruct((late,) + edge.shape, BF)] * 2,
            limit=16,
        )(place, keys, values)
        halos.append((a, b, lax.ppermute(a, "strip", near), lax.ppermute(b, "strip", far)))

    def out_pairs(j):
        return [(i, peer(i, j, groups)) for i in range(groups)]

    def send(x, j):
        return x if j == 0 else lax.ppermute(x, "frame", out_pairs(j))

    own_hidden = call(
        split_kernel,
        [
            pl.BlockSpec((late, share, model), lambda _, at, j=j: (1, peer(at[0], j, groups), 0))
            for j in range(groups)
        ],
        [whole((late, share, model))] * groups,
        [jax.ShapeDtypeStruct((late, share, model), BF)] * groups,
        prefetch=1,
        limit=16,
    )(place, *[hidden_far] * groups)
    far_hidden = [send(x, j) for j, x in enumerate(own_hidden)]

    mixed = [[None] * early for _ in range(groups)]
    projected = []
    for f in range(early):
        edge_block = pl.BlockSpec((1,) + edge.shape, lambda *_, f=f: (f, 0, 0))
        parts = call(
            functools.partial(spatial_kernel, f, groups),
            [smem, smem, smem, frame_block(f)]
            + [edge_block] * 4
            + [
                pl.BlockSpec((1, tokens, model), lambda *_, f=f: (f, 0, 0)),
                whole((width, model)),
                whole((1, model)),
            ],
            [whole((share, model))] * groups,
            [jax.ShapeDtypeStruct((share, model), BF)] * groups,
            [pltpu.VMEM((1, width, tokens), BF), pltpu.VMEM((tokens, model), BF)],
        )(place, counts, lists, queries, *halos[0], hidden, spatial_out_weight, gain_one)
        for j in range(groups):
            mixed[j][f] = parts[j]
        projected.append(
            call(
                functools.partial(project_kernel, f, frames),
                [whole((share, model))] * groups + [whole((3 * width, model))],
                whole((3 * width, tokens)),
                jax.ShapeDtypeStruct((3 * width, tokens), BF),
                [pltpu.VMEM((tokens, model), BF)],
            )(*[send(x, j) for j, x in enumerate(parts)], qkv_weight)
        )

    late_shape = (rows, late * width)
    own_late = call(
        functools.partial(late_kernel, early, groups, halves),
        [smem, smem, smem, pl.BlockSpec((late, width, tokens), lambda *_: (1, 0, 0))]
        + [whole((late,) + edge.shape)] * 4,
        [whole(late_shape)] * (groups * halves),
        [jax.ShapeDtypeStruct(late_shape, BF)] * (groups * halves),
        [pltpu.VMEM((late, width, tokens), F32), pltpu.VMEM((tokens, late * width), BF)],
    )(place, counts, lists, queries, *halos[1])
    own_late = [own_late[half * groups:(half + 1) * groups] for half in range(halves)]
    far_late = [[send(x, j) for j, x in enumerate(some)] for some in own_late]

    returned, late_mixed = [], []
    back_shape = (rows, frames * width)
    lanes = tokens // halves
    for half in range(halves):
        hid_block = pl.BlockSpec((late, rows, model), lambda *_, half=half: (0, half, 0))
        late_specs = [whole(late_shape)] * groups + [hid_block] * groups
        late_specs += [whole((width, model)), whole((1, model))]
        late_projected = call(
            functools.partial(late_project_kernel, early, frames),
            late_specs + [whole((3 * width, model))],
            whole((3 * width, late * lanes)),
            jax.ShapeDtypeStruct((3 * width, late * lanes), BF),
            [
                pltpu.VMEM((late * lanes, width), BF),
                pltpu.VMEM((late * lanes, model), BF),
                pltpu.VMEM((late * lanes, model), BF),
            ],
        )(*far_late[half], *far_hidden, spatial_out_weight, gain_one, qkv_weight)
        back = call(
            functools.partial(temporal_kernel, groups),
            [pl.BlockSpec((3 * width, lanes), lambda *_, half=half: (0, half))] * early
            + [pl.BlockSpec((3 * width, lanes), lambda *_, f=f: (0, f)) for f in range(late)],
            [whole(back_shape)] * groups,
            [jax.ShapeDtypeStruct(back_shape, BF)] * groups,
            [pltpu.VMEM((rows // SUB, width, groups * frames * SUB), F32)],
        )(*projected, *[late_projected] * late)
        got = []
        for j in range(groups):
            pairs = [(b, a) for a, b in out_pairs(j)]
            got.append(back[j] if j == 0 else lax.ppermute(back[j], "frame", pairs))
        returned.append(got)
        late_mixed.append(
            call(
                mix_kernel,
                late_specs,
                whole((groups, late, rows, model)),
                jax.ShapeDtypeStruct((groups, late, rows, model), BF),
            )(*own_late[half], *own_hidden, spatial_out_weight, gain_one)
        )

    out = None
    any_spec = pl.BlockSpec(memory_space=pl.ANY)
    for half in range(halves):
        piece = pl.BlockSpec((rows, model), lambda *_, half=half: (half, 0))
        cuts = [groups] if half + 1 < halves else [groups // 2, groups * 3 // 4, groups]
        for lo, hi in zip([0] + cuts, cuts):
            js = range(lo, hi)
            if not js:
                continue
            extra = [] if out is None else [out]
            out = call(
                functools.partial(output_kernel, groups, tuple(js), early, half, halves, len(extra)),
                [smem]
                + [whole(back_shape)] * len(js)
                + [piece] * (len(js) * early)
                + [whole((groups, late, rows, model)), whole((width, model)), whole((1, model))]
                + [any_spec] * len(extra),
                any_spec,
                jax.ShapeDtypeStruct((frames, tokens, model), BF),
                [
                    pltpu.VMEM((len(js), frames, rows, model), BF),
                    pltpu.SemaphoreType.DMA((len(js),)),
                ],
                alias={4 + len(js) * (1 + early): 0} if extra else None,
            )(
                place,
                *[returned[half][j] for j in js],
                *[mixed[j][f] for j in js for f in range(early)],
                late_mixed[half],
                temporal_out_weight,
                gain_two,
                *extra,
            )
    return out


def solution(mesh):
    rows = P(("group", "frame"), "strip", None)
    placed = (rows, rows, rows, rows, P(), P(), P(), P(), P(), rows, P(("group", "frame"), "strip"))

    return jax.shard_map(shards, mesh=mesh, in_specs=placed, out_specs=rows, check_vma=False)
```

```python
import functools
import math

import jax
import jax.numpy as jnp
from jax import lax
from jax.experimental import pallas as pl
from jax.experimental.pallas import tpu as pltpu
from jax.sharding import PartitionSpec as P


HEAD_DIM = 72
TILE = 128
MAXT = 3
SUB = 16
EPS = 1e-06
EXP2_SCALE = HEAD_DIM ** -0.5 * math.log2(math.e)

BF = jnp.bfloat16
F32 = jnp.float32


def peer(i, j, n):
    return i ^ j if n & (n - 1) == 0 else (i + j) % n


def vmem(limit):
    return pltpu.CompilerParams(vmem_limit_bytes=limit << 20)


def whole(shape):
    return pl.BlockSpec(shape, lambda *_: (0,) * len(shape))


def contract(a, b, da, db):
    return lax.dot_general(a, b, (((da,), (db,)), ((), ())), preferred_element_type=F32)


def head_scale(x):
    return lax.rsqrt(jnp.mean(x * x, axis=0, keepdims=True) + EPS)


def head(h, base=0):
    return slice(base + h * HEAD_DIM, base + (h + 1) * HEAD_DIM)


def pipeline(steps, scores, weigh, gather):
    ahead, behind = scores(*steps[0]), None
    for n, step in enumerate(steps):
        now = ahead
        if n + 1 < len(steps):
            ahead = scores(*steps[n + 1])
        weighed = weigh(now)
        if behind is not None:
            gather(*steps[n - 1], *behind)
        behind = weighed
    gather(*steps[-1], *behind)


def prep_kernel(place, k_ref, v_ref, a_ref, b_ref):
    n, width, _ = k_ref.shape
    even = place[1] % 2 == 0

    def fill(first, second):
        for f in range(n):
            for h in range(width // HEAD_DIM):
                x = k_ref[f, head(h), :].astype(F32)
                y = (x * head_scale(x)).astype(BF)
                first[f, head(h), :] = y[:, :TILE]
                second[f, head(h), :] = y[:, TILE:]
            first[f, width:, :] = v_ref[f, :, :TILE]
            second[f, width:, :] = v_ref[f, :, TILE:]

    pl.when(even)(functools.partial(fill, b_ref, a_ref))
    pl.when(jnp.logical_not(even))(functools.partial(fill, a_ref, b_ref))


def split_kernel(place, src, *refs):
    outs, sems = refs[:-1], refs[-1]
    late, share, _ = outs[0].shape
    copies = []
    for j, dst in enumerate(outs):
        start = pl.multiple_of(peer(place[0], j, len(outs)) * share, SUB)
        part = src.at[pl.ds(src.shape[0] - late, late), pl.ds(start, share), :]
        copies.append(pltpu.make_async_copy(part, dst, sems.at[j]))
        copies[-1].start()
    for copy in copies:
        copy.wait()


def attend(frame, place, counts, lists, q_ref, keys, att):
    n, width, tokens = q_ref.shape
    tiles = tokens // TILE
    strip = place[1]
    odd = strip % 2
    first = strip * tiles
    places = (first + 1 - odd, first + odd, first + 2 - 3 * odd, first - 1 + 3 * odd)
    masks = []
    for f in range(n):
        table = []
        for t in range(tiles):
            live = counts[t, frame + f]
            cells = []
            for spot in places:
                hit = jnp.bool_(False)
                for j in range(MAXT):
                    hit = hit | ((lists[j, t, frame + f] == spot) & (j < live))
                cells.append(jnp.where(hit, 1.0, 0.0).astype(F32))
            table.append(cells)
        masks.append(table)

    def scores(f, h):
        q = q_ref[f, head(h), :].astype(F32)
        qn = (q * head_scale(q)).astype(BF)
        return f, [contract(ref[f, head(h), :], qn, 0, 0) for ref in keys]

    def weigh(scored):
        f, s = scored
        partial, packed = [], []
        for i, x in enumerate(s):
            p = jnp.exp2(x * EXP2_SCALE)
            p = jnp.concatenate(
                [p[:, t * TILE:(t + 1) * TILE] * masks[f][t][i] for t in range(tiles)], axis=1
            )
            partial.append(jnp.sum(p.reshape(TILE // 8, 8, tokens), axis=0))
            packed.append(p.astype(BF))
        halves = [jnp.concatenate(packed[i:i + 2], axis=0) for i in (0, 2)]
        return jnp.sum(sum(partial), axis=0, keepdims=True), halves

    def gather(f, h, total, halves):
        o = 0
        for i in range(2):
            v = jnp.concatenate([r[f, head(h, width), :] for r in keys[2 * i:2 * i + 2]], axis=1)
            o += contract(v, halves[i], 1, 0)
        att[f, head(h), :] = (o / total).astype(att.dtype)

    pipeline([(f, h) for f in range(n) for h in range(width // HEAD_DIM)], scores, weigh, gather)


def add_normed(blocks):
    ahead = blocks[0][0]()
    for n, (_, finish) in enumerate(blocks):
        proj = ahead
        if n + 1 < len(blocks):
            ahead = blocks[n + 1][0]()
        scale = lax.rsqrt(jnp.mean(proj * proj, axis=-1, keepdims=True) + EPS)
        finish(proj * scale)


def spatial_kernel(frame, n_groups, place, counts, lists, q_ref, a_ref, b_ref, ra_ref, rb_ref, h_ref, w_ref, g_ref, *rest):
    outs, (att, mix) = rest[:n_groups], rest[n_groups:]
    attend(frame, place, counts, lists, q_ref, (a_ref, b_ref, ra_ref, rb_ref), att)

    def block(at):
        rows = slice(at, at + TILE)

        def finish(normed):
            mix[rows, :] = (h_ref[0, rows, :].astype(F32) + normed * g_ref[...]).astype(BF)

        return lambda: contract(att[0, :, rows], w_ref[...], 0, 0), finish

    add_normed([block(at) for at in range(0, mix.shape[0], TILE)])
    share = mix.shape[0] // n_groups
    for j, out in enumerate(outs):
        group = peer(place[0], j, n_groups)
        out[...] = mix[pl.ds(pl.multiple_of(group * share, SUB), share), :]


def late_kernel(frame, n_groups, halves, place, counts, lists, q_ref, a_ref, b_ref, ra_ref, rb_ref, *rest):
    outs, (att, rows) = rest[:n_groups * halves], rest[n_groups * halves:]
    n, width, tokens = q_ref.shape
    attend(frame, place, counts, lists, q_ref, (a_ref, b_ref, ra_ref, rb_ref), att)
    for f in range(n):
        rows[:, f * width:(f + 1) * width] = att[f].T.astype(BF)
    size = tokens // n_groups // halves
    for half in range(halves):
        for j in range(n_groups):
            start = (peer(place[0], j, n_groups) * halves + half) * size
            outs[half * n_groups + j][...] = rows[pl.ds(pl.multiple_of(start, SUB), size), :]


def mix_kernel(*refs):
    atts, hids = refs[:len(refs) // 2 - 1], refs[len(refs) // 2 - 1:-3]
    w_ref, g_ref, out = refs[-3:]
    width = w_ref.shape[0]
    n, _, _ = hids[0].shape

    def block(j, f):
        def finish(normed):
            out[j, f] = (hids[j][f].astype(F32) + normed * g_ref[...]).astype(BF)

        return lambda: contract(atts[j][:, f * width:(f + 1) * width], w_ref[...], 1, 0), finish

    add_normed([block(j, f) for j in range(len(atts)) for f in range(n)])


def paired(chunks, lanes, frames):
    return chunks % 2 == 0 and frames % 2 == 0 and 2 * lanes == TILE


def slot(c, frame, chunks, n_groups, frames):
    return c ^ (frame & 1) if paired(chunks, n_groups * SUB, frames) else c


def project(w_ref, x, out):
    width = w_ref.shape[0] // 3
    cut = w_ref.shape[0] // 2
    heads = width // HEAD_DIM
    parts = [contract(w_ref[i * cut:(i + 1) * cut, :], x[...], 1, 1) for i in range(2)]
    for h in range(3 * heads):
        i, at = divmod(h * HEAD_DIM, cut)
        y = parts[i][at:at + HEAD_DIM, :]
        if h < 2 * heads:
            y = y * head_scale(y)
        out[head(h), :] = y.astype(BF)


def project_kernel(frame, frames, *refs):
    pieces, w_ref, out, x = refs[:-3], refs[-3], refs[-2], refs[-1]
    n_groups = len(pieces)
    chunks = pieces[0].shape[0] // SUB
    for c in range(chunks):
        for j, piece in enumerate(pieces):
            at = (slot(c, frame, chunks, n_groups, frames) * n_groups + j) * SUB
            x[at:at + SUB, :] = piece[c * SUB:(c + 1) * SUB, :]
    project(w_ref, x, out)


def late_project_kernel(frame, frames, *refs):
    n_groups = (len(refs) - 7) // 2
    atts, hids = refs[:n_groups], refs[n_groups:2 * n_groups]
    w_ref, g_ref, qkv_ref, out, a, b, x = refs[2 * n_groups:]
    width = w_ref.shape[0]
    n, rows, _ = hids[0].shape
    chunks = rows // SUB
    for f in range(n):
        for c in range(chunks):
            for j in range(n_groups):
                at = ((f * chunks + slot(c, frame + f, chunks, n_groups, frames)) * n_groups + j) * SUB
                piece = slice(c * SUB, (c + 1) * SUB)
                a[at:at + SUB, :] = atts[j][piece, f * width:(f + 1) * width]
                b[at:at + SUB, :] = hids[j][f, piece, :]

    def block(at):
        cut = slice(at, at + TILE)

        def finish(normed):
            x[cut, :] = (b[cut, :].astype(F32) + normed * g_ref[...]).astype(BF)

        return lambda: contract(a[cut, :], w_ref[...], 1, 0), finish

    add_normed([block(at) for at in range(0, x.shape[0], TILE)])
    project(qkv_ref, x, out)


def temporal_kernel(n_groups, *refs):
    frames = len(refs) - n_groups - 1
    ins, outs, att = refs[:frames], refs[frames:frames + n_groups], refs[-1]
    lanes = n_groups * SUB
    chunks = ins[0].shape[1] // lanes
    width = ins[0].shape[0] // 3
    rows = frames * lanes
    pair = paired(chunks, lanes, frames)
    row_pos = lax.broadcasted_iota(jnp.int32, (rows, rows), 0) % SUB
    col_pos = lax.broadcasted_iota(jnp.int32, (rows, rows), 1) % SUB
    same = jnp.where(row_pos == col_pos, 1.0, 0.0).astype(F32)
    low = lax.broadcasted_iota(jnp.int32, (HEAD_DIM, TILE), 1) < lanes

    def take(c, where):
        if not pair:
            return jnp.concatenate([r[where, c * lanes:(c + 1) * lanes] for r in ins], axis=1)
        tile = slice(c // 2 * TILE, (c // 2 + 1) * TILE)
        got = [r[where, tile] for r in ins]
        return jnp.concatenate(
            [
                jnp.where(low, got[m + (c & 1)], got[m + 1 - (c & 1)])
                for m in range(0, frames, 2)
            ],
            axis=1,
        )

    def scores(c, h):
        return contract(take(c, head(h, width)), take(c, head(h)), 0, 0)

    def weigh(s):
        p = jnp.exp2(s * EXP2_SCALE) * same
        return jnp.sum(p, axis=0, keepdims=True), p.astype(BF)

    def gather(c, h, total, p):
        att[c, head(h), :] = contract(take(c, head(h, 2 * width)), p, 1, 0) / total

    steps = [(c, h) for c in range(chunks) for h in range(width // HEAD_DIM)]
    pipeline(steps, scores, weigh, gather)
    turned = [att[c].T.astype(BF) for c in range(chunks)]
    for j, out in enumerate(outs):
        for c in range(chunks):
            for f in range(frames):
                at = (f ^ (c & 1) if pair else f) * lanes + j * SUB
                out[c * SUB:(c + 1) * SUB, f * width:(f + 1) * width] = turned[c][at:at + SUB, :]


def output_kernel(n_groups, js, early, half, halves, aliased, place, *refs):
    n = len(js)
    atts, pieces = refs[:n], refs[n:n * (1 + early)]
    late_ref, w_ref, g_ref = refs[n * (1 + early):n * (1 + early) + 3]
    out, buf, sems = refs[n * (1 + early) + 3 + aliased:]
    _, late, rows, _ = late_ref.shape
    width = w_ref.shape[0]
    frames = early + late
    copies = []

    def block(i, j):
        def start():
            x = jnp.concatenate([atts[i][:, f * width:(f + 1) * width] for f in range(frames)], axis=0)
            return contract(x, w_ref[...], 1, 0)

        def finish(normed):
            for f in range(frames):
                mine = pieces[i * early + f][...] if f < early else late_ref[j, f - early]
                part = normed[f * rows:(f + 1) * rows, :] * g_ref[...]
                buf[i, f] = (mine.astype(F32) + part).astype(BF)
            group = peer(place[0], j, n_groups)
            at = pl.multiple_of((group * halves + half) * rows, SUB)
            copy = pltpu.make_async_copy(buf.at[i], out.at[:, pl.ds(at, rows), :], sems.at[i])
            copy.start()
            copies.append(copy)

        return start, finish

    add_normed([block(i, j) for i, j in enumerate(js)])
    for copy in copies:
        copy.wait()


def shards(
    spatial_queries,
    spatial_keys,
    spatial_values,
    hidden,
    spatial_out_weight,
    spatial_gain,
    temporal_qkv_weight,
    temporal_out_weight,
    temporal_gain,
    tile_list,
    tile_count,
):
    frames, tokens, width = spatial_queries.shape
    model = hidden.shape[2]
    groups = lax.axis_size("frame")
    strips = lax.axis_size("strip")
    share = tokens // groups
    halves = 2 if share % (4 * SUB) == 0 else 1
    rows = share // halves
    queries = jnp.transpose(spatial_queries, (0, 2, 1))
    keys = pltpu.with_memory_space_constraint(jnp.transpose(spatial_keys, (0, 2, 1)), pltpu.HBM)
    values = pltpu.with_memory_space_constraint(jnp.transpose(spatial_values, (0, 2, 1)), pltpu.HBM)
    hidden_far = pltpu.with_memory_space_constraint(hidden, pltpu.HBM)
    lists = jnp.transpose(tile_list, (2, 1, 0))
    counts = tile_count.T
    qkv_weight = temporal_qkv_weight.T
    gain_one = spatial_gain.reshape(1, model)
    gain_two = temporal_gain.reshape(1, model)
    place = jnp.stack([lax.axis_index("frame"), lax.axis_index("strip")]).astype(jnp.int32)
    near = [(i, i ^ 1) for i in range(strips) if i ^ 1 < strips]
    far = [e for i in range(1, strips - 1, 2) for e in ((i, i + 1), (i + 1, i))]
    edge = jax.ShapeDtypeStruct((2 * width, TILE), BF)
    smem = pl.BlockSpec(memory_space=pltpu.SMEM)
    any_spec = pl.BlockSpec(memory_space=pl.ANY)

    def call(kernel, in_specs, out_specs, out_shape, scratch=(), limit=32, prefetch=0, alias=None):
        return pl.pallas_call(
            kernel,
            grid_spec=pltpu.PrefetchScalarGridSpec(
                num_scalar_prefetch=prefetch,
                grid=(1,),
                in_specs=in_specs,
                out_specs=out_specs,
                scratch_shapes=list(scratch),
            ),
            out_shape=out_shape,
            input_output_aliases=alias or {},
            compiler_params=vmem(limit),
        )

    def frame_block(f):
        return pl.BlockSpec((1, width, tokens), lambda *_: (f, 0, 0))

    late = frames // 2
    early = frames - late

    halos = []
    for some in range(2):
        block = pl.BlockSpec((late, width, tokens), lambda *_, some=some: (some, 0, 0))
        a, b = call(
            prep_kernel,
            [smem, block, block],
            [whole((late,) + edge.shape)] * 2,
            [jax.ShapeDtypeStruct((late,) + edge.shape, BF)] * 2,
            limit=16,
        )(place, keys, values)
        halos.append((a, b, lax.ppermute(a, "strip", near), lax.ppermute(b, "strip", far)))

    def out_pairs(j):
        return [(i, peer(i, j, groups)) for i in range(groups)]

    def send(x, j):
        return x if j == 0 else lax.ppermute(x, "frame", out_pairs(j))

    own_hidden = call(
        split_kernel,
        [smem, any_spec],
        [any_spec] * groups,
        [jax.ShapeDtypeStruct((late, share, model), BF)] * groups,
        [pltpu.SemaphoreType.DMA((groups,))],
        limit=16,
    )(place, hidden_far)
    far_hidden = [send(x, j) for j, x in enumerate(own_hidden)]

    mixed = [[None] * early for _ in range(groups)]
    projected = []
    for f in range(early):
        edge_block = pl.BlockSpec((1,) + edge.shape, lambda *_, f=f: (f, 0, 0))
        parts = call(
            functools.partial(spatial_kernel, f, groups),
            [smem, smem, smem, frame_block(f)]
            + [edge_block] * 4
            + [
                pl.BlockSpec((1, tokens, model), lambda *_, f=f: (f, 0, 0)),
                whole((width, model)),
                whole((1, model)),
            ],
            [whole((share, model))] * groups,
            [jax.ShapeDtypeStruct((share, model), BF)] * groups,
            [pltpu.VMEM((1, width, tokens), BF), pltpu.VMEM((tokens, model), BF)],
        )(place, counts, lists, queries, *halos[0], hidden, spatial_out_weight, gain_one)
        for j in range(groups):
            mixed[j][f] = parts[j]
        arrived = [send(x, j) for j, x in enumerate(parts)]
        projected.append(
            call(
                functools.partial(project_kernel, f, frames),
                [whole((share, model))] * groups + [whole((3 * width, model))],
                whole((3 * width, tokens)),
                jax.ShapeDtypeStruct((3 * width, tokens), BF),
                [pltpu.VMEM((tokens, model), BF)],
            )(*arrived, qkv_weight)
        )

    late_shape = (rows, late * width)
    own_late = call(
        functools.partial(late_kernel, early, groups, halves),
        [smem, smem, smem, pl.BlockSpec((late, width, tokens), lambda *_: (1, 0, 0))]
        + [whole((late,) + edge.shape)] * 4,
        [whole(late_shape)] * (groups * halves),
        [jax.ShapeDtypeStruct(late_shape, BF)] * (groups * halves),
        [pltpu.VMEM((late, width, tokens), F32), pltpu.VMEM((tokens, late * width), BF)],
    )(place, counts, lists, queries, *halos[1])
    own_late = [own_late[half * groups:(half + 1) * groups] for half in range(halves)]
    far_late = []
    for half in range(halves):
        far_late.append([send(x, j) for j, x in enumerate(own_late[half])])

    returned, late_mixed = [], []
    back_shape = (rows, frames * width)
    lanes = tokens // halves
    for half in range(halves):
        hid_block = pl.BlockSpec((late, rows, model), lambda *_, half=half: (0, half, 0))
        late_specs = [whole(late_shape)] * groups + [hid_block] * groups
        late_specs += [whole((width, model)), whole((1, model))]
        late_projected = call(
            functools.partial(late_project_kernel, early, frames),
            late_specs + [whole((3 * width, model))],
            whole((3 * width, late * lanes)),
            jax.ShapeDtypeStruct((3 * width, late * lanes), BF),
            [
                pltpu.VMEM((late * lanes, width), BF),
                pltpu.VMEM((late * lanes, model), BF),
                pltpu.VMEM((late * lanes, model), BF),
            ],
        )(*far_late[half], *far_hidden, spatial_out_weight, gain_one, qkv_weight)
        back = call(
            functools.partial(temporal_kernel, groups),
            [pl.BlockSpec((3 * width, lanes), lambda *_, half=half: (0, half))] * early
            + [pl.BlockSpec((3 * width, lanes), lambda *_, f=f: (0, f)) for f in range(late)],
            [whole(back_shape)] * groups,
            [jax.ShapeDtypeStruct(back_shape, BF)] * groups,
            [pltpu.VMEM((rows // SUB, width, groups * frames * SUB), F32)],
        )(*projected, *[late_projected] * late)
        got = []
        for j in range(groups):
            pairs = [(b, a) for a, b in out_pairs(j)]
            got.append(back[j] if j == 0 else lax.ppermute(back[j], "frame", pairs))
        returned.append(got)
        late_mixed.append(
            call(
                mix_kernel,
                late_specs,
                whole((groups, late, rows, model)),
                jax.ShapeDtypeStruct((groups, late, rows, model), BF),
            )(*own_late[half], *own_hidden, spatial_out_weight, gain_one)
        )

    out = None
    for half in range(halves):
        piece = pl.BlockSpec((rows, model), lambda *_, half=half: (half, 0))
        cuts = [groups]
        for lo, hi in zip([0] + cuts, cuts):
            js = range(lo, hi)
            if not js:
                continue
            extra = [] if out is None else [out]
            out = call(
                functools.partial(output_kernel, groups, tuple(js), early, half, halves, len(extra)),
                [smem]
                + [whole(back_shape)] * len(js)
                + [piece] * (len(js) * early)
                + [whole((groups, late, rows, model)), whole((width, model)), whole((1, model))]
                + [any_spec] * len(extra),
                any_spec,
                jax.ShapeDtypeStruct((frames, tokens, model), BF),
                [
                    pltpu.VMEM((len(js), frames, rows, model), BF),
                    pltpu.SemaphoreType.DMA((len(js),)),
                ],
                alias={4 + len(js) * (1 + early): 0} if extra else None,
            )(
                place,
                *[returned[half][j] for j in js],
                *[mixed[j][f] for j in js for f in range(early)],
                late_mixed[half],
                temporal_out_weight,
                gain_two,
                *extra,
            )
    return out


def solution(mesh):
    rows = P(("group", "frame"), "strip", None)
    placed = (rows, rows, rows, rows, P(), P(), P(), P(), P(), rows, P(("group", "frame"), "strip"))

    return jax.shard_map(shards, mesh=mesh, in_specs=placed, out_specs=rows, check_vma=False)
```

```python
import functools
import math

import jax
import jax.numpy as jnp
from jax import lax
from jax.experimental import pallas as pl
from jax.experimental.pallas import tpu as pltpu
from jax.sharding import PartitionSpec as P


HEAD_DIM = 72
TILE = 128
MAXT = 3
SUB = 16
EPS = 1e-06
EXP2_SCALE = HEAD_DIM ** -0.5 * math.log2(math.e)

BF = jnp.bfloat16
F32 = jnp.float32


def peer(i, j, n):
    return i ^ j if n & (n - 1) == 0 else (i + j) % n


def vmem(limit):
    return pltpu.CompilerParams(vmem_limit_bytes=limit << 20)


def whole(shape):
    return pl.BlockSpec(shape, lambda *_: (0,) * len(shape))


def contract(a, b, da, db):
    return lax.dot_general(a, b, (((da,), (db,)), ((), ())), preferred_element_type=F32)


def head_scale(x):
    return lax.rsqrt(jnp.mean(x * x, axis=0, keepdims=True) + EPS)


def head(h, base=0):
    return slice(base + h * HEAD_DIM, base + (h + 1) * HEAD_DIM)


def with_ones(v):
    return jnp.concatenate([v, jnp.ones((8, v.shape[1]), v.dtype)], axis=0)


def averaged(o):
    return o[:HEAD_DIM, :] / o[HEAD_DIM:HEAD_DIM + 1, :]


def pipeline(steps, scores, weigh, gather):
    ahead, behind = scores(*steps[0]), None
    for n, step in enumerate(steps):
        now = ahead
        if n + 1 < len(steps):
            ahead = scores(*steps[n + 1])
        weighed = weigh(now)
        if behind is not None:
            gather(*steps[n - 1], behind)
        behind = weighed
    gather(*steps[-1], behind)


def prep_kernel(place, k_ref, v_ref, *refs):
    n, width, _ = k_ref.shape
    even = place[1] % 2 == 0
    copies = []
    if len(refs) > 2:
        src, (a_ref, b_ref), pieces, sems = refs[0], refs[1:3], refs[3:-1], refs[-1]
        late, share, _ = pieces[0].shape
        for j in reversed(range(len(pieces))):
            start = pl.multiple_of(peer(place[0], j, len(pieces)) * share, SUB)
            part = src.at[pl.ds(src.shape[0] - late, late), pl.ds(start, share), :]
            copies.append(pltpu.make_async_copy(part, pieces[j], sems.at[j]))
            copies[-1].start()
    else:
        a_ref, b_ref = refs

    def fill(first, second):
        for f in range(n):
            for h in range(width // HEAD_DIM):
                x = k_ref[f, head(h), :].astype(F32)
                y = (x * head_scale(x)).astype(BF)
                first[f, head(h), :] = y[:, :TILE]
                second[f, head(h), :] = y[:, TILE:]
            first[f, width:, :] = v_ref[f, :, :TILE]
            second[f, width:, :] = v_ref[f, :, TILE:]

    pl.when(even)(functools.partial(fill, b_ref, a_ref))
    pl.when(jnp.logical_not(even))(functools.partial(fill, a_ref, b_ref))
    for copy in copies:
        copy.wait()


def attend(frame, place, counts, lists, q_ref, keys, att):
    n, width, tokens = q_ref.shape
    tiles = tokens // TILE
    strip = place[1]
    odd = strip % 2
    first = strip * tiles
    places = (first + 1 - odd, first + odd, first + 2 - 3 * odd, first - 1 + 3 * odd)
    masks = []
    for f in range(n):
        table = []
        for t in range(tiles):
            live = counts[t, frame + f]
            cells = []
            for spot in places:
                hit = jnp.bool_(False)
                for j in range(MAXT):
                    hit = hit | ((lists[j, t, frame + f] == spot) & (j < live))
                cells.append(jnp.full((SUB, TILE), jnp.where(hit, 1.0, 0.0), F32))
            table.append(cells)
        masks.append([jnp.concatenate(row, axis=1).astype(BF) for row in zip(*table)])

    def scores(f, h):
        q = q_ref[f, head(h), :].astype(F32)
        qn = (q * head_scale(q)).astype(BF)
        return f, [contract(ref[f, head(h), :], qn, 0, 0) for ref in keys]

    def weigh(scored):
        f, s = scored
        packed = []
        for i, x in enumerate(s):
            p = jnp.exp2(x * EXP2_SCALE).astype(BF).reshape(TILE // SUB, SUB, tokens)
            packed.append((p * masks[f][i]).reshape(TILE, tokens))
        return [jnp.concatenate(packed[i:i + 2], axis=0) for i in (0, 2)]

    def gather(f, h, halves):
        o = 0
        for i in range(2):
            v = jnp.concatenate([r[f, head(h, width), :] for r in keys[2 * i:2 * i + 2]], axis=1)
            o += contract(with_ones(v), halves[i], 1, 0)
        att[f, head(h), :] = averaged(o).astype(att.dtype)

    pipeline([(f, h) for f in range(n) for h in range(width // HEAD_DIM)], scores, weigh, gather)


def add_normed(blocks):
    ahead = blocks[0][0]()
    for n, (_, finish) in enumerate(blocks):
        proj = ahead
        if n + 1 < len(blocks):
            ahead = blocks[n + 1][0]()
        scale = lax.rsqrt(jnp.mean(proj * proj, axis=-1, keepdims=True) + EPS)
        finish(proj * scale)


def spatial_kernel(frame, n_groups, place, counts, lists, q_ref, a_ref, b_ref, ra_ref, rb_ref, h_ref, w_ref, g_ref, *rest):
    outs, (att, mix) = rest[:n_groups], rest[n_groups:]
    attend(frame, place, counts, lists, q_ref, (a_ref, b_ref, ra_ref, rb_ref), att)

    def finish(normed):
        mix[...] = (h_ref[0].astype(F32) + normed * g_ref[...]).astype(BF)

    add_normed([(lambda: contract(att[0], w_ref[...], 0, 0), finish)])
    share = mix.shape[0] // n_groups
    for j, out in enumerate(outs):
        group = peer(place[0], j, n_groups)
        out[...] = mix[pl.ds(pl.multiple_of(group * share, SUB), share), :]


def late_kernel(frame, n_groups, halves, place, counts, lists, q_ref, a_ref, b_ref, ra_ref, rb_ref, *rest):
    outs, (att, rows) = rest[:n_groups * halves], rest[n_groups * halves:]
    n, width, tokens = q_ref.shape
    attend(frame, place, counts, lists, q_ref, (a_ref, b_ref, ra_ref, rb_ref), att)
    for f in range(n):
        rows[:, f * width:(f + 1) * width] = att[f].T.astype(BF)
    size = tokens // n_groups // halves
    for half in range(halves):
        for j in range(n_groups):
            start = (peer(place[0], j, n_groups) * halves + half) * size
            outs[half * n_groups + j][...] = rows[pl.ds(pl.multiple_of(start, SUB), size), :]


def mix_kernel(*refs):
    w_ref, g_ref, out = refs[-3:]
    n_groups, n, share, _ = out.shape
    atts, hids = refs[:-3 - n_groups], refs[-3 - n_groups:-3]
    width = w_ref.shape[0]
    rows = atts[0].shape[0]
    halves = share // rows

    def block(js):
        def start():
            x = [
                atts[half * n_groups + j][:, f * width:(f + 1) * width]
                for j in js
                for f in range(n)
                for half in range(halves)
            ]
            return contract(jnp.concatenate(x, axis=0), w_ref[...], 1, 0)

        def finish(normed):
            for i, j in enumerate(js):
                for f in range(n):
                    at = (i * n + f) * share
                    part = normed[at:at + share, :] * g_ref[...]
                    out[j, f] = (hids[j][f].astype(F32) + part).astype(BF)

        return start, finish

    add_normed([block(js) for js in blocks_of(n_groups, n * share)])


def blocks_of(n_groups, rows):
    size = max(1, min(n_groups, 2 * TILE // rows))
    return [range(at, min(at + size, n_groups)) for at in range(0, n_groups, size)]


def paired(chunks, lanes, frames):
    return chunks % 2 == 0 and frames % 2 == 0 and 2 * lanes == TILE


def slot(c, frame, chunks, n_groups, frames):
    return c ^ (frame & 1) if paired(chunks, n_groups * SUB, frames) else c


def project(w_ref, x, out):
    width = w_ref.shape[0] // 3
    cut = w_ref.shape[0] // 2
    heads = width // HEAD_DIM
    parts = [contract(w_ref[i * cut:(i + 1) * cut, :], x[...], 1, 1) for i in range(2)]
    for h in range(3 * heads):
        i, at = divmod(h * HEAD_DIM, cut)
        y = parts[i][at:at + HEAD_DIM, :]
        if h < 2 * heads:
            y = y * head_scale(y)
        out[head(h), :] = y.astype(BF)


def project_kernel(frame, frames, *refs):
    pieces, w_ref, out, x = refs[:-3], refs[-3], refs[-2], refs[-1]
    n_groups = len(pieces)
    chunks = pieces[0].shape[0] // SUB
    for c in range(chunks):
        for j, piece in enumerate(pieces):
            at = (slot(c, frame, chunks, n_groups, frames) * n_groups + j) * SUB
            x[at:at + SUB, :] = piece[c * SUB:(c + 1) * SUB, :]
    project(w_ref, x, out)


def late_project_kernel(frame, frames, *refs):
    n_groups = (len(refs) - 7) // 2
    atts, hids = refs[:n_groups], refs[n_groups:2 * n_groups]
    w_ref, g_ref, qkv_ref, out, a, b, x = refs[2 * n_groups:]
    width = w_ref.shape[0]
    n, rows, _ = hids[0].shape
    chunks = rows // SUB
    for f in range(n):
        for c in range(chunks):
            for j in range(n_groups):
                at = ((f * chunks + slot(c, frame + f, chunks, n_groups, frames)) * n_groups + j) * SUB
                piece = slice(c * SUB, (c + 1) * SUB)
                a[at:at + SUB, :] = atts[j][piece, f * width:(f + 1) * width]
                b[at:at + SUB, :] = hids[j][f, piece, :]

    def finish(normed):
        x[...] = (b[...].astype(F32) + normed * g_ref[...]).astype(BF)

    add_normed([(lambda: contract(a[...], w_ref[...], 1, 0), finish)])
    project(qkv_ref, x, out)


def temporal_kernel(n_groups, *refs):
    frames = len(refs) - n_groups - 1
    ins, outs, att = refs[:frames], refs[frames:frames + n_groups], refs[-1]
    lanes = n_groups * SUB
    chunks = ins[0].shape[1] // lanes
    width = ins[0].shape[0] // 3
    rows = frames * lanes
    pair = paired(chunks, lanes, frames)
    row_pos = lax.broadcasted_iota(jnp.int32, (rows, rows), 0) % SUB
    col_pos = lax.broadcasted_iota(jnp.int32, (rows, rows), 1) % SUB
    same = jnp.where(row_pos == col_pos, 1.0, 0.0).astype(BF)
    low = lax.broadcasted_iota(jnp.int32, (HEAD_DIM, TILE), 1) < lanes

    def take(c, where):
        if not pair:
            return jnp.concatenate([r[where, c * lanes:(c + 1) * lanes] for r in ins], axis=1)
        tile = slice(c // 2 * TILE, (c // 2 + 1) * TILE)
        got = [r[where, tile] for r in ins]
        return jnp.concatenate(
            [
                jnp.where(low, got[m + (c & 1)], got[m + 1 - (c & 1)])
                for m in range(0, frames, 2)
            ],
            axis=1,
        )

    def scores(c, h):
        return contract(take(c, head(h, width)), take(c, head(h)), 0, 0)

    def weigh(s):
        return jnp.exp2(s * EXP2_SCALE).astype(BF) * same

    def gather(c, h, p):
        att[c, head(h), :] = averaged(contract(with_ones(take(c, head(h, 2 * width))), p, 1, 0))

    steps = [(c, h) for c in range(chunks) for h in range(width // HEAD_DIM)]
    pipeline(steps, scores, weigh, gather)
    turned = [att[c].T.astype(BF) for c in range(chunks)]
    for j, out in enumerate(outs):
        for c in range(chunks):
            for f in range(frames):
                at = (f ^ (c & 1) if pair else f) * lanes + j * SUB
                out[c * SUB:(c + 1) * SUB, f * width:(f + 1) * width] = turned[c][at:at + SUB, :]


def output_kernel(n_groups, js, early, half, halves, aliased, place, *refs):
    n = len(js)
    atts, pieces = refs[:n], refs[n:n * (1 + early)]
    late_ref, w_ref, g_ref = refs[n * (1 + early):n * (1 + early) + 3]
    out, buf, sems = refs[n * (1 + early) + 3 + aliased:]
    _, late, rows, _ = late_ref.shape
    width = w_ref.shape[0]
    frames = early + late
    copies = []

    def block(some):
        def start():
            x = [atts[i][:, f * width:(f + 1) * width] for i in some for f in range(frames)]
            return contract(jnp.concatenate(x, axis=0), w_ref[...], 1, 0)

        def finish(normed):
            for k, i in enumerate(some):
                j = js[i]
                for f in range(frames):
                    mine = pieces[i * early + f][...] if f < early else late_ref[j, f - early]
                    at = (k * frames + f) * rows
                    part = normed[at:at + rows, :] * g_ref[...]
                    buf[i, f] = (mine.astype(F32) + part).astype(BF)
                group = peer(place[0], j, n_groups)
                at = pl.multiple_of((group * halves + half) * rows, SUB)
                copy = pltpu.make_async_copy(buf.at[i], out.at[:, pl.ds(at, rows), :], sems.at[i])
                copy.start()
                copies.append(copy)

        return start, finish

    add_normed([block(some) for some in blocks_of(len(js), frames * rows)])
    for copy in copies:
        copy.wait()


def shards(
    spatial_queries,
    spatial_keys,
    spatial_values,
    hidden,
    spatial_out_weight,
    spatial_gain,
    temporal_qkv_weight,
    temporal_out_weight,
    temporal_gain,
    tile_list,
    tile_count,
):
    frames, tokens, width = spatial_queries.shape
    model = hidden.shape[2]
    groups = lax.axis_size("frame")
    strips = lax.axis_size("strip")
    share = tokens // groups
    halves = 2 if share % (4 * SUB) == 0 else 1
    rows = share // halves
    queries = jnp.transpose(spatial_queries, (0, 2, 1))
    keys = pltpu.with_memory_space_constraint(jnp.transpose(spatial_keys, (0, 2, 1)), pltpu.HBM)
    values = pltpu.with_memory_space_constraint(jnp.transpose(spatial_values, (0, 2, 1)), pltpu.HBM)
    hidden_far = pltpu.with_memory_space_constraint(hidden, pltpu.HBM)
    lists = jnp.transpose(tile_list, (2, 1, 0))
    counts = tile_count.T
    qkv_weight = temporal_qkv_weight.T
    gain_one = spatial_gain.reshape(1, model)
    gain_two = temporal_gain.reshape(1, model)
    place = jnp.stack([lax.axis_index("frame"), lax.axis_index("strip")]).astype(jnp.int32)
    near = [(i, i ^ 1) for i in range(strips) if i ^ 1 < strips]
    far = [e for i in range(1, strips - 1, 2) for e in ((i, i + 1), (i + 1, i))]
    edge = jax.ShapeDtypeStruct((2 * width, TILE), BF)
    smem = pl.BlockSpec(memory_space=pltpu.SMEM)
    any_spec = pl.BlockSpec(memory_space=pl.ANY)

    def call(kernel, in_specs, out_specs, out_shape, scratch=(), limit=32, prefetch=0, alias=None):
        return pl.pallas_call(
            kernel,
            grid_spec=pltpu.PrefetchScalarGridSpec(
                num_scalar_prefetch=prefetch,
                grid=(1,),
                in_specs=in_specs,
                out_specs=out_specs,
                scratch_shapes=list(scratch),
            ),
            out_shape=out_shape,
            input_output_aliases=alias or {},
            compiler_params=vmem(limit),
        )

    def frame_block(f):
        return pl.BlockSpec((1, width, tokens), lambda *_: (f, 0, 0))

    late = frames // 2
    early = frames - late

    def out_pairs(j):
        return [(i, peer(i, j, groups)) for i in range(groups)]

    def send(parts):
        sent = {j: lax.ppermute(parts[j], "frame", out_pairs(j)) for j in reversed(range(1, groups))}
        return [parts[0]] + [sent[j] for j in range(1, groups)]

    halos = []
    for some in range(2):
        block = pl.BlockSpec((late, width, tokens), lambda *_, some=some: (some, 0, 0))
        split = groups if some == 0 else 0
        a, b, *pieces = call(
            prep_kernel,
            [smem, block, block] + [any_spec] * bool(split),
            [whole((late,) + edge.shape)] * 2 + [any_spec] * split,
            [jax.ShapeDtypeStruct((late,) + edge.shape, BF)] * 2
            + [jax.ShapeDtypeStruct((late, share, model), BF)] * split,
            [pltpu.SemaphoreType.DMA((groups,))] * bool(split),
            limit=16,
        )(place, keys, values, *[hidden_far] * bool(split))
        if split:
            own_hidden = pieces
        halos.append((a, b, lax.ppermute(a, "strip", near), lax.ppermute(b, "strip", far)))
    far_hidden = send(own_hidden)

    mixed = [[None] * early for _ in range(groups)]
    projected = []
    for f in range(early):
        edge_block = pl.BlockSpec((1,) + edge.shape, lambda *_, f=f: (f, 0, 0))
        parts = call(
            functools.partial(spatial_kernel, f, groups),
            [smem, smem, smem, frame_block(f)]
            + [edge_block] * 4
            + [
                pl.BlockSpec((1, tokens, model), lambda *_, f=f: (f, 0, 0)),
                whole((width, model)),
                whole((1, model)),
            ],
            [whole((share, model))] * groups,
            [jax.ShapeDtypeStruct((share, model), BF)] * groups,
            [pltpu.VMEM((1, width, tokens), BF), pltpu.VMEM((tokens, model), BF)],
        )(place, counts, lists, queries, *halos[0], hidden, spatial_out_weight, gain_one)
        for j in range(groups):
            mixed[j][f] = parts[j]
        arrived = send(parts)
        projected.append(
            call(
                functools.partial(project_kernel, f, frames),
                [whole((share, model))] * groups + [whole((3 * width, model))],
                whole((3 * width, tokens)),
                jax.ShapeDtypeStruct((3 * width, tokens), BF),
                [pltpu.VMEM((tokens, model), BF)],
            )(*arrived, qkv_weight)
        )

    late_shape = (rows, late * width)
    own_late = call(
        functools.partial(late_kernel, early, groups, halves),
        [smem, smem, smem, pl.BlockSpec((late, width, tokens), lambda *_: (1, 0, 0))]
        + [whole((late,) + edge.shape)] * 4,
        [whole(late_shape)] * (groups * halves),
        [jax.ShapeDtypeStruct(late_shape, BF)] * (groups * halves),
        [pltpu.VMEM((late, width, tokens), F32), pltpu.VMEM((tokens, late * width), BF)],
    )(place, counts, lists, queries, *halos[1])
    own_late = [own_late[half * groups:(half + 1) * groups] for half in range(halves)]
    far_late = []
    for half in range(halves):
        far_late.append(send(own_late[half]))

    returned = []
    back_shape = (rows, frames * width)
    lanes = tokens // halves
    for half in range(halves):
        hid_block = pl.BlockSpec((late, rows, model), lambda *_, half=half: (0, half, 0))
        late_specs = [whole(late_shape)] * groups + [hid_block] * groups
        late_specs += [whole((width, model)), whole((1, model))]
        late_projected = call(
            functools.partial(late_project_kernel, early, frames),
            late_specs + [whole((3 * width, model))],
            whole((3 * width, late * lanes)),
            jax.ShapeDtypeStruct((3 * width, late * lanes), BF),
            [
                pltpu.VMEM((late * lanes, width), BF),
                pltpu.VMEM((late * lanes, model), BF),
                pltpu.VMEM((late * lanes, model), BF),
            ],
        )(*far_late[half], *far_hidden, spatial_out_weight, gain_one, qkv_weight)
        back = call(
            functools.partial(temporal_kernel, groups),
            [pl.BlockSpec((3 * width, lanes), lambda *_, half=half: (0, half))] * early
            + [pl.BlockSpec((3 * width, lanes), lambda *_, f=f: (0, f)) for f in range(late)],
            [whole(back_shape)] * groups,
            [jax.ShapeDtypeStruct(back_shape, BF)] * groups,
            [pltpu.VMEM((rows // SUB, width, groups * frames * SUB), F32)],
        )(*projected, *[late_projected] * late)
        home = {
            j: lax.ppermute(back[j], "frame", [(b, a) for a, b in out_pairs(j)])
            for j in reversed(range(1, groups))
        }
        returned.append([back[0]] + [home[j] for j in range(1, groups)])

    late_mixed = call(
        mix_kernel,
        [whole(late_shape)] * (groups * halves)
        + [whole((late, share, model))] * groups
        + [whole((width, model)), whole((1, model))],
        whole((groups, late, share, model)),
        jax.ShapeDtypeStruct((groups, late, share, model), BF),
    )(*[x for some in own_late for x in some], *own_hidden, spatial_out_weight, gain_one)

    out = None
    for half in range(halves):
        piece = pl.BlockSpec((rows, model), lambda *_, half=half: (half, 0))
        cuts = [groups]
        for lo, hi in zip([0] + cuts, cuts):
            js = range(lo, hi)
            if not js:
                continue
            extra = [] if out is None else [out]
            out = call(
                functools.partial(output_kernel, groups, tuple(js), early, half, halves, len(extra)),
                [smem]
                + [whole(back_shape)] * len(js)
                + [piece] * (len(js) * early)
                + [pl.BlockSpec((groups, late, rows, model), lambda *_, half=half: (0, 0, half, 0))]
                + [whole((width, model)), whole((1, model))]
                + [any_spec] * len(extra),
                any_spec,
                jax.ShapeDtypeStruct((frames, tokens, model), BF),
                [
                    pltpu.VMEM((len(js), frames, rows, model), BF),
                    pltpu.SemaphoreType.DMA((len(js),)),
                ],
                alias={4 + len(js) * (1 + early): 0} if extra else None,
            )(
                place,
                *[returned[half][j] for j in js],
                *[mixed[j][f] for j in js for f in range(early)],
                late_mixed,
                temporal_out_weight,
                gain_two,
                *extra,
            )
    return out


def solution(mesh):
    rows = P(("group", "frame"), "strip", None)
    placed = (rows, rows, rows, rows, P(), P(), P(), P(), P(), rows, P(("group", "frame"), "strip"))

    return jax.shard_map(shards, mesh=mesh, in_specs=placed, out_specs=rows, check_vma=False)
```

```python
import functools
import math

import jax
import jax.numpy as jnp
from jax import lax
from jax.experimental import pallas as pl
from jax.experimental.pallas import tpu as pltpu
from jax.sharding import PartitionSpec as P


HEAD_DIM = 72
TILE = 128
MAXT = 3
SUB = 16
EPS = 1e-06
EXP2_SCALE = HEAD_DIM ** -0.5 * math.log2(math.e)

BF = jnp.bfloat16
F32 = jnp.float32


def peer(i, j, n):
    return i ^ j if n & (n - 1) == 0 else (i + j) % n


def vmem(limit):
    return pltpu.CompilerParams(vmem_limit_bytes=limit << 20)


def whole(shape):
    return pl.BlockSpec(shape, lambda *_: (0,) * len(shape))


def contract(a, b, da, db):
    return lax.dot_general(a, b, (((da,), (db,)), ((), ())), preferred_element_type=F32)


def head_scale(x):
    return lax.rsqrt(jnp.mean(x * x, axis=0, keepdims=True) + EPS)


def head(h, base=0):
    return slice(base + h * HEAD_DIM, base + (h + 1) * HEAD_DIM)


def with_ones(v):
    return jnp.concatenate([v, jnp.ones((8, v.shape[1]), v.dtype)], axis=0)


def averaged(o):
    return o[:HEAD_DIM, :] / o[HEAD_DIM:HEAD_DIM + 1, :]


def pipeline(steps, scores, weigh, gather):
    ahead, behind = scores(*steps[0]), None
    for n, step in enumerate(steps):
        now = ahead
        if n + 1 < len(steps):
            ahead = scores(*steps[n + 1])
        weighed = weigh(now)
        if behind is not None:
            gather(*steps[n - 1], behind)
        behind = weighed
    gather(*steps[-1], behind)


def prep_kernel(place, k_ref, v_ref, *refs):
    n, width, _ = k_ref.shape
    even = place[1] % 2 == 0
    copies = []
    if len(refs) > 2:
        src, (a_ref, b_ref), pieces, sems = refs[0], refs[1:3], refs[3:-1], refs[-1]
        late, share, _ = pieces[0].shape
        for j in reversed(range(len(pieces))):
            start = pl.multiple_of(peer(place[0], j, len(pieces)) * share, SUB)
            part = src.at[pl.ds(src.shape[0] - late, late), pl.ds(start, share), :]
            copies.append(pltpu.make_async_copy(part, pieces[j], sems.at[j]))
            copies[-1].start()
    else:
        a_ref, b_ref = refs

    def fill(first, second):
        for f in range(n):
            for h in range(width // HEAD_DIM):
                x = k_ref[f, head(h), :].astype(F32)
                y = (x * head_scale(x)).astype(BF)
                first[f, head(h), :] = y[:, :TILE]
                second[f, head(h), :] = y[:, TILE:]
            first[f, width:, :] = v_ref[f, :, :TILE]
            second[f, width:, :] = v_ref[f, :, TILE:]

    pl.when(even)(functools.partial(fill, b_ref, a_ref))
    pl.when(jnp.logical_not(even))(functools.partial(fill, a_ref, b_ref))
    for copy in copies:
        copy.wait()


def tile_masks(frame, n, tiles, local, place, counts, lists):
    strip = place[1]
    odd = strip % 2
    first = strip * tiles
    if local:
        spots = (first + 1 - odd, first + odd)
    else:
        spots = (first + 2 - 3 * odd, first - 1 + 3 * odd)
    masks = []
    for f in range(n):
        rows = []
        for spot in spots:
            cells = []
            for t in range(tiles):
                hit = jnp.bool_(False)
                for j in range(MAXT):
                    hit = hit | ((lists[j, t, frame + f] == spot) & (j < counts[t, frame + f]))
                cells.append(jnp.full((SUB, TILE), jnp.where(hit, 1.0, 0.0), F32))
            rows.append(jnp.concatenate(cells, axis=1).astype(BF))
        masks.append(rows)
    return masks


def attend(masks, keys, query, finish):
    n = keys[0].shape[0]
    width = keys[0].shape[1] // 2

    def scores(f, h):
        qn = query(f, h)
        return f, [contract(ref[f, head(h), :], qn, 0, 0) for ref in keys]

    def weigh(scored):
        f, s = scored
        packed = []
        for mask, x in zip(masks[f], s):
            p = jnp.exp2(x * EXP2_SCALE).astype(BF).reshape(TILE // SUB, SUB, x.shape[1])
            packed.append((p * mask).reshape(x.shape))
        return jnp.concatenate(packed, axis=0)

    def gather(f, h, weights):
        v = jnp.concatenate([ref[f, head(h, width), :] for ref in keys], axis=1)
        finish(f, h, contract(with_ones(v), weights, 1, 0))

    pipeline([(f, h) for f in range(n) for h in range(width // HEAD_DIM)], scores, weigh, gather)


def sums(h):
    return slice(h * (HEAD_DIM + 8), (h + 1) * (HEAD_DIM + 8))


def local_kernel(frame, place, counts, lists, q_ref, a_ref, b_ref, qn_ref, sum_ref):
    n, _, tokens = q_ref.shape

    def query(f, h):
        q = q_ref[f, head(h), :].astype(F32)
        qn = (q * head_scale(q)).astype(BF)
        qn_ref[f, head(h), :] = qn
        return qn

    def finish(f, h, o):
        sum_ref[f, sums(h), :] = o

    masks = tile_masks(frame, n, tokens // TILE, True, place, counts, lists)
    attend(masks, (a_ref, b_ref), query, finish)


def remote_attend(frame, place, counts, lists, qn_ref, sum_ref, ra_ref, rb_ref, att):
    n, _, tokens = qn_ref.shape

    def query(f, h):
        return qn_ref[f, head(h), :]

    def finish(f, h, o):
        att[f, head(h), :] = averaged(o + sum_ref[f, sums(h), :]).astype(att.dtype)

    masks = tile_masks(frame, n, tokens // TILE, False, place, counts, lists)
    attend(masks, (ra_ref, rb_ref), query, finish)


def add_normed(blocks):
    ahead = blocks[0][0]()
    for n, (_, finish) in enumerate(blocks):
        proj = ahead
        if n + 1 < len(blocks):
            ahead = blocks[n + 1][0]()
        scale = lax.rsqrt(jnp.mean(proj * proj, axis=-1, keepdims=True) + EPS)
        finish(proj * scale)


def spatial_kernel(n_groups, place, counts, lists, qn_ref, sum_ref, ra_ref, rb_ref, h_ref, w_ref, g_ref, *rest):
    outs, (att, hid, mix, sem) = rest[:n_groups], rest[n_groups:]
    copy = pltpu.make_async_copy(h_ref.at[pl.ds(0, hid.shape[0])], hid, sem)
    copy.start()
    remote_attend(0, place, counts, lists, qn_ref, sum_ref, ra_ref, rb_ref, att)
    copy.wait()
    n, tokens, _ = hid.shape

    def block(f):
        def finish(normed):
            mix[f] = (hid[f].astype(F32) + normed * g_ref[...]).astype(BF)

        return lambda: contract(att[f], w_ref[...], 0, 0), finish

    add_normed([block(f) for f in range(n)])
    share = tokens // n_groups
    for j, out in enumerate(outs):
        group = peer(place[0], j, n_groups)
        for f in range(n):
            out[f] = mix[f, pl.ds(pl.multiple_of(group * share, SUB), share), :]


def late_kernel(frame, n_groups, halves, place, counts, lists, qn_ref, sum_ref, ra_ref, rb_ref, *rest):
    outs, (att, rows) = rest[:n_groups * halves], rest[n_groups * halves:]
    n, width, tokens = qn_ref.shape
    remote_attend(frame, place, counts, lists, qn_ref, sum_ref, ra_ref, rb_ref, att)
    for f in range(n):
        rows[:, f * width:(f + 1) * width] = att[f].T.astype(BF)
    size = tokens // n_groups // halves
    for half in range(halves):
        for j in range(n_groups):
            start = (peer(place[0], j, n_groups) * halves + half) * size
            outs[half * n_groups + j][...] = rows[pl.ds(pl.multiple_of(start, SUB), size), :]


def mix_kernel(*refs):
    w_ref, g_ref, out = refs[-3:]
    n_groups, n, share, _ = out.shape
    atts, hids = refs[:-3 - n_groups], refs[-3 - n_groups:-3]
    width = w_ref.shape[0]
    rows = atts[0].shape[0]
    halves = share // rows

    def block(js):
        def start():
            x = [
                atts[half * n_groups + j][:, f * width:(f + 1) * width]
                for j in js
                for f in range(n)
                for half in range(halves)
            ]
            return contract(jnp.concatenate(x, axis=0), w_ref[...], 1, 0)

        def finish(normed):
            for i, j in enumerate(js):
                for f in range(n):
                    at = (i * n + f) * share
                    part = normed[at:at + share, :] * g_ref[...]
                    out[j, f] = (hids[j][f].astype(F32) + part).astype(BF)

        return start, finish

    add_normed([block(js) for js in blocks_of(n_groups, n * share)])


def blocks_of(n_groups, rows):
    size = max(1, min(n_groups, 2 * TILE // rows))
    return [range(at, min(at + size, n_groups)) for at in range(0, n_groups, size)]


def paired(chunks, lanes, frames):
    return chunks % 2 == 0 and frames % 2 == 0 and 2 * lanes == TILE


def slot(c, frame, chunks, n_groups, frames):
    return c ^ (frame & 1) if paired(chunks, n_groups * SUB, frames) else c


def project(w_ref, x, out, base=0):
    width = w_ref.shape[0] // 3
    cut = w_ref.shape[0] // 2
    heads = width // HEAD_DIM
    parts = [contract(w_ref[i * cut:(i + 1) * cut, :], x, 1, 1) for i in range(2)]
    for h in range(3 * heads):
        i, at = divmod(h * HEAD_DIM, cut)
        y = parts[i][at:at + HEAD_DIM, :]
        if h < 2 * heads:
            y = y * head_scale(y)
        out[head(h), base:base + x.shape[0]] = y.astype(BF)


def project_kernel(frames, *refs):
    pieces, w_ref, out, x = refs[:-3], refs[-3], refs[-2], refs[-1]
    n_groups = len(pieces)
    n, share, _ = pieces[0].shape
    chunks = share // SUB
    for f in range(n):
        for c in range(chunks):
            for j, piece in enumerate(pieces):
                at = (slot(c, f, chunks, n_groups, frames) * n_groups + j) * SUB
                x[f, at:at + SUB, :] = piece[f, c * SUB:(c + 1) * SUB, :]
        project(w_ref, x[f], out, f * x.shape[1])


def late_project_kernel(frame, frames, *refs):
    n_groups = (len(refs) - 7) // 2
    atts, hids = refs[:n_groups], refs[n_groups:2 * n_groups]
    w_ref, g_ref, qkv_ref, out, a, b, x = refs[2 * n_groups:]
    width = w_ref.shape[0]
    n, rows, _ = hids[0].shape
    chunks = rows // SUB
    for f in range(n):
        for c in range(chunks):
            for j in range(n_groups):
                at = ((f * chunks + slot(c, frame + f, chunks, n_groups, frames)) * n_groups + j) * SUB
                piece = slice(c * SUB, (c + 1) * SUB)
                a[at:at + SUB, :] = atts[j][piece, f * width:(f + 1) * width]
                b[at:at + SUB, :] = hids[j][f, piece, :]

    def finish(normed):
        x[...] = (b[...].astype(F32) + normed * g_ref[...]).astype(BF)

    add_normed([(lambda: contract(a[...], w_ref[...], 1, 0), finish)])
    project(qkv_ref, x[...], out)


def temporal_kernel(n_groups, *refs):
    frames = len(refs) - n_groups - 1
    ins, outs, att = refs[:frames], refs[frames:frames + n_groups], refs[-1]
    lanes = n_groups * SUB
    chunks = ins[0].shape[1] // lanes
    width = ins[0].shape[0] // 3
    rows = frames * lanes
    pair = paired(chunks, lanes, frames)
    row_pos = lax.broadcasted_iota(jnp.int32, (rows, rows), 0) % SUB
    col_pos = lax.broadcasted_iota(jnp.int32, (rows, rows), 1) % SUB
    same = jnp.where(row_pos == col_pos, 1.0, 0.0).astype(BF)
    low = lax.broadcasted_iota(jnp.int32, (HEAD_DIM, TILE), 1) < lanes

    def take(c, where):
        if not pair:
            return jnp.concatenate([r[where, c * lanes:(c + 1) * lanes] for r in ins], axis=1)
        tile = slice(c // 2 * TILE, (c // 2 + 1) * TILE)
        got = [r[where, tile] for r in ins]
        return jnp.concatenate(
            [
                jnp.where(low, got[m + (c & 1)], got[m + 1 - (c & 1)])
                for m in range(0, frames, 2)
            ],
            axis=1,
        )

    def scores(c, h):
        return contract(take(c, head(h, width)), take(c, head(h)), 0, 0)

    def weigh(s):
        return jnp.exp2(s * EXP2_SCALE).astype(BF) * same

    def gather(c, h, p):
        att[c, head(h), :] = averaged(contract(with_ones(take(c, head(h, 2 * width))), p, 1, 0))

    steps = [(c, h) for c in range(chunks) for h in range(width // HEAD_DIM)]
    pipeline(steps, scores, weigh, gather)
    turned = [att[c].T.astype(BF) for c in range(chunks)]
    for j, out in enumerate(outs):
        for c in range(chunks):
            for f in range(frames):
                at = (f ^ (c & 1) if pair else f) * lanes + j * SUB
                out[c * SUB:(c + 1) * SUB, f * width:(f + 1) * width] = turned[c][at:at + SUB, :]


def output_kernel(n_groups, js, early, half, halves, aliased, place, *refs):
    n = len(js)
    atts, pieces = refs[:n], refs[n:2 * n]
    late_ref, w_ref, g_ref = refs[2 * n:2 * n + 3]
    out, buf, sems = refs[2 * n + 3 + aliased:]
    _, late, rows, _ = late_ref.shape
    width = w_ref.shape[0]
    frames = early + late
    copies = []

    def block(some):
        def start():
            x = [atts[i][:, f * width:(f + 1) * width] for i in some for f in range(frames)]
            return contract(jnp.concatenate(x, axis=0), w_ref[...], 1, 0)

        def finish(normed):
            for k, i in enumerate(some):
                j = js[i]
                for f in range(frames):
                    mine = pieces[i][f] if f < early else late_ref[j, f - early]
                    at = (k * frames + f) * rows
                    part = normed[at:at + rows, :] * g_ref[...]
                    buf[i, f] = (mine.astype(F32) + part).astype(BF)
                group = peer(place[0], j, n_groups)
                at = pl.multiple_of((group * halves + half) * rows, SUB)
                copy = pltpu.make_async_copy(buf.at[i], out.at[:, pl.ds(at, rows), :], sems.at[i])
                copy.start()
                copies.append(copy)

        return start, finish

    add_normed([block(some) for some in blocks_of(len(js), frames * rows)])
    for copy in copies:
        copy.wait()


def shards(
    spatial_queries,
    spatial_keys,
    spatial_values,
    hidden,
    spatial_out_weight,
    spatial_gain,
    temporal_qkv_weight,
    temporal_out_weight,
    temporal_gain,
    tile_list,
    tile_count,
):
    frames, tokens, width = spatial_queries.shape
    model = hidden.shape[2]
    groups = lax.axis_size("frame")
    strips = lax.axis_size("strip")
    share = tokens // groups
    halves = 2 if share % (4 * SUB) == 0 else 1
    rows = share // halves
    queries = pltpu.with_memory_space_constraint(jnp.transpose(spatial_queries, (0, 2, 1)), pltpu.HBM)
    keys = pltpu.with_memory_space_constraint(jnp.transpose(spatial_keys, (0, 2, 1)), pltpu.HBM)
    values = pltpu.with_memory_space_constraint(jnp.transpose(spatial_values, (0, 2, 1)), pltpu.HBM)
    hidden_far = pltpu.with_memory_space_constraint(hidden, pltpu.HBM)
    lists = jnp.transpose(tile_list, (2, 1, 0))
    counts = tile_count.T
    qkv_weight = temporal_qkv_weight.T
    gain_one = spatial_gain.reshape(1, model)
    gain_two = temporal_gain.reshape(1, model)
    place = jnp.stack([lax.axis_index("frame"), lax.axis_index("strip")]).astype(jnp.int32)
    near = [(i, i ^ 1) for i in range(strips) if i ^ 1 < strips]
    far = [e for i in range(1, strips - 1, 2) for e in ((i, i + 1), (i + 1, i))]
    edge = jax.ShapeDtypeStruct((2 * width, TILE), BF)
    smem = pl.BlockSpec(memory_space=pltpu.SMEM)
    any_spec = pl.BlockSpec(memory_space=pl.ANY)

    def call(kernel, in_specs, out_specs, out_shape, scratch=(), limit=32, prefetch=0, alias=None):
        return pl.pallas_call(
            kernel,
            grid_spec=pltpu.PrefetchScalarGridSpec(
                num_scalar_prefetch=prefetch,
                grid=(1,),
                in_specs=in_specs,
                out_specs=out_specs,
                scratch_shapes=list(scratch),
            ),
            out_shape=out_shape,
            input_output_aliases=alias or {},
            compiler_params=vmem(limit),
        )

    late = frames // 2
    early = frames - late

    def out_pairs(j):
        return [(i, peer(i, j, groups)) for i in range(groups)]

    def send(parts):
        sent = {j: lax.ppermute(parts[j], "frame", out_pairs(j)) for j in reversed(range(1, groups))}
        return [parts[0]] + [sent[j] for j in range(1, groups)]

    halos = []
    for some in range(2):
        block = pl.BlockSpec((late, width, tokens), lambda *_, some=some: (some, 0, 0))
        split = groups if some == 0 else 0
        a, b, *pieces = call(
            prep_kernel,
            [smem, block, block] + [any_spec] * bool(split),
            [whole((late,) + edge.shape)] * 2 + [any_spec] * split,
            [jax.ShapeDtypeStruct((late,) + edge.shape, BF)] * 2
            + [jax.ShapeDtypeStruct((late, share, model), BF)] * split,
            [pltpu.SemaphoreType.DMA((groups,))] * bool(split),
            limit=16,
        )(place, keys, values, *[hidden_far] * bool(split))
        if split:
            own_hidden = pieces
        halos.append((a, b, lax.ppermute(a, "strip", near), lax.ppermute(b, "strip", far)))
    far_hidden = send(own_hidden)

    sum_shape = (late, width // HEAD_DIM * (HEAD_DIM + 8), tokens)
    own_sums = []
    for some in range(2):
        block = pl.BlockSpec((late, width, tokens), lambda *_, some=some: (some, 0, 0))
        own_sums.append(
            call(
                functools.partial(local_kernel, some * late),
                [smem, smem, smem, block] + [whole((late,) + edge.shape)] * 2,
                [whole((late, width, tokens)), whole(sum_shape)],
                [
                    jax.ShapeDtypeStruct((late, width, tokens), BF),
                    jax.ShapeDtypeStruct(sum_shape, F32),
                ],
            )(place, counts, lists, queries, *halos[some][:2])
        )
    sum_specs = [whole((late, width, tokens)), whole(sum_shape)]

    mixed = call(
        functools.partial(spatial_kernel, groups),
        [smem, smem, smem]
        + sum_specs
        + [whole((late,) + edge.shape)] * 2
        + [any_spec, whole((width, model)), whole((1, model))],
        [whole((early, share, model))] * groups,
        [jax.ShapeDtypeStruct((early, share, model), BF)] * groups,
        [
            pltpu.VMEM((early, width, tokens), BF),
            pltpu.VMEM((early, tokens, model), BF),
            pltpu.VMEM((early, tokens, model), BF),
            pltpu.SemaphoreType.DMA,
        ],
    )(place, counts, lists, *own_sums[0], *halos[0][2:], hidden_far, spatial_out_weight, gain_one)
    arrived = send(mixed)
    projected = call(
        functools.partial(project_kernel, frames),
        [whole((early, share, model))] * groups + [whole((3 * width, model))],
        whole((3 * width, early * tokens)),
        jax.ShapeDtypeStruct((3 * width, early * tokens), BF),
        [pltpu.VMEM((early, tokens, model), BF)],
    )(*arrived, qkv_weight)

    late_shape = (rows, late * width)
    own_late = call(
        functools.partial(late_kernel, early, groups, halves),
        [smem, smem, smem] + sum_specs + [whole((late,) + edge.shape)] * 2,
        [whole(late_shape)] * (groups * halves),
        [jax.ShapeDtypeStruct(late_shape, BF)] * (groups * halves),
        [pltpu.VMEM((late, width, tokens), F32), pltpu.VMEM((tokens, late * width), BF)],
    )(place, counts, lists, *own_sums[1], *halos[1][2:])
    own_late = [own_late[half * groups:(half + 1) * groups] for half in range(halves)]
    far_late = []
    for half in range(halves):
        far_late.append(send(own_late[half]))

    returned = []
    back_shape = (rows, frames * width)
    lanes = tokens // halves
    for half in range(halves):
        hid_block = pl.BlockSpec((late, rows, model), lambda *_, half=half: (0, half, 0))
        late_specs = [whole(late_shape)] * groups + [hid_block] * groups
        late_specs += [whole((width, model)), whole((1, model))]
        late_projected = call(
            functools.partial(late_project_kernel, early, frames),
            late_specs + [whole((3 * width, model))],
            whole((3 * width, late * lanes)),
            jax.ShapeDtypeStruct((3 * width, late * lanes), BF),
            [
                pltpu.VMEM((late * lanes, width), BF),
                pltpu.VMEM((late * lanes, model), BF),
                pltpu.VMEM((late * lanes, model), BF),
            ],
        )(*far_late[half], *far_hidden, spatial_out_weight, gain_one, qkv_weight)
        back = call(
            functools.partial(temporal_kernel, groups),
            [
                pl.BlockSpec((3 * width, lanes), lambda *_, at=f * halves + half: (0, at))
                for f in range(early)
            ]
            + [pl.BlockSpec((3 * width, lanes), lambda *_, f=f: (0, f)) for f in range(late)],
            [whole(back_shape)] * groups,
            [jax.ShapeDtypeStruct(back_shape, BF)] * groups,
            [pltpu.VMEM((rows // SUB, width, groups * frames * SUB), F32)],
        )(*[projected] * early, *[late_projected] * late)
        home = {
            j: lax.ppermute(back[j], "frame", [(b, a) for a, b in out_pairs(j)])
            for j in reversed(range(1, groups))
        }
        returned.append([back[0]] + [home[j] for j in range(1, groups)])

    late_mixed = call(
        mix_kernel,
        [whole(late_shape)] * (groups * halves)
        + [whole((late, share, model))] * groups
        + [whole((width, model)), whole((1, model))],
        whole((groups, late, share, model)),
        jax.ShapeDtypeStruct((groups, late, share, model), BF),
    )(*[x for some in own_late for x in some], *own_hidden, spatial_out_weight, gain_one)

    out = None
    for half in range(halves):
        piece = pl.BlockSpec((early, rows, model), lambda *_, half=half: (0, half, 0))
        cuts = [groups]
        for lo, hi in zip([0] + cuts, cuts):
            js = range(lo, hi)
            if not js:
                continue
            extra = [] if out is None else [out]
            out = call(
                functools.partial(output_kernel, groups, tuple(js), early, half, halves, len(extra)),
                [smem]
                + [whole(back_shape)] * len(js)
                + [piece] * len(js)
                + [pl.BlockSpec((groups, late, rows, model), lambda *_, half=half: (0, 0, half, 0))]
                + [whole((width, model)), whole((1, model))]
                + [any_spec] * len(extra),
                any_spec,
                jax.ShapeDtypeStruct((frames, tokens, model), BF),
                [
                    pltpu.VMEM((len(js), frames, rows, model), BF),
                    pltpu.SemaphoreType.DMA((len(js),)),
                ],
                alias={4 + 2 * len(js): 0} if extra else None,
            )(
                place,
                *[returned[half][j] for j in js],
                *[mixed[j] for j in js],
                late_mixed,
                temporal_out_weight,
                gain_two,
                *extra,
            )
    return out


def solution(mesh):
    rows = P(("group", "frame"), "strip", None)
    placed = (rows, rows, rows, rows, P(), P(), P(), P(), P(), rows, P(("group", "frame"), "strip"))

    return jax.shard_map(shards, mesh=mesh, in_specs=placed, out_specs=rows, check_vma=False)
```

```python
import functools
import math

import jax
import jax.numpy as jnp
from jax import lax
from jax.experimental import pallas as pl
from jax.experimental.pallas import tpu as pltpu
from jax.sharding import PartitionSpec as P


HEAD_DIM = 72
TILE = 128
MAXT = 3
SUB = 16
EPS = 1e-06
EXP2_SCALE = HEAD_DIM ** -0.5 * math.log2(math.e)

BF = jnp.bfloat16
F32 = jnp.float32


def peer(i, j, n):
    return i ^ j if n & (n - 1) == 0 else (i + j) % n


def vmem(limit):
    return pltpu.CompilerParams(vmem_limit_bytes=limit << 20)


def whole(shape):
    return pl.BlockSpec(shape, lambda *_: (0,) * len(shape))


def contract(a, b, da, db):
    return lax.dot_general(a, b, (((da,), (db,)), ((), ())), preferred_element_type=F32)


def head_scale(x):
    return lax.rsqrt(jnp.mean(x * x, axis=0, keepdims=True) + EPS)


def head(h, base=0):
    return slice(base + h * HEAD_DIM, base + (h + 1) * HEAD_DIM)


def with_ones(v):
    return jnp.concatenate([v, jnp.ones((8, v.shape[1]), v.dtype)], axis=0)


def averaged(o):
    return o[:HEAD_DIM, :] / o[HEAD_DIM:HEAD_DIM + 1, :]


def pipeline(steps, scores, weigh, gather):
    ahead, behind = scores(*steps[0]), None
    for n, step in enumerate(steps):
        now = ahead
        if n + 1 < len(steps):
            ahead = scores(*steps[n + 1])
        weighed = weigh(now)
        if behind is not None:
            gather(*steps[n - 1], behind)
        behind = weighed
    gather(*steps[-1], behind)


def prep_kernel(place, k_ref, v_ref, *refs):
    n, width, _ = k_ref.shape
    even = place[1] % 2 == 0
    copies = []
    if len(refs) > 2:
        src, (a_ref, b_ref), pieces, sems = refs[0], refs[1:3], refs[3:-1], refs[-1]
        late, share, _ = pieces[0].shape
        for j in reversed(range(len(pieces))):
            start = pl.multiple_of(peer(place[0], j, len(pieces)) * share, SUB)
            part = src.at[pl.ds(src.shape[0] - late, late), pl.ds(start, share), :]
            copies.append(pltpu.make_async_copy(part, pieces[j], sems.at[j]))
            copies[-1].start()
    else:
        a_ref, b_ref = refs

    def fill(first, second):
        for f in range(n):
            for h in range(width // HEAD_DIM):
                x = k_ref[f, head(h), :].astype(F32)
                y = (x * head_scale(x)).astype(BF)
                first[f, head(h), :] = y[:, :TILE]
                second[f, head(h), :] = y[:, TILE:]
            first[f, width:, :] = v_ref[f, :, :TILE]
            second[f, width:, :] = v_ref[f, :, TILE:]

    pl.when(even)(functools.partial(fill, b_ref, a_ref))
    pl.when(jnp.logical_not(even))(functools.partial(fill, a_ref, b_ref))
    for copy in copies:
        copy.wait()


def tile_masks(frame, n, tiles, local, place, counts, lists):
    strip = place[1]
    odd = strip % 2
    first = strip * tiles
    if local:
        spots = (first + 1 - odd, first + odd)
    else:
        spots = (first + 2 - 3 * odd, first - 1 + 3 * odd)
    masks = []
    for f in range(n):
        rows = []
        for spot in spots:
            cells = []
            for t in range(tiles):
                hit = jnp.bool_(False)
                for j in range(MAXT):
                    hit = hit | ((lists[j, t, frame + f] == spot) & (j < counts[t, frame + f]))
                cells.append(jnp.full((SUB, TILE), jnp.where(hit, 1.0, 0.0), F32))
            rows.append(jnp.concatenate(cells, axis=1).astype(BF))
        masks.append(rows)
    return masks


def attend(masks, keys, query, finish):
    n = keys[0].shape[0]
    width = keys[0].shape[1] // 2

    def scores(f, h):
        qn = query(f, h)
        return f, [contract(ref[f, head(h), :], qn, 0, 0) for ref in keys]

    def weigh(scored):
        f, s = scored
        packed = []
        for mask, x in zip(masks[f], s):
            p = jnp.exp2(x * EXP2_SCALE).astype(BF).reshape(TILE // SUB, SUB, x.shape[1])
            packed.append((p * mask).reshape(x.shape))
        return jnp.concatenate(packed, axis=0)

    def gather(f, h, weights):
        v = jnp.concatenate([ref[f, head(h, width), :] for ref in keys], axis=1)
        finish(f, h, contract(with_ones(v), weights, 1, 0))

    pipeline([(f, h) for f in range(n) for h in range(width // HEAD_DIM)], scores, weigh, gather)


def sums(h):
    return slice(h * (HEAD_DIM + 8), (h + 1) * (HEAD_DIM + 8))


def local_kernel(frame, place, counts, lists, q_ref, a_ref, b_ref, qn_ref, sum_ref):
    n, _, tokens = q_ref.shape

    def query(f, h):
        q = q_ref[f, head(h), :].astype(F32)
        qn = (q * head_scale(q)).astype(BF)
        qn_ref[f, head(h), :] = qn
        return qn

    def finish(f, h, o):
        sum_ref[f, sums(h), :] = o

    masks = tile_masks(frame, n, tokens // TILE, True, place, counts, lists)
    attend(masks, (a_ref, b_ref), query, finish)


def remote_attend(frame, place, counts, lists, qn_ref, sum_ref, ra_ref, rb_ref, att):
    n, _, tokens = qn_ref.shape

    def query(f, h):
        return qn_ref[f, head(h), :]

    def finish(f, h, o):
        att[f, head(h), :] = averaged(o + sum_ref[f, sums(h), :]).astype(att.dtype)

    masks = tile_masks(frame, n, tokens // TILE, False, place, counts, lists)
    attend(masks, (ra_ref, rb_ref), query, finish)


def add_normed(blocks):
    ahead = blocks[0][0]()
    for n, (_, finish) in enumerate(blocks):
        proj = ahead
        if n + 1 < len(blocks):
            ahead = blocks[n + 1][0]()
        scale = lax.rsqrt(jnp.mean(proj * proj, axis=-1, keepdims=True) + EPS)
        finish(proj * scale)


def spatial_kernel(frame, n_groups, place, counts, lists, qn_ref, sum_ref, ra_ref, rb_ref, h_ref, w_ref, g_ref, *rest):
    outs, (att, hid, mix, sem) = rest[:n_groups], rest[n_groups:]
    copy = pltpu.make_async_copy(h_ref.at[pl.ds(frame, hid.shape[0])], hid, sem)
    copy.start()
    remote_attend(frame, place, counts, lists, qn_ref, sum_ref, ra_ref, rb_ref, att)
    copy.wait()
    n, tokens, _ = hid.shape

    def block(f):
        def finish(normed):
            mix[f] = (hid[f].astype(F32) + normed * g_ref[...]).astype(BF)

        return lambda: contract(att[f], w_ref[...], 0, 0), finish

    add_normed([block(f) for f in range(n)])
    share = tokens // n_groups
    for j, out in enumerate(outs):
        group = peer(place[0], j, n_groups)
        for f in range(n):
            out[f] = mix[f, pl.ds(pl.multiple_of(group * share, SUB), share), :]


def late_kernel(frame, n_groups, halves, place, counts, lists, qn_ref, sum_ref, ra_ref, rb_ref, *rest):
    outs, (att, rows) = rest[:n_groups * halves], rest[n_groups * halves:]
    n, width, tokens = qn_ref.shape
    remote_attend(frame, place, counts, lists, qn_ref, sum_ref, ra_ref, rb_ref, att)
    for f in range(n):
        rows[:, f * width:(f + 1) * width] = att[f].T.astype(BF)
    size = tokens // n_groups // halves
    for half in range(halves):
        for j in range(n_groups):
            start = (peer(place[0], j, n_groups) * halves + half) * size
            outs[half * n_groups + j][...] = rows[pl.ds(pl.multiple_of(start, SUB), size), :]


def mix_kernel(*refs):
    w_ref, g_ref, out = refs[-3:]
    n_groups, n, share, _ = out.shape
    atts, hids = refs[:-3 - n_groups], refs[-3 - n_groups:-3]
    width = w_ref.shape[0]
    rows = atts[0].shape[0]
    halves = share // rows

    def block(js):
        def start():
            x = [
                atts[half * n_groups + j][:, f * width:(f + 1) * width]
                for j in js
                for f in range(n)
                for half in range(halves)
            ]
            return contract(jnp.concatenate(x, axis=0), w_ref[...], 1, 0)

        def finish(normed):
            for i, j in enumerate(js):
                for f in range(n):
                    at = (i * n + f) * share
                    part = normed[at:at + share, :] * g_ref[...]
                    out[j, f] = (hids[j][f].astype(F32) + part).astype(BF)

        return start, finish

    add_normed([block(js) for js in blocks_of(n_groups, n * share)])


def blocks_of(n_groups, rows):
    size = max(1, min(n_groups, 2 * TILE // rows))
    return [range(at, min(at + size, n_groups)) for at in range(0, n_groups, size)]


def paired(chunks, lanes, frames):
    return chunks % 2 == 0 and frames % 2 == 0 and 2 * lanes == TILE


def slot(c, frame, chunks, n_groups, frames):
    return c ^ (frame & 1) if paired(chunks, n_groups * SUB, frames) else c


def project(w_ref, x, out):
    width = w_ref.shape[0] // 3
    cut = w_ref.shape[0] // 2
    heads = width // HEAD_DIM
    parts = [contract(w_ref[i * cut:(i + 1) * cut, :], x, 1, 1) for i in range(2)]
    for h in range(3 * heads):
        i, at = divmod(h * HEAD_DIM, cut)
        y = parts[i][at:at + HEAD_DIM, :]
        if h < 2 * heads:
            y = y * head_scale(y)
        out[head(h), :] = y.astype(BF)


def project_kernel(frame, frames, *refs):
    pieces, w_ref, out, x = refs[:-3], refs[-3], refs[-2], refs[-1]
    n_groups = len(pieces)
    chunks = pieces[0].shape[1] // SUB
    for c in range(chunks):
        for j, piece in enumerate(pieces):
            at = (slot(c, frame, chunks, n_groups, frames) * n_groups + j) * SUB
            x[at:at + SUB, :] = piece[0, c * SUB:(c + 1) * SUB, :]
    project(w_ref, x[...], out)


def late_project_kernel(frame, frames, *refs):
    n_groups = (len(refs) - 7) // 2
    atts, hids = refs[:n_groups], refs[n_groups:2 * n_groups]
    w_ref, g_ref, qkv_ref, out, a, b, x = refs[2 * n_groups:]
    width = w_ref.shape[0]
    n, rows, _ = hids[0].shape
    chunks = rows // SUB
    for f in range(n):
        for c in range(chunks):
            for j in range(n_groups):
                at = ((f * chunks + slot(c, frame + f, chunks, n_groups, frames)) * n_groups + j) * SUB
                piece = slice(c * SUB, (c + 1) * SUB)
                a[at:at + SUB, :] = atts[j][piece, f * width:(f + 1) * width]
                b[at:at + SUB, :] = hids[j][f, piece, :]

    def finish(normed):
        x[...] = (b[...].astype(F32) + normed * g_ref[...]).astype(BF)

    add_normed([(lambda: contract(a[...], w_ref[...], 1, 0), finish)])
    project(qkv_ref, x[...], out)


def temporal_kernel(n_groups, *refs):
    frames = len(refs) - n_groups - 1
    ins, outs, att = refs[:frames], refs[frames:frames + n_groups], refs[-1]
    lanes = n_groups * SUB
    chunks = ins[0].shape[1] // lanes
    width = ins[0].shape[0] // 3
    rows = frames * lanes
    pair = paired(chunks, lanes, frames)
    row_pos = lax.broadcasted_iota(jnp.int32, (rows, rows), 0) % SUB
    col_pos = lax.broadcasted_iota(jnp.int32, (rows, rows), 1) % SUB
    same = jnp.where(row_pos == col_pos, 1.0, 0.0).astype(BF)
    low = lax.broadcasted_iota(jnp.int32, (HEAD_DIM, TILE), 1) < lanes

    def take(c, where):
        if not pair:
            return jnp.concatenate([r[where, c * lanes:(c + 1) * lanes] for r in ins], axis=1)
        tile = slice(c // 2 * TILE, (c // 2 + 1) * TILE)
        got = [r[where, tile] for r in ins]
        return jnp.concatenate(
            [
                jnp.where(low, got[m + (c & 1)], got[m + 1 - (c & 1)])
                for m in range(0, frames, 2)
            ],
            axis=1,
        )

    def scores(c, h):
        return contract(take(c, head(h, width)), take(c, head(h)), 0, 0)

    def weigh(s):
        return jnp.exp2(s * EXP2_SCALE).astype(BF) * same

    def gather(c, h, p):
        att[c, head(h), :] = averaged(contract(with_ones(take(c, head(h, 2 * width))), p, 1, 0))

    steps = [(c, h) for c in range(chunks) for h in range(width // HEAD_DIM)]
    pipeline(steps, scores, weigh, gather)
    turned = [att[c].T.astype(BF) for c in range(chunks)]
    for j, out in enumerate(outs):
        for c in range(chunks):
            for f in range(frames):
                at = (f ^ (c & 1) if pair else f) * lanes + j * SUB
                out[c * SUB:(c + 1) * SUB, f * width:(f + 1) * width] = turned[c][at:at + SUB, :]


def output_kernel(n_groups, js, early, half, halves, aliased, place, *refs):
    n = len(js)
    atts, pieces = refs[:n], refs[n:n * (1 + early)]
    late_ref, w_ref, g_ref = refs[n * (1 + early):n * (1 + early) + 3]
    out, buf, sems = refs[n * (1 + early) + 3 + aliased:]
    _, late, rows, _ = late_ref.shape
    width = w_ref.shape[0]
    frames = early + late
    copies = []

    def block(some):
        def start():
            x = [atts[i][:, f * width:(f + 1) * width] for i in some for f in range(frames)]
            return contract(jnp.concatenate(x, axis=0), w_ref[...], 1, 0)

        def finish(normed):
            for k, i in enumerate(some):
                j = js[i]
                for f in range(frames):
                    mine = pieces[i * early + f][0] if f < early else late_ref[j, f - early]
                    at = (k * frames + f) * rows
                    part = normed[at:at + rows, :] * g_ref[...]
                    buf[i, f] = (mine.astype(F32) + part).astype(BF)
                group = peer(place[0], j, n_groups)
                at = pl.multiple_of((group * halves + half) * rows, SUB)
                copy = pltpu.make_async_copy(buf.at[i], out.at[:, pl.ds(at, rows), :], sems.at[i])
                copy.start()
                copies.append(copy)

        return start, finish

    add_normed([block(some) for some in blocks_of(len(js), frames * rows)])
    for copy in copies:
        copy.wait()


def shards(
    spatial_queries,
    spatial_keys,
    spatial_values,
    hidden,
    spatial_out_weight,
    spatial_gain,
    temporal_qkv_weight,
    temporal_out_weight,
    temporal_gain,
    tile_list,
    tile_count,
):
    frames, tokens, width = spatial_queries.shape
    model = hidden.shape[2]
    groups = lax.axis_size("frame")
    strips = lax.axis_size("strip")
    share = tokens // groups
    halves = 2 if share % (4 * SUB) == 0 else 1
    rows = share // halves
    queries = pltpu.with_memory_space_constraint(jnp.transpose(spatial_queries, (0, 2, 1)), pltpu.HBM)
    keys = pltpu.with_memory_space_constraint(jnp.transpose(spatial_keys, (0, 2, 1)), pltpu.HBM)
    values = pltpu.with_memory_space_constraint(jnp.transpose(spatial_values, (0, 2, 1)), pltpu.HBM)
    hidden_far = pltpu.with_memory_space_constraint(hidden, pltpu.HBM)
    lists = jnp.transpose(tile_list, (2, 1, 0))
    counts = tile_count.T
    qkv_weight = temporal_qkv_weight.T
    gain_one = spatial_gain.reshape(1, model)
    gain_two = temporal_gain.reshape(1, model)
    place = jnp.stack([lax.axis_index("frame"), lax.axis_index("strip")]).astype(jnp.int32)
    near = [(i, i ^ 1) for i in range(strips) if i ^ 1 < strips]
    far = [e for i in range(1, strips - 1, 2) for e in ((i, i + 1), (i + 1, i))]
    edge = jax.ShapeDtypeStruct((2 * width, TILE), BF)
    smem = pl.BlockSpec(memory_space=pltpu.SMEM)
    any_spec = pl.BlockSpec(memory_space=pl.ANY)

    def call(kernel, in_specs, out_specs, out_shape, scratch=(), limit=32, prefetch=0, alias=None):
        return pl.pallas_call(
            kernel,
            grid_spec=pltpu.PrefetchScalarGridSpec(
                num_scalar_prefetch=prefetch,
                grid=(1,),
                in_specs=in_specs,
                out_specs=out_specs,
                scratch_shapes=list(scratch),
            ),
            out_shape=out_shape,
            input_output_aliases=alias or {},
            compiler_params=vmem(limit),
        )

    late = frames // 2
    early = frames - late

    def out_pairs(j):
        return [(i, peer(i, j, groups)) for i in range(groups)]

    def send(parts):
        sent = {j: lax.ppermute(parts[j], "frame", out_pairs(j)) for j in reversed(range(1, groups))}
        return [parts[0]] + [sent[j] for j in range(1, groups)]

    halos = []
    for some in range(2):
        block = pl.BlockSpec((late, width, tokens), lambda *_, some=some: (some, 0, 0))
        split = groups if some == 1 else 0
        a, b, *pieces = call(
            prep_kernel,
            [smem, block, block] + [any_spec] * bool(split),
            [whole((late,) + edge.shape)] * 2 + [any_spec] * split,
            [jax.ShapeDtypeStruct((late,) + edge.shape, BF)] * 2
            + [jax.ShapeDtypeStruct((late, share, model), BF)] * split,
            [pltpu.SemaphoreType.DMA((groups,))] * bool(split),
            limit=16,
        )(place, keys, values, *[hidden_far] * bool(split))
        if split:
            own_hidden = pieces
        halos.append((a, b, lax.ppermute(a, "strip", near), lax.ppermute(b, "strip", far)))
    far_hidden = send(own_hidden)

    sum_shape = (late, width // HEAD_DIM * (HEAD_DIM + 8), tokens)
    own_sums = []
    for some in range(2):
        block = pl.BlockSpec((late, width, tokens), lambda *_, some=some: (some, 0, 0))
        own_sums.append(
            call(
                functools.partial(local_kernel, some * late),
                [smem, smem, smem, block] + [whole((late,) + edge.shape)] * 2,
                [whole((late, width, tokens)), whole(sum_shape)],
                [
                    jax.ShapeDtypeStruct((late, width, tokens), BF),
                    jax.ShapeDtypeStruct(sum_shape, F32),
                ],
            )(place, counts, lists, queries, *halos[some][:2])
        )
    sum_specs = [whole((late, width, tokens)), whole(sum_shape)]

    def one(shape, f):
        return pl.BlockSpec((1,) + shape[1:], lambda *_: (f, 0, 0))

    mixed, projected = [], []
    for f in range(early):
        mixed.append(
            call(
                functools.partial(spatial_kernel, f, groups),
                [smem, smem, smem, one((late, width, tokens), f), one(sum_shape, f)]
                + [one((late,) + edge.shape, f)] * 2
                + [any_spec, whole((width, model)), whole((1, model))],
                [whole((1, share, model))] * groups,
                [jax.ShapeDtypeStruct((1, share, model), BF)] * groups,
                [
                    pltpu.VMEM((1, width, tokens), BF),
                    pltpu.VMEM((1, tokens, model), BF),
                    pltpu.VMEM((1, tokens, model), BF),
                    pltpu.SemaphoreType.DMA,
                ],
            )(place, counts, lists, *own_sums[0], *halos[0][2:], hidden_far, spatial_out_weight, gain_one)
        )
        arrived = send(mixed[f])
        projected.append(
            call(
                functools.partial(project_kernel, f, frames),
                [whole((1, share, model))] * groups + [whole((3 * width, model))],
                whole((3 * width, tokens)),
                jax.ShapeDtypeStruct((3 * width, tokens), BF),
                [pltpu.VMEM((tokens, model), BF)],
            )(*arrived, qkv_weight)
        )

    late_shape = (rows, late * width)
    own_late = call(
        functools.partial(late_kernel, early, groups, halves),
        [smem, smem, smem] + sum_specs + [whole((late,) + edge.shape)] * 2,
        [whole(late_shape)] * (groups * halves),
        [jax.ShapeDtypeStruct(late_shape, BF)] * (groups * halves),
        [pltpu.VMEM((late, width, tokens), F32), pltpu.VMEM((tokens, late * width), BF)],
    )(place, counts, lists, *own_sums[1], *halos[1][2:])
    own_late = [own_late[half * groups:(half + 1) * groups] for half in range(halves)]
    far_late = []
    for half in range(halves):
        far_late.append(send(own_late[half]))

    returned = []
    back_shape = (rows, frames * width)
    lanes = tokens // halves
    for half in range(halves):
        hid_block = pl.BlockSpec((late, rows, model), lambda *_, half=half: (0, half, 0))
        late_specs = [whole(late_shape)] * groups + [hid_block] * groups
        late_specs += [whole((width, model)), whole((1, model))]
        late_projected = call(
            functools.partial(late_project_kernel, early, frames),
            late_specs + [whole((3 * width, model))],
            whole((3 * width, late * lanes)),
            jax.ShapeDtypeStruct((3 * width, late * lanes), BF),
            [
                pltpu.VMEM((late * lanes, width), BF),
                pltpu.VMEM((late * lanes, model), BF),
                pltpu.VMEM((late * lanes, model), BF),
            ],
        )(*far_late[half], *far_hidden, spatial_out_weight, gain_one, qkv_weight)
        back = call(
            functools.partial(temporal_kernel, groups),
            [pl.BlockSpec((3 * width, lanes), lambda *_, half=half: (0, half))] * early
            + [pl.BlockSpec((3 * width, lanes), lambda *_, f=f: (0, f)) for f in range(late)],
            [whole(back_shape)] * groups,
            [jax.ShapeDtypeStruct(back_shape, BF)] * groups,
            [pltpu.VMEM((rows // SUB, width, groups * frames * SUB), F32)],
        )(*projected, *[late_projected] * late)
        home = {
            j: lax.ppermute(back[j], "frame", [(b, a) for a, b in out_pairs(j)])
            for j in reversed(range(1, groups))
        }
        returned.append([back[0]] + [home[j] for j in range(1, groups)])

    late_mixed = call(
        mix_kernel,
        [whole(late_shape)] * (groups * halves)
        + [whole((late, share, model))] * groups
        + [whole((width, model)), whole((1, model))],
        whole((groups, late, share, model)),
        jax.ShapeDtypeStruct((groups, late, share, model), BF),
    )(*[x for some in own_late for x in some], *own_hidden, spatial_out_weight, gain_one)

    out = None
    for half in range(halves):
        piece = pl.BlockSpec((1, rows, model), lambda *_, half=half: (0, half, 0))
        cuts = [groups] if half + 1 < halves else [groups // 2, groups]
        for lo, hi in zip([0] + cuts, cuts):
            js = range(lo, hi)
            if not js:
                continue
            extra = [] if out is None else [out]
            out = call(
                functools.partial(output_kernel, groups, tuple(js), early, half, halves, len(extra)),
                [smem]
                + [whole(back_shape)] * len(js)
                + [piece] * (len(js) * early)
                + [pl.BlockSpec((groups, late, rows, model), lambda *_, half=half: (0, 0, half, 0))]
                + [whole((width, model)), whole((1, model))]
                + [any_spec] * len(extra),
                any_spec,
                jax.ShapeDtypeStruct((frames, tokens, model), BF),
                [
                    pltpu.VMEM((len(js), frames, rows, model), BF),
                    pltpu.SemaphoreType.DMA((len(js),)),
                ],
                alias={4 + len(js) * (1 + early): 0} if extra else None,
            )(
                place,
                *[returned[half][j] for j in js],
                *[mixed[f][j] for j in js for f in range(early)],
                late_mixed,
                temporal_out_weight,
                gain_two,
                *extra,
            )
    return out


def solution(mesh):
    rows = P(("group", "frame"), "strip", None)
    placed = (rows, rows, rows, rows, P(), P(), P(), P(), P(), rows, P(("group", "frame"), "strip"))

    return jax.shard_map(shards, mesh=mesh, in_specs=placed, out_specs=rows, check_vma=False)
```

```python
import functools
import math

import jax
import jax.numpy as jnp
from jax import lax
from jax.experimental import pallas as pl
from jax.experimental.pallas import tpu as pltpu
from jax.sharding import PartitionSpec as P


HEAD_DIM = 72
TILE = 128
MAXT = 3
SUB = 16
EPS = 1e-06
EXP2_SCALE = HEAD_DIM ** -0.5 * math.log2(math.e)

BF = jnp.bfloat16
F32 = jnp.float32


def peer(i, j, n):
    return i ^ j if n & (n - 1) == 0 else (i + j) % n


def vmem(limit):
    return pltpu.CompilerParams(vmem_limit_bytes=limit << 20)


def whole(shape):
    return pl.BlockSpec(shape, lambda *_: (0,) * len(shape))


def contract(a, b, da, db):
    return lax.dot_general(a, b, (((da,), (db,)), ((), ())), preferred_element_type=F32)


def head_scale(x):
    return lax.rsqrt(jnp.mean(x * x, axis=0, keepdims=True) + EPS)


def head(h, base=0):
    return slice(base + h * HEAD_DIM, base + (h + 1) * HEAD_DIM)


def with_ones(v):
    return jnp.concatenate([v, jnp.ones((8, v.shape[1]), v.dtype)], axis=0)


def averaged(o):
    return o[:HEAD_DIM, :] / o[HEAD_DIM:HEAD_DIM + 1, :]


def pipeline(steps, scores, weigh, gather):
    ahead, behind = scores(*steps[0]), None
    for n, step in enumerate(steps):
        now = ahead
        if n + 1 < len(steps):
            ahead = scores(*steps[n + 1])
        weighed = weigh(now)
        if behind is not None:
            gather(*steps[n - 1], behind)
        behind = weighed
    gather(*steps[-1], behind)


def prep_kernel(place, k_ref, v_ref, *refs):
    n, width, _ = k_ref.shape
    even = place[1] % 2 == 0
    copies = []
    if len(refs) > 2:
        src, (a_ref, b_ref), pieces, sems = refs[0], refs[1:3], refs[3:-1], refs[-1]
        late, share, _ = pieces[0].shape
        for j in reversed(range(len(pieces))):
            start = pl.multiple_of(peer(place[0], j, len(pieces)) * share, SUB)
            part = src.at[pl.ds(src.shape[0] - late, late), pl.ds(start, share), :]
            copies.append(pltpu.make_async_copy(part, pieces[j], sems.at[j]))
            copies[-1].start()
    else:
        a_ref, b_ref = refs

    def fill(first, second):
        for f in range(n):
            for h in range(width // HEAD_DIM):
                x = k_ref[f, head(h), :].astype(F32)
                y = (x * head_scale(x)).astype(BF)
                first[f, head(h), :] = y[:, :TILE]
                second[f, head(h), :] = y[:, TILE:]
            first[f, width:, :] = v_ref[f, :, :TILE]
            second[f, width:, :] = v_ref[f, :, TILE:]

    pl.when(even)(functools.partial(fill, b_ref, a_ref))
    pl.when(jnp.logical_not(even))(functools.partial(fill, a_ref, b_ref))
    for copy in copies:
        copy.wait()


def tile_masks(frame, n, tiles, local, place, counts, lists):
    strip = place[1]
    odd = strip % 2
    first = strip * tiles
    if local:
        spots = (first + 1 - odd, first + odd)
    else:
        spots = (first + 2 - 3 * odd, first - 1 + 3 * odd)
    masks = []
    for f in range(n):
        rows = []
        for spot in spots:
            cells = []
            for t in range(tiles):
                hit = jnp.bool_(False)
                for j in range(MAXT):
                    hit = hit | ((lists[j, t, frame + f] == spot) & (j < counts[t, frame + f]))
                cells.append(jnp.full((SUB, TILE), jnp.where(hit, 1.0, 0.0), F32))
            rows.append(jnp.concatenate(cells, axis=1).astype(BF))
        masks.append(rows)
    return masks


def attend(masks, keys, query, finish):
    n = keys[0].shape[0]
    width = keys[0].shape[1] // 2

    def scores(f, h):
        qn = query(f, h)
        return f, [contract(ref[f, head(h), :], qn, 0, 0) for ref in keys]

    def weigh(scored):
        f, s = scored
        packed = []
        for mask, x in zip(masks[f], s):
            p = jnp.exp2(x * EXP2_SCALE).astype(BF).reshape(TILE // SUB, SUB, x.shape[1])
            packed.append((p * mask).reshape(x.shape))
        return jnp.concatenate(packed, axis=0)

    def gather(f, h, weights):
        v = jnp.concatenate([ref[f, head(h, width), :] for ref in keys], axis=1)
        finish(f, h, contract(with_ones(v), weights, 1, 0))

    pipeline([(f, h) for f in range(n) for h in range(width // HEAD_DIM)], scores, weigh, gather)


def sums(h):
    return slice(h * (HEAD_DIM + 8), (h + 1) * (HEAD_DIM + 8))


def local_kernel(frame, place, counts, lists, q_ref, a_ref, b_ref, qn_ref, sum_ref):
    n, _, tokens = q_ref.shape

    def query(f, h):
        q = q_ref[f, head(h), :].astype(F32)
        qn = (q * head_scale(q)).astype(BF)
        qn_ref[f, head(h), :] = qn
        return qn

    def finish(f, h, o):
        sum_ref[f, sums(h), :] = o

    masks = tile_masks(frame, n, tokens // TILE, True, place, counts, lists)
    attend(masks, (a_ref, b_ref), query, finish)


def remote_attend(frame, place, counts, lists, qn_ref, sum_ref, ra_ref, rb_ref, att):
    n, _, tokens = qn_ref.shape

    def query(f, h):
        return qn_ref[f, head(h), :]

    def finish(f, h, o):
        att[f, head(h), :] = averaged(o + sum_ref[f, sums(h), :]).astype(att.dtype)

    masks = tile_masks(frame, n, tokens // TILE, False, place, counts, lists)
    attend(masks, (ra_ref, rb_ref), query, finish)


def add_normed(blocks):
    ahead = blocks[0][0]()
    for n, (_, finish) in enumerate(blocks):
        proj = ahead
        if n + 1 < len(blocks):
            ahead = blocks[n + 1][0]()
        scale = lax.rsqrt(jnp.mean(proj * proj, axis=-1, keepdims=True) + EPS)
        finish(proj * scale)


def spatial_kernel(frame, n_groups, place, counts, lists, qn_ref, sum_ref, ra_ref, rb_ref, h_ref, w_ref, g_ref, *rest):
    outs, (att, mix) = rest[:n_groups], rest[n_groups:]
    remote_attend(frame, place, counts, lists, qn_ref, sum_ref, ra_ref, rb_ref, att)
    n, tokens, _ = h_ref.shape

    def block(f):
        def finish(normed):
            mix[f] = (h_ref[f].astype(F32) + normed * g_ref[...]).astype(BF)

        return lambda: contract(att[f], w_ref[...], 0, 0), finish

    add_normed([block(f) for f in range(n)])
    share = tokens // n_groups
    for j, out in enumerate(outs):
        group = peer(place[0], j, n_groups)
        for f in range(n):
            out[f] = mix[f, pl.ds(pl.multiple_of(group * share, SUB), share), :]


def late_kernel(frame, n_groups, halves, place, counts, lists, qn_ref, sum_ref, ra_ref, rb_ref, *rest):
    outs, (att, rows) = rest[:n_groups * halves], rest[n_groups * halves:]
    n, width, tokens = qn_ref.shape
    remote_attend(frame, place, counts, lists, qn_ref, sum_ref, ra_ref, rb_ref, att)
    for f in range(n):
        rows[:, f * width:(f + 1) * width] = att[f].T.astype(BF)
    size = tokens // n_groups // halves
    for half in range(halves):
        for j in range(n_groups):
            start = (peer(place[0], j, n_groups) * halves + half) * size
            outs[half * n_groups + j][...] = rows[pl.ds(pl.multiple_of(start, SUB), size), :]


def mix_kernel(*refs):
    w_ref, g_ref, out = refs[-3:]
    n_groups, n, share, _ = out.shape
    atts, hids = refs[:-3 - n_groups], refs[-3 - n_groups:-3]
    width = w_ref.shape[0]
    rows = atts[0].shape[0]
    halves = share // rows

    def block(js):
        def start():
            x = [
                atts[half * n_groups + j][:, f * width:(f + 1) * width]
                for j in js
                for f in range(n)
                for half in range(halves)
            ]
            return contract(jnp.concatenate(x, axis=0), w_ref[...], 1, 0)

        def finish(normed):
            for i, j in enumerate(js):
                for f in range(n):
                    at = (i * n + f) * share
                    part = normed[at:at + share, :] * g_ref[...]
                    out[j, f] = (hids[j][f].astype(F32) + part).astype(BF)

        return start, finish

    add_normed([block(js) for js in blocks_of(n_groups, n * share)])


def blocks_of(n_groups, rows):
    size = max(1, min(n_groups, 2 * TILE // rows))
    return [range(at, min(at + size, n_groups)) for at in range(0, n_groups, size)]


def paired(chunks, lanes, frames):
    return chunks % 2 == 0 and frames % 2 == 0 and 2 * lanes == TILE


def slot(c, frame, chunks, n_groups, frames):
    return c ^ (frame & 1) if paired(chunks, n_groups * SUB, frames) else c


def project(w_ref, x, out):
    width = w_ref.shape[0] // 3
    cut = w_ref.shape[0] // 2
    heads = width // HEAD_DIM
    parts = [contract(w_ref[i * cut:(i + 1) * cut, :], x, 1, 1) for i in range(2)]
    for h in range(3 * heads):
        i, at = divmod(h * HEAD_DIM, cut)
        y = parts[i][at:at + HEAD_DIM, :]
        if h < 2 * heads:
            y = y * head_scale(y)
        out[head(h), :] = y.astype(BF)


def project_kernel(frame, frames, *refs):
    pieces, w_ref, out, x = refs[:-3], refs[-3], refs[-2], refs[-1]
    n_groups = len(pieces)
    chunks = pieces[0].shape[1] // SUB
    for c in range(chunks):
        for j, piece in enumerate(pieces):
            at = (slot(c, frame, chunks, n_groups, frames) * n_groups + j) * SUB
            x[at:at + SUB, :] = piece[0, c * SUB:(c + 1) * SUB, :]
    project(w_ref, x[...], out)


def late_project_kernel(frame, frames, *refs):
    n_groups = (len(refs) - 7) // 2
    atts, hids = refs[:n_groups], refs[n_groups:2 * n_groups]
    w_ref, g_ref, qkv_ref, out, a, b, x = refs[2 * n_groups:]
    width = w_ref.shape[0]
    n, rows, _ = hids[0].shape
    chunks = rows // SUB
    for f in range(n):
        for c in range(chunks):
            for j in range(n_groups):
                at = ((f * chunks + slot(c, frame + f, chunks, n_groups, frames)) * n_groups + j) * SUB
                piece = slice(c * SUB, (c + 1) * SUB)
                a[at:at + SUB, :] = atts[j][piece, f * width:(f + 1) * width]
                b[at:at + SUB, :] = hids[j][f, piece, :]

    def finish(normed):
        x[...] = (b[...].astype(F32) + normed * g_ref[...]).astype(BF)

    add_normed([(lambda: contract(a[...], w_ref[...], 1, 0), finish)])
    project(qkv_ref, x[...], out)


def temporal_kernel(n_groups, *refs):
    frames = len(refs) - n_groups - 1
    ins, outs, att = refs[:frames], refs[frames:frames + n_groups], refs[-1]
    lanes = n_groups * SUB
    chunks = ins[0].shape[1] // lanes
    width = ins[0].shape[0] // 3
    rows = frames * lanes
    pair = paired(chunks, lanes, frames)
    row_pos = lax.broadcasted_iota(jnp.int32, (rows, rows), 0) % SUB
    col_pos = lax.broadcasted_iota(jnp.int32, (rows, rows), 1) % SUB
    same = jnp.where(row_pos == col_pos, 1.0, 0.0).astype(BF)
    low = lax.broadcasted_iota(jnp.int32, (HEAD_DIM, TILE), 1) < lanes

    def take(c, where):
        if not pair:
            return jnp.concatenate([r[where, c * lanes:(c + 1) * lanes] for r in ins], axis=1)
        tile = slice(c // 2 * TILE, (c // 2 + 1) * TILE)
        got = [r[where, tile] for r in ins]
        return jnp.concatenate(
            [
                jnp.where(low, got[m + (c & 1)], got[m + 1 - (c & 1)])
                for m in range(0, frames, 2)
            ],
            axis=1,
        )

    def scores(c, h):
        return contract(take(c, head(h, width)), take(c, head(h)), 0, 0)

    def weigh(s):
        return jnp.exp2(s * EXP2_SCALE).astype(BF) * same

    def gather(c, h, p):
        att[c, head(h), :] = averaged(contract(with_ones(take(c, head(h, 2 * width))), p, 1, 0))

    steps = [(c, h) for c in range(chunks) for h in range(width // HEAD_DIM)]
    pipeline(steps, scores, weigh, gather)
    turned = [att[c].T.astype(BF) for c in range(chunks)]
    for j, out in enumerate(outs):
        for c in range(chunks):
            for f in range(frames):
                at = (f ^ (c & 1) if pair else f) * lanes + j * SUB
                out[c * SUB:(c + 1) * SUB, f * width:(f + 1) * width] = turned[c][at:at + SUB, :]


def output_kernel(n_groups, js, early, half, halves, aliased, place, *refs):
    n = len(js)
    atts, pieces = refs[:n], refs[n:n * (1 + early)]
    late_ref, w_ref, g_ref = refs[n * (1 + early):n * (1 + early) + 3]
    out, buf, sems = refs[n * (1 + early) + 3 + aliased:]
    _, late, rows, _ = late_ref.shape
    width = w_ref.shape[0]
    frames = early + late
    copies = []

    def block(some):
        def start():
            x = [atts[i][:, f * width:(f + 1) * width] for i in some for f in range(frames)]
            return contract(jnp.concatenate(x, axis=0), w_ref[...], 1, 0)

        def finish(normed):
            for k, i in enumerate(some):
                j = js[i]
                for f in range(frames):
                    mine = pieces[i * early + f][0] if f < early else late_ref[j, f - early]
                    at = (k * frames + f) * rows
                    part = normed[at:at + rows, :] * g_ref[...]
                    buf[i, f] = (mine.astype(F32) + part).astype(BF)
                group = peer(place[0], j, n_groups)
                at = pl.multiple_of((group * halves + half) * rows, SUB)
                copy = pltpu.make_async_copy(buf.at[i], out.at[:, pl.ds(at, rows), :], sems.at[i])
                copy.start()
                copies.append(copy)

        return start, finish

    add_normed([block(some) for some in blocks_of(len(js), frames * rows)])
    for copy in copies:
        copy.wait()


def shards(
    spatial_queries,
    spatial_keys,
    spatial_values,
    hidden,
    spatial_out_weight,
    spatial_gain,
    temporal_qkv_weight,
    temporal_out_weight,
    temporal_gain,
    tile_list,
    tile_count,
):
    frames, tokens, width = spatial_queries.shape
    model = hidden.shape[2]
    groups = lax.axis_size("frame")
    strips = lax.axis_size("strip")
    share = tokens // groups
    halves = 2 if share % (4 * SUB) == 0 else 1
    rows = share // halves
    queries = pltpu.with_memory_space_constraint(jnp.transpose(spatial_queries, (0, 2, 1)), pltpu.HBM)
    keys = pltpu.with_memory_space_constraint(jnp.transpose(spatial_keys, (0, 2, 1)), pltpu.HBM)
    values = pltpu.with_memory_space_constraint(jnp.transpose(spatial_values, (0, 2, 1)), pltpu.HBM)
    hidden_far = pltpu.with_memory_space_constraint(hidden, pltpu.HBM)
    lists = jnp.transpose(tile_list, (2, 1, 0))
    counts = tile_count.T
    qkv_weight = temporal_qkv_weight.T
    gain_one = spatial_gain.reshape(1, model)
    gain_two = temporal_gain.reshape(1, model)
    place = jnp.stack([lax.axis_index("frame"), lax.axis_index("strip")]).astype(jnp.int32)
    near = [(i, i ^ 1) for i in range(strips) if i ^ 1 < strips]
    far = [e for i in range(1, strips - 1, 2) for e in ((i, i + 1), (i + 1, i))]
    edge = jax.ShapeDtypeStruct((2 * width, TILE), BF)
    smem = pl.BlockSpec(memory_space=pltpu.SMEM)
    any_spec = pl.BlockSpec(memory_space=pl.ANY)

    def call(kernel, in_specs, out_specs, out_shape, scratch=(), limit=32, prefetch=0, alias=None):
        return pl.pallas_call(
            kernel,
            grid_spec=pltpu.PrefetchScalarGridSpec(
                num_scalar_prefetch=prefetch,
                grid=(1,),
                in_specs=in_specs,
                out_specs=out_specs,
                scratch_shapes=list(scratch),
            ),
            out_shape=out_shape,
            input_output_aliases=alias or {},
            compiler_params=vmem(limit),
        )

    late = frames // 2
    early = frames - late

    def out_pairs(j):
        return [(i, peer(i, j, groups)) for i in range(groups)]

    def send(parts):
        sent = {j: lax.ppermute(parts[j], "frame", out_pairs(j)) for j in reversed(range(1, groups))}
        return [parts[0]] + [sent[j] for j in range(1, groups)]

    halos = []
    for some in range(2):
        block = pl.BlockSpec((late, width, tokens), lambda *_, some=some: (some, 0, 0))
        split = groups if some == 1 else 0
        a, b, *pieces = call(
            prep_kernel,
            [smem, block, block] + [any_spec] * bool(split),
            [whole((late,) + edge.shape)] * 2 + [any_spec] * split,
            [jax.ShapeDtypeStruct((late,) + edge.shape, BF)] * 2
            + [jax.ShapeDtypeStruct((late, share, model), BF)] * split,
            [pltpu.SemaphoreType.DMA((groups,))] * bool(split),
            limit=16,
        )(place, keys, values, *[hidden_far] * bool(split))
        if split:
            own_hidden = pieces
        halos.append((a, b, lax.ppermute(a, "strip", near), lax.ppermute(b, "strip", far)))
    far_hidden = send(own_hidden)

    sum_shape = (late, width // HEAD_DIM * (HEAD_DIM + 8), tokens)
    own_sums = []
    for some in range(2):
        block = pl.BlockSpec((late, width, tokens), lambda *_, some=some: (some, 0, 0))
        own_sums.append(
            call(
                functools.partial(local_kernel, some * late),
                [smem, smem, smem, block] + [whole((late,) + edge.shape)] * 2,
                [whole((late, width, tokens)), whole(sum_shape)],
                [
                    jax.ShapeDtypeStruct((late, width, tokens), BF),
                    jax.ShapeDtypeStruct(sum_shape, F32),
                ],
            )(place, counts, lists, queries, *halos[some][:2])
        )
    sum_specs = [whole((late, width, tokens)), whole(sum_shape)]

    def one(shape, f):
        return pl.BlockSpec((1,) + shape[1:], lambda *_: (f, 0, 0))

    mixed, projected = [], []
    for f in range(early):
        mixed.append(
            call(
                functools.partial(spatial_kernel, f, groups),
                [smem, smem, smem, one((late, width, tokens), f), one(sum_shape, f)]
                + [one((late,) + edge.shape, f)] * 2
                + [one(hidden.shape, f), whole((width, model)), whole((1, model))],
                [whole((1, share, model))] * groups,
                [jax.ShapeDtypeStruct((1, share, model), BF)] * groups,
                [
                    pltpu.VMEM((1, width, tokens), BF),
                    pltpu.VMEM((1, tokens, model), BF),
                ],
            )(place, counts, lists, *own_sums[0], *halos[0][2:], hidden, spatial_out_weight, gain_one)
        )
        arrived = send(mixed[f])
        projected.append(
            call(
                functools.partial(project_kernel, f, frames),
                [whole((1, share, model))] * groups + [whole((3 * width, model))],
                whole((3 * width, tokens)),
                jax.ShapeDtypeStruct((3 * width, tokens), BF),
                [pltpu.VMEM((tokens, model), BF)],
            )(*arrived, qkv_weight)
        )

    late_shape = (rows, late * width)
    own_late = call(
        functools.partial(late_kernel, early, groups, halves),
        [smem, smem, smem] + sum_specs + [whole((late,) + edge.shape)] * 2,
        [whole(late_shape)] * (groups * halves),
        [jax.ShapeDtypeStruct(late_shape, BF)] * (groups * halves),
        [pltpu.VMEM((late, width, tokens), F32), pltpu.VMEM((tokens, late * width), BF)],
    )(place, counts, lists, *own_sums[1], *halos[1][2:])
    own_late = [own_late[half * groups:(half + 1) * groups] for half in range(halves)]
    far_late = []
    for half in range(halves):
        far_late.append(send(own_late[half]))

    returned = []
    back_shape = (rows, frames * width)
    lanes = tokens // halves
    for half in range(halves):
        hid_block = pl.BlockSpec((late, rows, model), lambda *_, half=half: (0, half, 0))
        late_specs = [whole(late_shape)] * groups + [hid_block] * groups
        late_specs += [whole((width, model)), whole((1, model))]
        late_projected = call(
            functools.partial(late_project_kernel, early, frames),
            late_specs + [whole((3 * width, model))],
            whole((3 * width, late * lanes)),
            jax.ShapeDtypeStruct((3 * width, late * lanes), BF),
            [
                pltpu.VMEM((late * lanes, width), BF),
                pltpu.VMEM((late * lanes, model), BF),
                pltpu.VMEM((late * lanes, model), BF),
            ],
        )(*far_late[half], *far_hidden, spatial_out_weight, gain_one, qkv_weight)
        back = call(
            functools.partial(temporal_kernel, groups),
            [pl.BlockSpec((3 * width, lanes), lambda *_, half=half: (0, half))] * early
            + [pl.BlockSpec((3 * width, lanes), lambda *_, f=f: (0, f)) for f in range(late)],
            [whole(back_shape)] * groups,
            [jax.ShapeDtypeStruct(back_shape, BF)] * groups,
            [pltpu.VMEM((rows // SUB, width, groups * frames * SUB), F32)],
        )(*projected, *[late_projected] * late)
        home = {
            j: lax.ppermute(back[j], "frame", [(b, a) for a, b in out_pairs(j)])
            for j in reversed(range(1, groups))
        }
        returned.append([back[0]] + [home[j] for j in range(1, groups)])

    late_mixed = call(
        mix_kernel,
        [whole(late_shape)] * (groups * halves)
        + [whole((late, share, model))] * groups
        + [whole((width, model)), whole((1, model))],
        whole((groups, late, share, model)),
        jax.ShapeDtypeStruct((groups, late, share, model), BF),
    )(*[x for some in own_late for x in some], *own_hidden, spatial_out_weight, gain_one)

    out = None
    for half in range(halves):
        piece = pl.BlockSpec((1, rows, model), lambda *_, half=half: (0, half, 0))
        cuts = [groups] if half + 1 < halves else [groups // 2, groups]
        for lo, hi in zip([0] + cuts, cuts):
            js = range(lo, hi)
            if not js:
                continue
            extra = [] if out is None else [out]
            out = call(
                functools.partial(output_kernel, groups, tuple(js), early, half, halves, len(extra)),
                [smem]
                + [whole(back_shape)] * len(js)
                + [piece] * (len(js) * early)
                + [pl.BlockSpec((groups, late, rows, model), lambda *_, half=half: (0, 0, half, 0))]
                + [whole((width, model)), whole((1, model))]
                + [any_spec] * len(extra),
                any_spec,
                jax.ShapeDtypeStruct((frames, tokens, model), BF),
                [
                    pltpu.VMEM((len(js), frames, rows, model), BF),
                    pltpu.SemaphoreType.DMA((len(js),)),
                ],
                alias={4 + len(js) * (1 + early): 0} if extra else None,
            )(
                place,
                *[returned[half][j] for j in js],
                *[mixed[f][j] for j in js for f in range(early)],
                late_mixed,
                temporal_out_weight,
                gain_two,
                *extra,
            )
    return out


def solution(mesh):
    rows = P(("group", "frame"), "strip", None)
    placed = (rows, rows, rows, rows, P(), P(), P(), P(), P(), rows, P(("group", "frame"), "strip"))

    return jax.shard_map(shards, mesh=mesh, in_specs=placed, out_specs=rows, check_vma=False)
```

```python
import functools
import math

import jax
import jax.numpy as jnp
from jax import lax
from jax.experimental import pallas as pl
from jax.experimental.pallas import tpu as pltpu
from jax.sharding import PartitionSpec as P


HEAD_DIM = 72
TILE = 128
MAXT = 3
SUB = 16
EPS = 1e-06
EXP2_SCALE = HEAD_DIM ** -0.5 * math.log2(math.e)

BF = jnp.bfloat16
F32 = jnp.float32


def peer(i, j, n):
    return i ^ j if n & (n - 1) == 0 else (i + j) % n


def vmem(limit):
    return pltpu.CompilerParams(vmem_limit_bytes=limit << 20)


def whole(shape):
    return pl.BlockSpec(shape, lambda *_: (0,) * len(shape))


def contract(a, b, da, db):
    return lax.dot_general(a, b, (((da,), (db,)), ((), ())), preferred_element_type=F32)


def head_scale(x):
    return lax.rsqrt(jnp.mean(x * x, axis=0, keepdims=True) + EPS)


def head(h, base=0):
    return slice(base + h * HEAD_DIM, base + (h + 1) * HEAD_DIM)


def with_ones(v):
    return jnp.concatenate([v, jnp.ones((8, v.shape[1]), v.dtype)], axis=0)


def averaged(o):
    return o[:HEAD_DIM, :] / o[HEAD_DIM:HEAD_DIM + 1, :]


def pipeline(steps, scores, weigh, gather):
    ahead, behind = scores(*steps[0]), None
    for n, step in enumerate(steps):
        now = ahead
        if n + 1 < len(steps):
            ahead = scores(*steps[n + 1])
        weighed = weigh(now)
        if behind is not None:
            gather(*steps[n - 1], behind)
        behind = weighed
    gather(*steps[-1], behind)


def prep_kernel(place, k_ref, v_ref, *refs):
    n, width, _ = k_ref.shape
    even = place[1] % 2 == 0
    copies = []
    if len(refs) > 2:
        src, (a_ref, b_ref), pieces, sems = refs[0], refs[1:3], refs[3:-1], refs[-1]
        late, share, _ = pieces[0].shape
        for j in reversed(range(len(pieces))):
            start = pl.multiple_of(peer(place[0], j, len(pieces)) * share, SUB)
            part = src.at[pl.ds(src.shape[0] - late, late), pl.ds(start, share), :]
            copies.append(pltpu.make_async_copy(part, pieces[j], sems.at[j]))
            copies[-1].start()
    else:
        a_ref, b_ref = refs

    def fill(first, second):
        for f in range(n):
            for h in range(width // HEAD_DIM):
                x = k_ref[f, head(h), :].astype(F32)
                y = (x * head_scale(x)).astype(BF)
                first[f, head(h), :] = y[:, :TILE]
                second[f, head(h), :] = y[:, TILE:]
            first[f, width:, :] = v_ref[f, :, :TILE]
            second[f, width:, :] = v_ref[f, :, TILE:]

    pl.when(even)(functools.partial(fill, b_ref, a_ref))
    pl.when(jnp.logical_not(even))(functools.partial(fill, a_ref, b_ref))
    for copy in copies:
        copy.wait()


def tile_masks(frame, n, tiles, local, place, counts, lists):
    strip = place[1]
    odd = strip % 2
    first = strip * tiles
    if local:
        spots = (first + 1 - odd, first + odd)
    else:
        spots = (first + 2 - 3 * odd, first - 1 + 3 * odd)
    masks = []
    for f in range(n):
        rows = []
        for spot in spots:
            cells = []
            for t in range(tiles):
                hit = jnp.bool_(False)
                for j in range(MAXT):
                    hit = hit | ((lists[j, t, frame + f] == spot) & (j < counts[t, frame + f]))
                cells.append(jnp.full((SUB, TILE), jnp.where(hit, 1.0, 0.0), F32))
            rows.append(jnp.concatenate(cells, axis=1).astype(BF))
        masks.append(rows)
    return masks


def attend(masks, keys, query, finish):
    n = keys[0].shape[0]
    width = keys[0].shape[1] // 2

    def scores(f, h):
        qn = query(f, h)
        return f, [contract(ref[f, head(h), :], qn, 0, 0) for ref in keys]

    def weigh(scored):
        f, s = scored
        packed = []
        for mask, x in zip(masks[f], s):
            p = jnp.exp2(x * EXP2_SCALE).astype(BF).reshape(TILE // SUB, SUB, x.shape[1])
            packed.append((p * mask).reshape(x.shape))
        return jnp.concatenate(packed, axis=0)

    def gather(f, h, weights):
        v = jnp.concatenate([ref[f, head(h, width), :] for ref in keys], axis=1)
        finish(f, h, contract(with_ones(v), weights, 1, 0))

    pipeline([(f, h) for f in range(n) for h in range(width // HEAD_DIM)], scores, weigh, gather)


def sums(h):
    return slice(h * (HEAD_DIM + 8), (h + 1) * (HEAD_DIM + 8))


def local_kernel(frame, place, counts, lists, q_ref, a_ref, b_ref, qn_ref, sum_ref):
    n, _, tokens = q_ref.shape

    def query(f, h):
        q = q_ref[f, head(h), :].astype(F32)
        qn = (q * head_scale(q)).astype(BF)
        qn_ref[f, head(h), :] = qn
        return qn

    def finish(f, h, o):
        sum_ref[f, sums(h), :] = o

    masks = tile_masks(frame, n, tokens // TILE, True, place, counts, lists)
    attend(masks, (a_ref, b_ref), query, finish)


def remote_attend(frame, place, counts, lists, qn_ref, sum_ref, ra_ref, rb_ref, att, done=None):
    n, width, tokens = qn_ref.shape

    def query(f, h):
        return qn_ref[f, head(h), :]

    def finish(f, h, o):
        att[f, head(h), :] = averaged(o + sum_ref[f, sums(h), :]).astype(att.dtype)
        if done and (h + 1) * HEAD_DIM == width:
            done(f)

    masks = tile_masks(frame, n, tokens // TILE, False, place, counts, lists)
    attend(masks, (ra_ref, rb_ref), query, finish)


def add_normed(blocks):
    ahead = blocks[0][0]()
    for n, (_, finish) in enumerate(blocks):
        proj = ahead
        if n + 1 < len(blocks):
            ahead = blocks[n + 1][0]()
        scale = lax.rsqrt(jnp.mean(proj * proj, axis=-1, keepdims=True) + EPS)
        finish(proj * scale)


def spatial_kernel(frame, n_groups, place, counts, lists, qn_ref, sum_ref, ra_ref, rb_ref, h_ref, w_ref, g_ref, *rest):
    outs, (att, mix) = rest[:n_groups], rest[n_groups:]
    remote_attend(frame, place, counts, lists, qn_ref, sum_ref, ra_ref, rb_ref, att)
    n, tokens, _ = h_ref.shape

    def block(f):
        def finish(normed):
            mix[f] = (h_ref[f].astype(F32) + normed * g_ref[...]).astype(BF)

        return lambda: contract(att[f], w_ref[...], 0, 0), finish

    add_normed([block(f) for f in range(n)])
    share = tokens // n_groups
    for j, out in enumerate(outs):
        group = peer(place[0], j, n_groups)
        for f in range(n):
            out[f] = mix[f, pl.ds(pl.multiple_of(group * share, SUB), share), :]


def late_kernel(frame, n_groups, halves, place, counts, lists, qn_ref, sum_ref, ra_ref, rb_ref, *rest):
    outs, (att, rows) = rest[:n_groups * halves], rest[n_groups * halves:]
    _, width, tokens = qn_ref.shape

    def turn(f):
        rows[:, f * width:(f + 1) * width] = att[f].T.astype(BF)

    remote_attend(frame, place, counts, lists, qn_ref, sum_ref, ra_ref, rb_ref, att, turn)
    size = tokens // n_groups // halves
    for half in range(halves):
        for j in range(n_groups):
            start = (peer(place[0], j, n_groups) * halves + half) * size
            outs[half * n_groups + j][...] = rows[pl.ds(pl.multiple_of(start, SUB), size), :]


def mix_kernel(*refs):
    w_ref, g_ref, out = refs[-3:]
    n_groups, n, share, _ = out.shape
    atts, hids = refs[:-3 - n_groups], refs[-3 - n_groups:-3]
    width = w_ref.shape[0]
    rows = atts[0].shape[0]
    halves = share // rows

    def block(js):
        def start():
            x = [
                atts[half * n_groups + j][:, f * width:(f + 1) * width]
                for j in js
                for f in range(n)
                for half in range(halves)
            ]
            return contract(jnp.concatenate(x, axis=0), w_ref[...], 1, 0)

        def finish(normed):
            for i, j in enumerate(js):
                for f in range(n):
                    at = (i * n + f) * share
                    part = normed[at:at + share, :] * g_ref[...]
                    out[j, f] = (hids[j][f].astype(F32) + part).astype(BF)

        return start, finish

    add_normed([block(js) for js in blocks_of(n_groups, n * share)])


def blocks_of(n_groups, rows):
    size = max(1, min(n_groups, 2 * TILE // rows))
    return [range(at, min(at + size, n_groups)) for at in range(0, n_groups, size)]


def paired(chunks, lanes, frames):
    return chunks % 2 == 0 and frames % 2 == 0 and 2 * lanes == TILE


def slot(c, frame, chunks, n_groups, frames):
    return c ^ (frame & 1) if paired(chunks, n_groups * SUB, frames) else c


def project(w_ref, x, out):
    width = w_ref.shape[0] // 3
    cut = w_ref.shape[0] // 2
    heads = width // HEAD_DIM
    parts = [contract(w_ref[i * cut:(i + 1) * cut, :], x, 1, 1) for i in range(2)]
    for h in range(3 * heads):
        i, at = divmod(h * HEAD_DIM, cut)
        y = parts[i][at:at + HEAD_DIM, :]
        if h < 2 * heads:
            y = y * head_scale(y)
        out[head(h), :] = y.astype(BF)


def project_kernel(frame, frames, *refs):
    pieces, w_ref, out, x = refs[:-3], refs[-3], refs[-2], refs[-1]
    n_groups = len(pieces)
    chunks = pieces[0].shape[1] // SUB
    for c in range(chunks):
        for j, piece in enumerate(pieces):
            at = (slot(c, frame, chunks, n_groups, frames) * n_groups + j) * SUB
            x[at:at + SUB, :] = piece[0, c * SUB:(c + 1) * SUB, :]
    project(w_ref, x[...], out)


def late_project_kernel(frame, frames, *refs):
    n_groups = (len(refs) - 7) // 2
    atts, hids = refs[:n_groups], refs[n_groups:2 * n_groups]
    w_ref, g_ref, qkv_ref, out, a, b, x = refs[2 * n_groups:]
    width = w_ref.shape[0]
    n, rows, _ = hids[0].shape
    chunks = rows // SUB
    for f in range(n):
        for c in range(chunks):
            for j in range(n_groups):
                at = ((f * chunks + slot(c, frame + f, chunks, n_groups, frames)) * n_groups + j) * SUB
                piece = slice(c * SUB, (c + 1) * SUB)
                a[at:at + SUB, :] = atts[j][piece, f * width:(f + 1) * width]
                b[at:at + SUB, :] = hids[j][f, piece, :]

    def finish(normed):
        x[...] = (b[...].astype(F32) + normed * g_ref[...]).astype(BF)

    add_normed([(lambda: contract(a[...], w_ref[...], 1, 0), finish)])
    project(qkv_ref, x[...], out)


def temporal_kernel(n_groups, *refs):
    frames = len(refs) - n_groups - 1
    ins, outs, att = refs[:frames], refs[frames:frames + n_groups], refs[-1]
    lanes = n_groups * SUB
    chunks = ins[0].shape[1] // lanes
    width = ins[0].shape[0] // 3
    rows = frames * lanes
    pair = paired(chunks, lanes, frames)
    row_pos = lax.broadcasted_iota(jnp.int32, (rows, rows), 0) % SUB
    col_pos = lax.broadcasted_iota(jnp.int32, (rows, rows), 1) % SUB
    same = jnp.where(row_pos == col_pos, 1.0, 0.0).astype(BF)
    low = lax.broadcasted_iota(jnp.int32, (HEAD_DIM, TILE), 1) < lanes

    def take(c, where):
        if not pair:
            return jnp.concatenate([r[where, c * lanes:(c + 1) * lanes] for r in ins], axis=1)
        tile = slice(c // 2 * TILE, (c // 2 + 1) * TILE)
        got = [r[where, tile] for r in ins]
        return jnp.concatenate(
            [
                jnp.where(low, got[m + (c & 1)], got[m + 1 - (c & 1)])
                for m in range(0, frames, 2)
            ],
            axis=1,
        )

    def scores(c, h):
        return contract(take(c, head(h, width)), take(c, head(h)), 0, 0)

    def weigh(s):
        return jnp.exp2(s * EXP2_SCALE).astype(BF) * same

    def gather(c, h, p):
        att[c, head(h), :] = averaged(contract(with_ones(take(c, head(h, 2 * width))), p, 1, 0))
        if (h + 1) * HEAD_DIM == width:
            turn(c)

    def turn(c):
        turned = att[c].T.astype(BF)
        for j, out in enumerate(outs):
            for f in range(frames):
                at = (f ^ (c & 1) if pair else f) * lanes + j * SUB
                out[c * SUB:(c + 1) * SUB, f * width:(f + 1) * width] = turned[at:at + SUB, :]

    steps = [(c, h) for c in range(chunks) for h in range(width // HEAD_DIM)]
    pipeline(steps, scores, weigh, gather)


def output_kernel(n_groups, js, early, half, halves, aliased, place, *refs):
    n = len(js)
    atts, pieces = refs[:n], refs[n:n * (1 + early)]
    late_ref, w_ref, g_ref = refs[n * (1 + early):n * (1 + early) + 3]
    out, buf, sems = refs[n * (1 + early) + 3 + aliased:]
    _, late, rows, _ = late_ref.shape
    width = w_ref.shape[0]
    frames = early + late
    copies = []

    def block(some):
        def start():
            x = [atts[i][:, f * width:(f + 1) * width] for i in some for f in range(frames)]
            return contract(jnp.concatenate(x, axis=0), w_ref[...], 1, 0)

        def finish(normed):
            for k, i in enumerate(some):
                j = js[i]
                for f in range(frames):
                    mine = pieces[i * early + f][0] if f < early else late_ref[j, f - early]
                    at = (k * frames + f) * rows
                    part = normed[at:at + rows, :] * g_ref[...]
                    buf[i, f] = (mine.astype(F32) + part).astype(BF)
                group = peer(place[0], j, n_groups)
                at = pl.multiple_of((group * halves + half) * rows, SUB)
                copy = pltpu.make_async_copy(buf.at[i], out.at[:, pl.ds(at, rows), :], sems.at[i])
                copy.start()
                copies.append(copy)

        return start, finish

    add_normed([block(some) for some in blocks_of(len(js), frames * rows)])
    for copy in copies:
        copy.wait()


def shards(
    spatial_queries,
    spatial_keys,
    spatial_values,
    hidden,
    spatial_out_weight,
    spatial_gain,
    temporal_qkv_weight,
    temporal_out_weight,
    temporal_gain,
    tile_list,
    tile_count,
):
    frames, tokens, width = spatial_queries.shape
    model = hidden.shape[2]
    groups = lax.axis_size("frame")
    strips = lax.axis_size("strip")
    share = tokens // groups
    halves = 2 if share % (4 * SUB) == 0 else 1
    rows = share // halves
    queries = pltpu.with_memory_space_constraint(jnp.transpose(spatial_queries, (0, 2, 1)), pltpu.HBM)
    keys = pltpu.with_memory_space_constraint(jnp.transpose(spatial_keys, (0, 2, 1)), pltpu.HBM)
    values = pltpu.with_memory_space_constraint(jnp.transpose(spatial_values, (0, 2, 1)), pltpu.HBM)
    hidden_far = pltpu.with_memory_space_constraint(hidden, pltpu.HBM)
    lists = jnp.transpose(tile_list, (2, 1, 0))
    counts = tile_count.T
    qkv_weight = temporal_qkv_weight.T
    gain_one = spatial_gain.reshape(1, model)
    gain_two = temporal_gain.reshape(1, model)
    place = jnp.stack([lax.axis_index("frame"), lax.axis_index("strip")]).astype(jnp.int32)
    near = [(i, i ^ 1) for i in range(strips) if i ^ 1 < strips]
    far = [e for i in range(1, strips - 1, 2) for e in ((i, i + 1), (i + 1, i))]
    edge = jax.ShapeDtypeStruct((2 * width, TILE), BF)
    smem = pl.BlockSpec(memory_space=pltpu.SMEM)
    any_spec = pl.BlockSpec(memory_space=pl.ANY)

    def call(kernel, in_specs, out_specs, out_shape, scratch=(), limit=32, prefetch=0, alias=None):
        return pl.pallas_call(
            kernel,
            grid_spec=pltpu.PrefetchScalarGridSpec(
                num_scalar_prefetch=prefetch,
                grid=(1,),
                in_specs=in_specs,
                out_specs=out_specs,
                scratch_shapes=list(scratch),
            ),
            out_shape=out_shape,
            input_output_aliases=alias or {},
            compiler_params=vmem(limit),
        )

    late = frames // 2
    early = frames - late

    def out_pairs(j):
        return [(i, peer(i, j, groups)) for i in range(groups)]

    def send(parts):
        sent = {j: lax.ppermute(parts[j], "frame", out_pairs(j)) for j in reversed(range(1, groups))}
        return [parts[0]] + [sent[j] for j in range(1, groups)]

    halos = []
    for some in range(2):
        block = pl.BlockSpec((late, width, tokens), lambda *_, some=some: (some, 0, 0))
        split = groups if some == 1 else 0
        a, b, *pieces = call(
            prep_kernel,
            [smem, block, block] + [any_spec] * bool(split),
            [whole((late,) + edge.shape)] * 2 + [any_spec] * split,
            [jax.ShapeDtypeStruct((late,) + edge.shape, BF)] * 2
            + [jax.ShapeDtypeStruct((late, share, model), BF)] * split,
            [pltpu.SemaphoreType.DMA((groups,))] * bool(split),
            limit=16,
        )(place, keys, values, *[hidden_far] * bool(split))
        if split:
            own_hidden = pieces
        halos.append((a, b, lax.ppermute(a, "strip", near), lax.ppermute(b, "strip", far)))
    far_hidden = send(own_hidden)

    sum_shape = (late, width // HEAD_DIM * (HEAD_DIM + 8), tokens)
    own_sums = []
    for some in range(2):
        block = pl.BlockSpec((late, width, tokens), lambda *_, some=some: (some, 0, 0))
        own_sums.append(
            call(
                functools.partial(local_kernel, some * late),
                [smem, smem, smem, block] + [whole((late,) + edge.shape)] * 2,
                [whole((late, width, tokens)), whole(sum_shape)],
                [
                    jax.ShapeDtypeStruct((late, width, tokens), BF),
                    jax.ShapeDtypeStruct(sum_shape, F32),
                ],
            )(place, counts, lists, queries, *halos[some][:2])
        )
    sum_specs = [whole((late, width, tokens)), whole(sum_shape)]

    def one(shape, f):
        return pl.BlockSpec((1,) + shape[1:], lambda *_: (f, 0, 0))

    mixed, projected = [], []
    for f in range(early):
        mixed.append(
            call(
                functools.partial(spatial_kernel, f, groups),
                [smem, smem, smem, one((late, width, tokens), f), one(sum_shape, f)]
                + [one((late,) + edge.shape, f)] * 2
                + [one(hidden.shape, f), whole((width, model)), whole((1, model))],
                [whole((1, share, model))] * groups,
                [jax.ShapeDtypeStruct((1, share, model), BF)] * groups,
                [
                    pltpu.VMEM((1, width, tokens), BF),
                    pltpu.VMEM((1, tokens, model), BF),
                ],
            )(place, counts, lists, *own_sums[0], *halos[0][2:], hidden, spatial_out_weight, gain_one)
        )
        arrived = send(mixed[f])
        projected.append(
            call(
                functools.partial(project_kernel, f, frames),
                [whole((1, share, model))] * groups + [whole((3 * width, model))],
                whole((3 * width, tokens)),
                jax.ShapeDtypeStruct((3 * width, tokens), BF),
                [pltpu.VMEM((tokens, model), BF)],
            )(*arrived, qkv_weight)
        )

    late_shape = (rows, late * width)
    own_late = call(
        functools.partial(late_kernel, early, groups, halves),
        [smem, smem, smem] + sum_specs + [whole((late,) + edge.shape)] * 2,
        [whole(late_shape)] * (groups * halves),
        [jax.ShapeDtypeStruct(late_shape, BF)] * (groups * halves),
        [pltpu.VMEM((late, width, tokens), F32), pltpu.VMEM((tokens, late * width), BF)],
    )(place, counts, lists, *own_sums[1], *halos[1][2:])
    own_late = [own_late[half * groups:(half + 1) * groups] for half in range(halves)]
    far_late = []
    for half in range(halves):
        far_late.append(send(own_late[half]))

    returned = []
    back_shape = (rows, frames * width)
    lanes = tokens // halves
    for half in range(halves):
        hid_block = pl.BlockSpec((late, rows, model), lambda *_, half=half: (0, half, 0))
        late_specs = [whole(late_shape)] * groups + [hid_block] * groups
        late_specs += [whole((width, model)), whole((1, model))]
        late_projected = call(
            functools.partial(late_project_kernel, early, frames),
            late_specs + [whole((3 * width, model))],
            whole((3 * width, late * lanes)),
            jax.ShapeDtypeStruct((3 * width, late * lanes), BF),
            [
                pltpu.VMEM((late * lanes, width), BF),
                pltpu.VMEM((late * lanes, model), BF),
                pltpu.VMEM((late * lanes, model), BF),
            ],
        )(*far_late[half], *far_hidden, spatial_out_weight, gain_one, qkv_weight)
        back = call(
            functools.partial(temporal_kernel, groups),
            [pl.BlockSpec((3 * width, lanes), lambda *_, half=half: (0, half))] * early
            + [pl.BlockSpec((3 * width, lanes), lambda *_, f=f: (0, f)) for f in range(late)],
            [whole(back_shape)] * groups,
            [jax.ShapeDtypeStruct(back_shape, BF)] * groups,
            [pltpu.VMEM((rows // SUB, width, groups * frames * SUB), F32)],
        )(*projected, *[late_projected] * late)
        home = {
            j: lax.ppermute(back[j], "frame", [(b, a) for a, b in out_pairs(j)])
            for j in reversed(range(1, groups))
        }
        returned.append([back[0]] + [home[j] for j in range(1, groups)])

    late_mixed = call(
        mix_kernel,
        [whole(late_shape)] * (groups * halves)
        + [whole((late, share, model))] * groups
        + [whole((width, model)), whole((1, model))],
        whole((groups, late, share, model)),
        jax.ShapeDtypeStruct((groups, late, share, model), BF),
    )(*[x for some in own_late for x in some], *own_hidden, spatial_out_weight, gain_one)

    out = None
    for half in range(halves):
        piece = pl.BlockSpec((1, rows, model), lambda *_, half=half: (0, half, 0))
        cuts = [groups] if half + 1 < halves else [groups // 2, groups]
        for lo, hi in zip([0] + cuts, cuts):
            js = range(lo, hi)
            if not js:
                continue
            extra = [] if out is None else [out]
            out = call(
                functools.partial(output_kernel, groups, tuple(js), early, half, halves, len(extra)),
                [smem]
                + [whole(back_shape)] * len(js)
                + [piece] * (len(js) * early)
                + [pl.BlockSpec((groups, late, rows, model), lambda *_, half=half: (0, 0, half, 0))]
                + [whole((width, model)), whole((1, model))]
                + [any_spec] * len(extra),
                any_spec,
                jax.ShapeDtypeStruct((frames, tokens, model), BF),
                [
                    pltpu.VMEM((len(js), frames, rows, model), BF),
                    pltpu.SemaphoreType.DMA((len(js),)),
                ],
                alias={4 + len(js) * (1 + early): 0} if extra else None,
            )(
                place,
                *[returned[half][j] for j in js],
                *[mixed[f][j] for j in js for f in range(early)],
                late_mixed,
                temporal_out_weight,
                gain_two,
                *extra,
            )
    return out


def solution(mesh):
    rows = P(("group", "frame"), "strip", None)
    placed = (rows, rows, rows, rows, P(), P(), P(), P(), P(), rows, P(("group", "frame"), "strip"))

    return jax.shard_map(shards, mesh=mesh, in_specs=placed, out_specs=rows, check_vma=False)
```

```python
import functools
import math

import jax
import jax.numpy as jnp
from jax import lax
from jax.experimental import pallas as pl
from jax.experimental.pallas import tpu as pltpu
from jax.sharding import PartitionSpec as P


HEAD_DIM = 72
TILE = 128
MAXT = 3
SUB = 16
EPS = 1e-06
EXP2_SCALE = HEAD_DIM ** -0.5 * math.log2(math.e)

BF = jnp.bfloat16
F32 = jnp.float32


def peer(i, j, n):
    return i ^ j if n & (n - 1) == 0 else (i + j) % n


def vmem(limit):
    return pltpu.CompilerParams(vmem_limit_bytes=limit << 20)


def whole(shape):
    return pl.BlockSpec(shape, lambda *_: (0,) * len(shape))


def contract(a, b, da, db):
    return lax.dot_general(a, b, (((da,), (db,)), ((), ())), preferred_element_type=F32)


def head_scale(x):
    return lax.rsqrt(jnp.mean(x * x, axis=0, keepdims=True) + EPS)


def head(h, base=0):
    return slice(base + h * HEAD_DIM, base + (h + 1) * HEAD_DIM)


def with_ones(v):
    return jnp.concatenate([v, jnp.ones((8, v.shape[1]), v.dtype)], axis=0)


def averaged(o):
    return o[:HEAD_DIM, :] / o[HEAD_DIM:HEAD_DIM + 1, :]


def pipeline(steps, scores, weigh, gather):
    ahead, behind = scores(*steps[0]), None
    for n, step in enumerate(steps):
        now = ahead
        if n + 1 < len(steps):
            ahead = scores(*steps[n + 1])
        weighed = weigh(now)
        if behind is not None:
            gather(*steps[n - 1], behind)
        behind = weighed
    gather(*steps[-1], behind)


def prep_kernel(place, k_ref, v_ref, *refs):
    n, width, _ = k_ref.shape
    even = place[1] % 2 == 0
    copies = []
    if len(refs) > 2:
        src, (a_ref, b_ref), pieces, sems = refs[0], refs[1:3], refs[3:-1], refs[-1]
        late, share, _ = pieces[0].shape
        for j in reversed(range(len(pieces))):
            start = pl.multiple_of(peer(place[0], j, len(pieces)) * share, SUB)
            part = src.at[pl.ds(src.shape[0] - late, late), pl.ds(start, share), :]
            copies.append(pltpu.make_async_copy(part, pieces[j], sems.at[j]))
            copies[-1].start()
    else:
        a_ref, b_ref = refs

    def fill(first, second):
        for f in range(n):
            for h in range(width // HEAD_DIM):
                x = k_ref[f, head(h), :].astype(F32)
                y = (x * head_scale(x)).astype(BF)
                first[f, head(h), :] = y[:, :TILE]
                second[f, head(h), :] = y[:, TILE:]
            first[f, width:, :] = v_ref[f, :, :TILE]
            second[f, width:, :] = v_ref[f, :, TILE:]

    pl.when(even)(functools.partial(fill, b_ref, a_ref))
    pl.when(jnp.logical_not(even))(functools.partial(fill, a_ref, b_ref))
    for copy in copies:
        copy.wait()


def tile_masks(frame, n, tiles, local, place, counts, lists):
    strip = place[1]
    odd = strip % 2
    first = strip * tiles
    if local:
        spots = (first + 1 - odd, first + odd)
    else:
        spots = (first + 2 - 3 * odd, first - 1 + 3 * odd)
    masks = []
    for f in range(n):
        rows = []
        for spot in spots:
            cells = []
            for t in range(tiles):
                hit = jnp.bool_(False)
                for j in range(MAXT):
                    hit = hit | ((lists[j, t, frame + f] == spot) & (j < counts[t, frame + f]))
                cells.append(jnp.full((SUB, TILE), jnp.where(hit, 1.0, 0.0), F32))
            rows.append(jnp.concatenate(cells, axis=1).astype(BF))
        masks.append(rows)
    return masks


def attend(masks, keys, query, finish):
    n = keys[0].shape[0]
    width = keys[0].shape[1] // 2

    def scores(f, h):
        qn = query(f, h)
        return f, [contract(ref[f, head(h), :], qn, 0, 0) for ref in keys]

    def weigh(scored):
        f, s = scored
        packed = []
        for mask, x in zip(masks[f], s):
            p = jnp.exp2(x * EXP2_SCALE).astype(BF).reshape(TILE // SUB, SUB, x.shape[1])
            packed.append((p * mask).reshape(x.shape))
        return jnp.concatenate(packed, axis=0)

    def gather(f, h, weights):
        v = jnp.concatenate([ref[f, head(h, width), :] for ref in keys], axis=1)
        finish(f, h, contract(with_ones(v), weights, 1, 0))

    pipeline([(f, h) for f in range(n) for h in range(width // HEAD_DIM)], scores, weigh, gather)


def sums(h):
    return slice(h * (HEAD_DIM + 8), (h + 1) * (HEAD_DIM + 8))


def local_kernel(frame, place, counts, lists, q_ref, a_ref, b_ref, qn_ref, sum_ref):
    n, _, tokens = q_ref.shape

    def query(f, h):
        q = q_ref[f, head(h), :].astype(F32)
        qn = (q * head_scale(q)).astype(BF)
        qn_ref[f, head(h), :] = qn
        return qn

    def finish(f, h, o):
        sum_ref[f, sums(h), :] = o

    masks = tile_masks(frame, n, tokens // TILE, True, place, counts, lists)
    attend(masks, (a_ref, b_ref), query, finish)


def remote_attend(frame, place, counts, lists, qn_ref, sum_ref, ra_ref, rb_ref, att, done=None):
    n, width, tokens = qn_ref.shape

    def query(f, h):
        return qn_ref[f, head(h), :]

    def finish(f, h, o):
        att[f, head(h), :] = averaged(o + sum_ref[f, sums(h), :]).astype(att.dtype)
        if done and (h + 1) * HEAD_DIM == width:
            done(f)

    masks = tile_masks(frame, n, tokens // TILE, False, place, counts, lists)
    attend(masks, (ra_ref, rb_ref), query, finish)


def add_normed(blocks):
    ahead = blocks[0][0]()
    for n, (_, finish) in enumerate(blocks):
        proj = ahead
        if n + 1 < len(blocks):
            ahead = blocks[n + 1][0]()
        scale = lax.rsqrt(jnp.mean(proj * proj, axis=-1, keepdims=True) + EPS)
        finish(proj * scale)


def spatial_kernel(frame, n_groups, place, counts, lists, qn_ref, sum_ref, ra_ref, rb_ref, h_ref, w_ref, g_ref, *rest):
    outs, (att, mix) = rest[:n_groups], rest[n_groups:]
    remote_attend(frame, place, counts, lists, qn_ref, sum_ref, ra_ref, rb_ref, att)
    n, tokens, _ = h_ref.shape

    def block(f):
        def finish(normed):
            mix[f] = (h_ref[f].astype(F32) + normed * g_ref[...]).astype(BF)

        return lambda: contract(att[f], w_ref[...], 0, 0), finish

    add_normed([block(f) for f in range(n)])
    share = tokens // n_groups
    for j, out in enumerate(outs):
        group = peer(place[0], j, n_groups)
        for f in range(n):
            out[f] = mix[f, pl.ds(pl.multiple_of(group * share, SUB), share), :]


def late_kernel(frame, n_groups, halves, place, counts, lists, qn_ref, sum_ref, ra_ref, rb_ref, *rest):
    outs, (att, rows) = rest[:n_groups * halves], rest[n_groups * halves:]
    _, width, tokens = qn_ref.shape

    def turn(f):
        rows[:, f * width:(f + 1) * width] = att[f].T

    remote_attend(frame, place, counts, lists, qn_ref, sum_ref, ra_ref, rb_ref, att, turn)
    size = tokens // n_groups // halves
    for half in range(halves):
        for j in range(n_groups):
            start = (peer(place[0], j, n_groups) * halves + half) * size
            outs[half * n_groups + j][...] = rows[pl.ds(pl.multiple_of(start, SUB), size), :]


def mix_kernel(*refs):
    w_ref, g_ref, out = refs[-3:]
    n_groups, n, share, _ = out.shape
    atts, hids = refs[:-3 - n_groups], refs[-3 - n_groups:-3]
    width = w_ref.shape[0]
    rows = atts[0].shape[0]
    halves = share // rows

    def block(js):
        def start():
            x = [
                atts[half * n_groups + j][:, f * width:(f + 1) * width]
                for j in js
                for f in range(n)
                for half in range(halves)
            ]
            return contract(jnp.concatenate(x, axis=0), w_ref[...], 1, 0)

        def finish(normed):
            for i, j in enumerate(js):
                for f in range(n):
                    at = (i * n + f) * share
                    part = normed[at:at + share, :] * g_ref[...]
                    out[j, f] = (hids[j][f].astype(F32) + part).astype(BF)

        return start, finish

    add_normed([block(js) for js in blocks_of(n_groups, n * share)])


def blocks_of(n_groups, rows):
    size = max(1, min(n_groups, 2 * TILE // rows))
    return [range(at, min(at + size, n_groups)) for at in range(0, n_groups, size)]


def paired(chunks, lanes, frames):
    return chunks % 2 == 0 and frames % 2 == 0 and 2 * lanes == TILE


def slot(c, frame, chunks, n_groups, frames):
    return c ^ (frame & 1) if paired(chunks, n_groups * SUB, frames) else c


def project(w_ref, x, out):
    width = w_ref.shape[0] // 3
    cut = w_ref.shape[0] // 2
    heads = width // HEAD_DIM
    parts = [contract(w_ref[i * cut:(i + 1) * cut, :], x, 1, 1) for i in range(2)]
    for h in range(3 * heads):
        i, at = divmod(h * HEAD_DIM, cut)
        y = parts[i][at:at + HEAD_DIM, :]
        if h < 2 * heads:
            y = y * head_scale(y)
        pad = jnp.full((8, y.shape[1]), 0.0 if h < 2 * heads else 1.0, F32)
        out[sums(h), :] = jnp.concatenate([y, pad], axis=0).astype(BF)


def project_kernel(frame, frames, *refs):
    pieces, w_ref, out, x = refs[:-3], refs[-3], refs[-2], refs[-1]
    n_groups = len(pieces)
    chunks = pieces[0].shape[1] // SUB
    for c in range(chunks):
        for j, piece in enumerate(pieces):
            at = (slot(c, frame, chunks, n_groups, frames) * n_groups + j) * SUB
            x[at:at + SUB, :] = piece[0, c * SUB:(c + 1) * SUB, :]
    project(w_ref, x[...], out)


def late_project_kernel(frame, frames, *refs):
    n_groups = (len(refs) - 7) // 2
    atts, hids = refs[:n_groups], refs[n_groups:2 * n_groups]
    w_ref, g_ref, qkv_ref, out, a, b, x = refs[2 * n_groups:]
    width = w_ref.shape[0]
    n = hids[0].shape[0]
    rows = atts[0].shape[0]
    chunks = rows // SUB
    for f in range(n):
        for c in range(chunks):
            for j in range(n_groups):
                at = ((f * chunks + slot(c, frame + f, chunks, n_groups, frames)) * n_groups + j) * SUB
                piece = slice(c * SUB, (c + 1) * SUB)
                a[at:at + SUB, :] = atts[j][piece, f * width:(f + 1) * width]
                b[at:at + SUB, :] = hids[j][f, piece, :]

    def finish(normed):
        x[...] = (b[...].astype(F32) + normed * g_ref[...]).astype(BF)

    add_normed([(lambda: contract(a[...], w_ref[...], 1, 0), finish)])
    project(qkv_ref, x[...], out)


def temporal_kernel(n_groups, late, half, span, *refs):
    early_refs, late_ref = refs[:-n_groups - 2], refs[-n_groups - 2]
    outs, att = refs[-n_groups - 1:-1], refs[-1]
    early = len(early_refs)
    frames = early + late
    ins = [(ref, half * span) for ref in early_refs] + [(late_ref, f * span) for f in range(late)]
    lanes = n_groups * SUB
    chunks = span // lanes
    heads = late_ref.shape[0] // 3 // (HEAD_DIM + 8)
    width = heads * HEAD_DIM
    rows = frames * lanes
    pair = paired(chunks, lanes, frames)
    row_pos = lax.broadcasted_iota(jnp.int32, (rows, rows), 0) % SUB
    col_pos = lax.broadcasted_iota(jnp.int32, (rows, rows), 1) % SUB
    same = jnp.where(row_pos == col_pos, 1.0, 0.0).astype(BF)
    low = lax.broadcasted_iota(jnp.int32, (HEAD_DIM + 8, TILE), 1) < lanes

    def take(c, where):
        if not pair:
            return jnp.concatenate(
                [r[where, at + c * lanes:at + (c + 1) * lanes] for r, at in ins], axis=1
            )
        got = [r[where, at + c // 2 * TILE:at + (c // 2 + 1) * TILE] for r, at in ins]
        return jnp.concatenate(
            [
                jnp.where(low, got[m + (c & 1)], got[m + 1 - (c & 1)])
                for m in range(0, frames, 2)
            ],
            axis=1,
        )

    def scores(c, h):
        return contract(take(c, sums(heads + h)), take(c, sums(h)), 0, 0)

    def weigh(s):
        return jnp.exp2(s * EXP2_SCALE).astype(BF) * same

    def gather(c, h, p):
        att[c, head(h), :] = averaged(contract(take(c, sums(2 * heads + h)), p, 1, 0)).astype(BF)
        if h + 1 == heads:
            turn(c)

    def turn(c):
        turned = att[c].T
        for j, out in enumerate(outs):
            for f in range(frames):
                at = (f ^ (c & 1) if pair else f) * lanes + j * SUB
                out[c * SUB:(c + 1) * SUB, f * width:(f + 1) * width] = turned[at:at + SUB, :]

    steps = [(c, h) for c in range(chunks) for h in range(heads)]
    pipeline(steps, scores, weigh, gather)


def output_kernel(n_groups, js, early, half, halves, aliased, place, *refs):
    n = len(js)
    atts, pieces = refs[:n], refs[n:n * (1 + early)]
    late_ref, w_ref, g_ref = refs[n * (1 + early):n * (1 + early) + 3]
    out, buf, sems = refs[n * (1 + early) + 3 + aliased:]
    late = late_ref.shape[1]
    rows = atts[0].shape[0]
    cut = slice(half * rows, (half + 1) * rows)
    width = w_ref.shape[0]
    frames = early + late
    copies = []

    def block(some):
        def start():
            x = [atts[i][:, f * width:(f + 1) * width] for i in some for f in range(frames)]
            return contract(jnp.concatenate(x, axis=0), w_ref[...], 1, 0)

        def finish(normed):
            for k, i in enumerate(some):
                j = js[i]
                for f in range(frames):
                    mine = pieces[i * early + f][0, cut, :] if f < early else late_ref[j, f - early, cut, :]
                    at = (k * frames + f) * rows
                    part = normed[at:at + rows, :] * g_ref[...]
                    buf[i, f] = (mine.astype(F32) + part).astype(BF)
                group = peer(place[0], j, n_groups)
                at = pl.multiple_of((group * halves + half) * rows, SUB)
                copy = pltpu.make_async_copy(buf.at[i], out.at[:, pl.ds(at, rows), :], sems.at[i])
                copy.start()
                copies.append(copy)

        return start, finish

    add_normed([block(some) for some in blocks_of(len(js), frames * rows)])
    for copy in copies:
        copy.wait()


def shards(
    spatial_queries,
    spatial_keys,
    spatial_values,
    hidden,
    spatial_out_weight,
    spatial_gain,
    temporal_qkv_weight,
    temporal_out_weight,
    temporal_gain,
    tile_list,
    tile_count,
):
    frames, tokens, width = spatial_queries.shape
    model = hidden.shape[2]
    groups = lax.axis_size("frame")
    strips = lax.axis_size("strip")
    share = tokens // groups
    halves = 2 if share % (4 * SUB) == 0 else 1
    rows = share // halves
    queries = pltpu.with_memory_space_constraint(jnp.transpose(spatial_queries, (0, 2, 1)), pltpu.HBM)
    keys = pltpu.with_memory_space_constraint(jnp.transpose(spatial_keys, (0, 2, 1)), pltpu.HBM)
    values = pltpu.with_memory_space_constraint(jnp.transpose(spatial_values, (0, 2, 1)), pltpu.HBM)
    hidden_far = pltpu.with_memory_space_constraint(hidden, pltpu.HBM)
    lists = jnp.transpose(tile_list, (2, 1, 0))
    counts = tile_count.T
    qkv_weight = temporal_qkv_weight.T
    gain_one = spatial_gain.reshape(1, model)
    gain_two = temporal_gain.reshape(1, model)
    place = jnp.stack([lax.axis_index("frame"), lax.axis_index("strip")]).astype(jnp.int32)
    near = [(i, i ^ 1) for i in range(strips) if i ^ 1 < strips]
    far = [e for i in range(1, strips - 1, 2) for e in ((i, i + 1), (i + 1, i))]
    edge = jax.ShapeDtypeStruct((2 * width, TILE), BF)
    smem = pl.BlockSpec(memory_space=pltpu.SMEM)
    any_spec = pl.BlockSpec(memory_space=pl.ANY)

    def call(kernel, in_specs, out_specs, out_shape, scratch=(), limit=32, prefetch=0, alias=None):
        return pl.pallas_call(
            kernel,
            grid_spec=pltpu.PrefetchScalarGridSpec(
                num_scalar_prefetch=prefetch,
                grid=(1,),
                in_specs=in_specs,
                out_specs=out_specs,
                scratch_shapes=list(scratch),
            ),
            out_shape=out_shape,
            input_output_aliases=alias or {},
            compiler_params=vmem(limit),
        )

    late = frames // 2
    early = frames - late

    def out_pairs(j):
        return [(i, peer(i, j, groups)) for i in range(groups)]

    def send(parts):
        sent = {j: lax.ppermute(parts[j], "frame", out_pairs(j)) for j in reversed(range(1, groups))}
        return [parts[0]] + [sent[j] for j in range(1, groups)]

    halos = []
    for some in range(2):
        block = pl.BlockSpec((late, width, tokens), lambda *_, some=some: (some, 0, 0))
        split = groups if some == 1 else 0
        a, b, *pieces = call(
            prep_kernel,
            [smem, block, block] + [any_spec] * bool(split),
            [whole((late,) + edge.shape)] * 2 + [any_spec] * split,
            [jax.ShapeDtypeStruct((late,) + edge.shape, BF)] * 2
            + [jax.ShapeDtypeStruct((late, share, model), BF)] * split,
            [pltpu.SemaphoreType.DMA((groups,))] * bool(split),
            limit=16,
        )(place, keys, values, *[hidden_far] * bool(split))
        if split:
            own_hidden = pieces
        halos.append((a, b, lax.ppermute(a, "strip", near), lax.ppermute(b, "strip", far)))
    far_hidden = send(own_hidden)

    padded = width // HEAD_DIM * (HEAD_DIM + 8)
    qkv_rows = 3 * padded
    sum_shape = (late, padded, tokens)
    own_sums = []
    for some in range(2):
        block = pl.BlockSpec((late, width, tokens), lambda *_, some=some: (some, 0, 0))
        own_sums.append(
            call(
                functools.partial(local_kernel, some * late),
                [smem, smem, smem, block] + [whole((late,) + edge.shape)] * 2,
                [whole((late, width, tokens)), whole(sum_shape)],
                [
                    jax.ShapeDtypeStruct((late, width, tokens), BF),
                    jax.ShapeDtypeStruct(sum_shape, F32),
                ],
            )(place, counts, lists, queries, *halos[some][:2])
        )
    sum_specs = [whole((late, width, tokens)), whole(sum_shape)]

    def one(shape, f):
        return pl.BlockSpec((1,) + shape[1:], lambda *_: (f, 0, 0))

    mixed, projected = [], []
    for f in range(early):
        mixed.append(
            call(
                functools.partial(spatial_kernel, f, groups),
                [smem, smem, smem, one((late, width, tokens), f), one(sum_shape, f)]
                + [one((late,) + edge.shape, f)] * 2
                + [one(hidden.shape, f), whole((width, model)), whole((1, model))],
                [whole((1, share, model))] * groups,
                [jax.ShapeDtypeStruct((1, share, model), BF)] * groups,
                [
                    pltpu.VMEM((1, width, tokens), BF),
                    pltpu.VMEM((1, tokens, model), BF),
                ],
            )(place, counts, lists, *own_sums[0], *halos[0][2:], hidden, spatial_out_weight, gain_one)
        )
        arrived = send(mixed[f])
        projected.append(
            call(
                functools.partial(project_kernel, f, frames),
                [whole((1, share, model))] * groups + [whole((3 * width, model))],
                whole((qkv_rows, tokens)),
                jax.ShapeDtypeStruct((qkv_rows, tokens), BF),
                [pltpu.VMEM((tokens, model), BF)],
            )(*arrived, qkv_weight)
        )

    late_shape = (rows, late * width)
    own_late = call(
        functools.partial(late_kernel, early, groups, halves),
        [smem, smem, smem] + sum_specs + [whole((late,) + edge.shape)] * 2,
        [whole(late_shape)] * (groups * halves),
        [jax.ShapeDtypeStruct(late_shape, BF)] * (groups * halves),
        [pltpu.VMEM((late, width, tokens), BF), pltpu.VMEM((tokens, late * width), BF)],
    )(place, counts, lists, *own_sums[1], *halos[1][2:])
    own_late = [own_late[half * groups:(half + 1) * groups] for half in range(halves)]
    far_late = []
    for half in range(halves):
        far_late.append(send(own_late[half]))

    returned = []
    back_shape = (rows, frames * width)
    lanes = tokens // halves
    for half in range(halves):
        hid_block = pl.BlockSpec((late, rows, model), lambda *_, half=half: (0, half, 0))
        late_specs = [whole(late_shape)] * groups + [hid_block] * groups
        late_specs += [whole((width, model)), whole((1, model))]
        late_projected = call(
            functools.partial(late_project_kernel, early, frames),
            late_specs + [whole((3 * width, model))],
            whole((qkv_rows, late * lanes)),
            jax.ShapeDtypeStruct((qkv_rows, late * lanes), BF),
            [
                pltpu.VMEM((late * lanes, width), BF),
                pltpu.VMEM((late * lanes, model), BF),
                pltpu.VMEM((late * lanes, model), BF),
            ],
        )(*far_late[half], *far_hidden, spatial_out_weight, gain_one, qkv_weight)
        back = call(
            functools.partial(temporal_kernel, groups, late, half, lanes),
            [whole((qkv_rows, tokens))] * early + [whole((qkv_rows, late * lanes))],
            [whole(back_shape)] * groups,
            [jax.ShapeDtypeStruct(back_shape, BF)] * groups,
            [pltpu.VMEM((rows // SUB, width, groups * frames * SUB), BF)],
        )(*projected, late_projected)
        home = {
            j: lax.ppermute(back[j], "frame", [(b, a) for a, b in out_pairs(j)])
            for j in reversed(range(1, groups))
        }
        returned.append([back[0]] + [home[j] for j in range(1, groups)])

    late_mixed = call(
        mix_kernel,
        [whole(late_shape)] * (groups * halves)
        + [whole((late, share, model))] * groups
        + [whole((width, model)), whole((1, model))],
        whole((groups, late, share, model)),
        jax.ShapeDtypeStruct((groups, late, share, model), BF),
    )(*[x for some in own_late for x in some], *own_hidden, spatial_out_weight, gain_one)

    out = None
    for half in range(halves):
        cuts = [groups] if half + 1 < halves else [groups // 2, groups]
        for lo, hi in zip([0] + cuts, cuts):
            js = range(lo, hi)
            if not js:
                continue
            extra = [] if out is None else [out]
            out = call(
                functools.partial(output_kernel, groups, tuple(js), early, half, halves, len(extra)),
                [smem]
                + [whole(back_shape)] * len(js)
                + [whole((1, share, model))] * (len(js) * early)
                + [whole((groups, late, share, model))]
                + [whole((width, model)), whole((1, model))]
                + [any_spec] * len(extra),
                any_spec,
                jax.ShapeDtypeStruct((frames, tokens, model), BF),
                [
                    pltpu.VMEM((len(js), frames, rows, model), BF),
                    pltpu.SemaphoreType.DMA((len(js),)),
                ],
                alias={4 + len(js) * (1 + early): 0} if extra else None,
            )(
                place,
                *[returned[half][j] for j in js],
                *[mixed[f][j] for j in js for f in range(early)],
                late_mixed,
                temporal_out_weight,
                gain_two,
                *extra,
            )
    return out


def solution(mesh):
    rows = P(("group", "frame"), "strip", None)
    placed = (rows, rows, rows, rows, P(), P(), P(), P(), P(), rows, P(("group", "frame"), "strip"))

    return jax.shard_map(shards, mesh=mesh, in_specs=placed, out_specs=rows, check_vma=False)
```

```python
import functools
import math

import jax
import jax.numpy as jnp
from jax import lax
from jax.experimental import pallas as pl
from jax.experimental.pallas import tpu as pltpu
from jax.sharding import PartitionSpec as P


HEAD_DIM = 72
TILE = 128
MAXT = 3
SUB = 16
EPS = 1e-06
EXP2_SCALE = HEAD_DIM ** -0.5 * math.log2(math.e)

BF = jnp.bfloat16
F32 = jnp.float32


def peer(i, j, n):
    return i ^ j if n & (n - 1) == 0 else (i + j) % n


def vmem(limit):
    return pltpu.CompilerParams(vmem_limit_bytes=limit << 20)


def whole(shape):
    return pl.BlockSpec(shape, lambda *_: (0,) * len(shape))


def contract(a, b, da, db):
    return lax.dot_general(a, b, (((da,), (db,)), ((), ())), preferred_element_type=F32)


def head_scale(x):
    return lax.rsqrt(jnp.mean(x * x, axis=0, keepdims=True) + EPS)


def head(h, base=0):
    return slice(base + h * HEAD_DIM, base + (h + 1) * HEAD_DIM)


def with_ones(v):
    return jnp.concatenate([v, jnp.ones((8, v.shape[1]), v.dtype)], axis=0)


def averaged(o):
    return o[:HEAD_DIM, :] / o[HEAD_DIM:HEAD_DIM + 1, :]


def pipeline(steps, scores, weigh, gather):
    ahead, behind = scores(*steps[0]), None
    for n, step in enumerate(steps):
        now = ahead
        if n + 1 < len(steps):
            ahead = scores(*steps[n + 1])
        weighed = weigh(now)
        if behind is not None:
            gather(*steps[n - 1], behind)
        behind = weighed
    gather(*steps[-1], behind)


def prep_kernel(place, k_ref, v_ref, *refs):
    n, width, _ = k_ref.shape
    even = place[1] % 2 == 0
    copies = []
    if len(refs) > 2:
        src, (a_ref, b_ref), pieces, sems = refs[0], refs[1:3], refs[3:-1], refs[-1]
        late, share, _ = pieces[0].shape
        for j in reversed(range(len(pieces))):
            start = pl.multiple_of(peer(place[0], j, len(pieces)) * share, SUB)
            part = src.at[pl.ds(src.shape[0] - late, late), pl.ds(start, share), :]
            copies.append(pltpu.make_async_copy(part, pieces[j], sems.at[j]))
            copies[-1].start()
    else:
        a_ref, b_ref = refs

    def fill(first, second):
        for f in range(n):
            for h in range(width // HEAD_DIM):
                x = k_ref[f, head(h), :].astype(F32)
                y = (x * head_scale(x)).astype(BF)
                first[f, head(h), :] = y[:, :TILE]
                second[f, head(h), :] = y[:, TILE:]
            first[f, width:, :] = v_ref[f, :, :TILE]
            second[f, width:, :] = v_ref[f, :, TILE:]

    pl.when(even)(functools.partial(fill, b_ref, a_ref))
    pl.when(jnp.logical_not(even))(functools.partial(fill, a_ref, b_ref))
    for copy in copies:
        copy.wait()


def tile_masks(frame, n, tiles, local, place, counts, lists):
    strip = place[1]
    odd = strip % 2
    first = strip * tiles
    if local:
        spots = (first + 1 - odd, first + odd)
    else:
        spots = (first + 2 - 3 * odd, first - 1 + 3 * odd)
    masks = []
    for f in range(n):
        rows = []
        for spot in spots:
            cells = []
            for t in range(tiles):
                hit = jnp.bool_(False)
                for j in range(MAXT):
                    hit = hit | ((lists[j, t, frame + f] == spot) & (j < counts[t, frame + f]))
                cells.append(jnp.full((SUB, TILE), jnp.where(hit, 1.0, 0.0), F32))
            rows.append(jnp.concatenate(cells, axis=1).astype(BF))
        masks.append(rows)
    return masks


def attend(masks, keys, query, finish):
    n = keys[0].shape[0]
    width = keys[0].shape[1] // 2

    def scores(f, h):
        qn = query(f, h)
        return f, [contract(ref[f, head(h), :], qn, 0, 0) for ref in keys]

    def weigh(scored):
        f, s = scored
        packed = []
        for mask, x in zip(masks[f], s):
            p = jnp.exp2(x * EXP2_SCALE).astype(BF).reshape(TILE // SUB, SUB, x.shape[1])
            packed.append((p * mask).reshape(x.shape))
        return jnp.concatenate(packed, axis=0)

    def gather(f, h, weights):
        v = jnp.concatenate([ref[f, head(h, width), :] for ref in keys], axis=1)
        finish(f, h, contract(with_ones(v), weights, 1, 0))

    pipeline([(f, h) for f in range(n) for h in range(width // HEAD_DIM)], scores, weigh, gather)


def sums(h):
    return slice(h * (HEAD_DIM + 8), (h + 1) * (HEAD_DIM + 8))


def local_kernel(frame, place, counts, lists, q_ref, a_ref, b_ref, qn_ref, sum_ref):
    n, _, tokens = q_ref.shape

    def query(f, h):
        q = q_ref[f, head(h), :].astype(F32)
        qn = (q * head_scale(q)).astype(BF)
        qn_ref[f, head(h), :] = qn
        return qn

    def finish(f, h, o):
        sum_ref[f, sums(h), :] = o

    masks = tile_masks(frame, n, tokens // TILE, True, place, counts, lists)
    attend(masks, (a_ref, b_ref), query, finish)


def remote_attend(frame, place, counts, lists, qn_ref, sum_ref, ra_ref, rb_ref, att, done=None):
    n, width, tokens = qn_ref.shape

    def query(f, h):
        return qn_ref[f, head(h), :]

    def finish(f, h, o):
        att[f, head(h), :] = averaged(o + sum_ref[f, sums(h), :]).astype(att.dtype)
        if done and (h + 1) * HEAD_DIM == width:
            done(f)

    masks = tile_masks(frame, n, tokens // TILE, False, place, counts, lists)
    attend(masks, (ra_ref, rb_ref), query, finish)


def add_normed(blocks):
    ahead = blocks[0][0]()
    for n, (_, finish) in enumerate(blocks):
        proj = ahead
        if n + 1 < len(blocks):
            ahead = blocks[n + 1][0]()
        scale = lax.rsqrt(jnp.mean(proj * proj, axis=-1, keepdims=True) + EPS)
        finish(proj * scale)


def spatial_kernel(frame, n_groups, place, counts, lists, qn_ref, sum_ref, ra_ref, rb_ref, h_ref, w_ref, g_ref, *rest):
    outs, (att, mix) = rest[:n_groups], rest[n_groups:]
    remote_attend(frame, place, counts, lists, qn_ref, sum_ref, ra_ref, rb_ref, att)
    n, tokens, _ = h_ref.shape

    def block(f):
        def finish(normed):
            mix[f] = (h_ref[f].astype(F32) + normed * g_ref[...]).astype(BF)

        return lambda: contract(att[f], w_ref[...], 0, 0), finish

    add_normed([block(f) for f in range(n)])
    share = tokens // n_groups
    for j, out in enumerate(outs):
        group = peer(place[0], j, n_groups)
        for f in range(n):
            out[f] = mix[f, pl.ds(pl.multiple_of(group * share, SUB), share), :]


def late_kernel(frame, n_groups, halves, place, counts, lists, qn_ref, sum_ref, ra_ref, rb_ref, *rest):
    outs, (att, rows) = rest[:n_groups * halves], rest[n_groups * halves:]
    _, width, tokens = qn_ref.shape

    def turn(f):
        rows[:, f * width:(f + 1) * width] = att[f].T

    remote_attend(frame, place, counts, lists, qn_ref, sum_ref, ra_ref, rb_ref, att, turn)
    size = tokens // n_groups // halves
    for half in range(halves):
        for j in range(n_groups):
            start = (peer(place[0], j, n_groups) * halves + half) * size
            outs[half * n_groups + j][...] = rows[pl.ds(pl.multiple_of(start, SUB), size), :]


def mix_kernel(*refs):
    w_ref, g_ref, out = refs[-3:]
    n_groups, n, share, _ = out.shape
    atts, hids = refs[:-3 - n_groups], refs[-3 - n_groups:-3]
    width = w_ref.shape[0]
    rows = atts[0].shape[0]
    halves = share // rows

    def block(js):
        def start():
            x = [
                atts[half * n_groups + j][:, f * width:(f + 1) * width]
                for j in js
                for f in range(n)
                for half in range(halves)
            ]
            return contract(jnp.concatenate(x, axis=0), w_ref[...], 1, 0)

        def finish(normed):
            for i, j in enumerate(js):
                for f in range(n):
                    at = (i * n + f) * share
                    part = normed[at:at + share, :] * g_ref[...]
                    out[j, f] = (hids[j][f].astype(F32) + part).astype(BF)

        return start, finish

    add_normed([block(js) for js in blocks_of(n_groups, n * share)])


def blocks_of(n_groups, rows):
    size = max(1, min(n_groups, 2 * TILE // rows))
    return [range(at, min(at + size, n_groups)) for at in range(0, n_groups, size)]


def paired(chunks, lanes, frames):
    return chunks % 2 == 0 and frames % 2 == 0 and 2 * lanes == TILE


def slot(c, frame, chunks, n_groups, frames):
    return c ^ (frame & 1) if paired(chunks, n_groups * SUB, frames) else c


def project(w_ref, x, out):
    width = w_ref.shape[0] // 3
    cut = w_ref.shape[0] // 2
    heads = width // HEAD_DIM
    parts = [contract(w_ref[i * cut:(i + 1) * cut, :], x, 1, 1) for i in range(2)]
    for h in range(3 * heads):
        i, at = divmod(h * HEAD_DIM, cut)
        y = parts[i][at:at + HEAD_DIM, :]
        if h < 2 * heads:
            y = y * head_scale(y)
        pad = jnp.full((8, y.shape[1]), 0.0 if h < 2 * heads else 1.0, F32)
        out[sums(h), :] = jnp.concatenate([y, pad], axis=0).astype(BF)


def project_kernel(frame, frames, *refs):
    pieces, w_ref, out, x = refs[:-3], refs[-3], refs[-2], refs[-1]
    n_groups = len(pieces)
    chunks = pieces[0].shape[1] // SUB
    for c in range(chunks):
        for j, piece in enumerate(pieces):
            at = (slot(c, frame, chunks, n_groups, frames) * n_groups + j) * SUB
            x[at:at + SUB, :] = piece[0, c * SUB:(c + 1) * SUB, :]
    project(w_ref, x[...], out)


def late_project_kernel(frame, frames, *refs):
    n_groups = (len(refs) - 7) // 2
    atts, hids = refs[:n_groups], refs[n_groups:2 * n_groups]
    w_ref, g_ref, qkv_ref, out, a, b, x = refs[2 * n_groups:]
    width = w_ref.shape[0]
    n = hids[0].shape[0]
    rows = atts[0].shape[0]
    chunks = rows // SUB
    for f in range(n):
        for c in range(chunks):
            for j in range(n_groups):
                at = ((f * chunks + slot(c, frame + f, chunks, n_groups, frames)) * n_groups + j) * SUB
                piece = slice(c * SUB, (c + 1) * SUB)
                a[at:at + SUB, :] = atts[j][piece, f * width:(f + 1) * width]
                b[at:at + SUB, :] = hids[j][f, piece, :]

    def finish(normed):
        x[...] = (b[...].astype(F32) + normed * g_ref[...]).astype(BF)

    add_normed([(lambda: contract(a[...], w_ref[...], 1, 0), finish)])
    project(qkv_ref, x[...], out)


def temporal_kernel(n_groups, late, half, span, *refs):
    early_refs, late_ref = refs[:-n_groups - 2], refs[-n_groups - 2]
    outs, att = refs[-n_groups - 1:-1], refs[-1]
    early = len(early_refs)
    frames = early + late
    ins = [(ref, half * span) for ref in early_refs] + [(late_ref, f * span) for f in range(late)]
    lanes = n_groups * SUB
    chunks = span // lanes
    heads = late_ref.shape[0] // 3 // (HEAD_DIM + 8)
    width = heads * HEAD_DIM
    rows = frames * lanes
    pair = paired(chunks, lanes, frames)
    row_pos = lax.broadcasted_iota(jnp.int32, (rows, rows), 0) % SUB
    col_pos = lax.broadcasted_iota(jnp.int32, (rows, rows), 1) % SUB
    same = jnp.where(row_pos == col_pos, 1.0, 0.0).astype(BF)
    low = lax.broadcasted_iota(jnp.int32, (HEAD_DIM + 8, TILE), 1) < lanes

    def take(c, where):
        if not pair:
            return jnp.concatenate(
                [r[where, at + c * lanes:at + (c + 1) * lanes] for r, at in ins], axis=1
            )
        got = [r[where, at + c // 2 * TILE:at + (c // 2 + 1) * TILE] for r, at in ins]
        return jnp.concatenate(
            [
                jnp.where(low, got[m + (c & 1)], got[m + 1 - (c & 1)])
                for m in range(0, frames, 2)
            ],
            axis=1,
        )

    def scores(c, h):
        return contract(take(c, sums(heads + h)), take(c, sums(h)), 0, 0)

    def weigh(s):
        return jnp.exp2(s * EXP2_SCALE).astype(BF) * same

    def gather(c, h, p):
        att[c, head(h), :] = averaged(contract(take(c, sums(2 * heads + h)), p, 1, 0)).astype(BF)
        if h + 1 == heads:
            turn(c)

    def turn(c):
        turned = att[c].T
        for j, out in enumerate(outs):
            for f in range(frames):
                at = (f ^ (c & 1) if pair else f) * lanes + j * SUB
                out[c * SUB:(c + 1) * SUB, f * width:(f + 1) * width] = turned[at:at + SUB, :]

    steps = [(c, h) for c in range(chunks) for h in range(heads)]
    pipeline(steps, scores, weigh, gather)


def output_kernel(n_groups, js, early, half, halves, before, last, aliased, place, *refs):
    n = len(js)
    atts, pieces = refs[:n], refs[n:n * (1 + early)]
    late_ref, w_ref, g_ref = refs[n * (1 + early):n * (1 + early) + 3]
    rest = list(refs[n * (1 + early) + 3:])
    handed = rest.pop(0) if before else None
    rest = rest[aliased:]
    out = rest.pop(0) if before or last else None
    buf = rest.pop(0)
    late = late_ref.shape[1]
    rows = atts[0].shape[0]
    cut = slice(half * rows, (half + 1) * rows)
    width = w_ref.shape[0]
    frames = early + late
    copies = []

    def write(src, j, some_half):
        group = peer(place[0], j, n_groups)
        at = pl.multiple_of((group * halves + some_half) * rows, SUB)
        copy = pltpu.make_async_copy(src, out.at[:, pl.ds(at, rows), :], rest[0].at[len(copies)])
        copy.start()
        copies.append(copy)

    if before:
        for i, j in enumerate(before[0]):
            write(handed.at[i], j, before[1])

    def block(some):
        def start():
            x = [atts[i][:, f * width:(f + 1) * width] for i in some for f in range(frames)]
            return contract(jnp.concatenate(x, axis=0), w_ref[...], 1, 0)

        def finish(normed):
            for k, i in enumerate(some):
                j = js[i]
                for f in range(frames):
                    mine = pieces[i * early + f][0, cut, :] if f < early else late_ref[j, f - early, cut, :]
                    at = (k * frames + f) * rows
                    part = normed[at:at + rows, :] * g_ref[...]
                    buf[i, f] = (mine.astype(F32) + part).astype(BF)
                if last:
                    write(buf.at[i], j, half)

        return start, finish

    add_normed([block(some) for some in blocks_of(n, frames * rows)])
    for copy in copies:
        copy.wait()


def shards(
    spatial_queries,
    spatial_keys,
    spatial_values,
    hidden,
    spatial_out_weight,
    spatial_gain,
    temporal_qkv_weight,
    temporal_out_weight,
    temporal_gain,
    tile_list,
    tile_count,
):
    frames, tokens, width = spatial_queries.shape
    model = hidden.shape[2]
    groups = lax.axis_size("frame")
    strips = lax.axis_size("strip")
    share = tokens // groups
    halves = 2 if share % (4 * SUB) == 0 else 1
    rows = share // halves
    queries = pltpu.with_memory_space_constraint(jnp.transpose(spatial_queries, (0, 2, 1)), pltpu.HBM)
    keys = pltpu.with_memory_space_constraint(jnp.transpose(spatial_keys, (0, 2, 1)), pltpu.HBM)
    values = pltpu.with_memory_space_constraint(jnp.transpose(spatial_values, (0, 2, 1)), pltpu.HBM)
    hidden_far = pltpu.with_memory_space_constraint(hidden, pltpu.HBM)
    lists = jnp.transpose(tile_list, (2, 1, 0))
    counts = tile_count.T
    qkv_weight = temporal_qkv_weight.T
    gain_one = spatial_gain.reshape(1, model)
    gain_two = temporal_gain.reshape(1, model)
    place = jnp.stack([lax.axis_index("frame"), lax.axis_index("strip")]).astype(jnp.int32)
    near = [(i, i ^ 1) for i in range(strips) if i ^ 1 < strips]
    far = [e for i in range(1, strips - 1, 2) for e in ((i, i + 1), (i + 1, i))]
    edge = jax.ShapeDtypeStruct((2 * width, TILE), BF)
    smem = pl.BlockSpec(memory_space=pltpu.SMEM)
    any_spec = pl.BlockSpec(memory_space=pl.ANY)

    def call(kernel, in_specs, out_specs, out_shape, scratch=(), limit=32, prefetch=0, alias=None):
        return pl.pallas_call(
            kernel,
            grid_spec=pltpu.PrefetchScalarGridSpec(
                num_scalar_prefetch=prefetch,
                grid=(1,),
                in_specs=in_specs,
                out_specs=out_specs,
                scratch_shapes=list(scratch),
            ),
            out_shape=out_shape,
            input_output_aliases=alias or {},
            compiler_params=vmem(limit),
        )

    late = frames // 2
    early = frames - late

    def out_pairs(j):
        return [(i, peer(i, j, groups)) for i in range(groups)]

    def send(parts):
        sent = {j: lax.ppermute(parts[j], "frame", out_pairs(j)) for j in reversed(range(1, groups))}
        return [parts[0]] + [sent[j] for j in range(1, groups)]

    halos = []
    for some in range(2):
        block = pl.BlockSpec((late, width, tokens), lambda *_, some=some: (some, 0, 0))
        split = groups if some == 1 else 0
        a, b, *pieces = call(
            prep_kernel,
            [smem, block, block] + [any_spec] * bool(split),
            [whole((late,) + edge.shape)] * 2 + [any_spec] * split,
            [jax.ShapeDtypeStruct((late,) + edge.shape, BF)] * 2
            + [jax.ShapeDtypeStruct((late, share, model), BF)] * split,
            [pltpu.SemaphoreType.DMA((groups,))] * bool(split),
            limit=16,
        )(place, keys, values, *[hidden_far] * bool(split))
        if split:
            own_hidden = pieces
        halos.append((a, b, lax.ppermute(a, "strip", near), lax.ppermute(b, "strip", far)))
    far_hidden = send(own_hidden)

    padded = width // HEAD_DIM * (HEAD_DIM + 8)
    qkv_rows = 3 * padded
    sum_shape = (late, padded, tokens)
    own_sums = []
    for some in range(2):
        block = pl.BlockSpec((late, width, tokens), lambda *_, some=some: (some, 0, 0))
        own_sums.append(
            call(
                functools.partial(local_kernel, some * late),
                [smem, smem, smem, block] + [whole((late,) + edge.shape)] * 2,
                [whole((late, width, tokens)), whole(sum_shape)],
                [
                    jax.ShapeDtypeStruct((late, width, tokens), BF),
                    jax.ShapeDtypeStruct(sum_shape, F32),
                ],
            )(place, counts, lists, queries, *halos[some][:2])
        )
    sum_specs = [whole((late, width, tokens)), whole(sum_shape)]

    def one(shape, f):
        return pl.BlockSpec((1,) + shape[1:], lambda *_: (f, 0, 0))

    mixed, projected = [], []
    for f in range(early):
        mixed.append(
            call(
                functools.partial(spatial_kernel, f, groups),
                [smem, smem, smem, one((late, width, tokens), f), one(sum_shape, f)]
                + [one((late,) + edge.shape, f)] * 2
                + [one(hidden.shape, f), whole((width, model)), whole((1, model))],
                [whole((1, share, model))] * groups,
                [jax.ShapeDtypeStruct((1, share, model), BF)] * groups,
                [
                    pltpu.VMEM((1, width, tokens), BF),
                    pltpu.VMEM((1, tokens, model), BF),
                ],
            )(place, counts, lists, *own_sums[0], *halos[0][2:], hidden, spatial_out_weight, gain_one)
        )
        arrived = send(mixed[f])
        projected.append(
            call(
                functools.partial(project_kernel, f, frames),
                [whole((1, share, model))] * groups + [whole((3 * width, model))],
                whole((qkv_rows, tokens)),
                jax.ShapeDtypeStruct((qkv_rows, tokens), BF),
                [pltpu.VMEM((tokens, model), BF)],
            )(*arrived, qkv_weight)
        )

    late_shape = (rows, late * width)
    own_late = call(
        functools.partial(late_kernel, early, groups, halves),
        [smem, smem, smem] + sum_specs + [whole((late,) + edge.shape)] * 2,
        [whole(late_shape)] * (groups * halves),
        [jax.ShapeDtypeStruct(late_shape, BF)] * (groups * halves),
        [pltpu.VMEM((late, width, tokens), BF), pltpu.VMEM((tokens, late * width), BF)],
    )(place, counts, lists, *own_sums[1], *halos[1][2:])
    own_late = [own_late[half * groups:(half + 1) * groups] for half in range(halves)]
    far_late = []
    for half in range(halves):
        far_late.append(send(own_late[half]))

    returned = []
    back_shape = (rows, frames * width)
    lanes = tokens // halves
    for half in range(halves):
        hid_block = pl.BlockSpec((late, rows, model), lambda *_, half=half: (0, half, 0))
        late_specs = [whole(late_shape)] * groups + [hid_block] * groups
        late_specs += [whole((width, model)), whole((1, model))]
        late_projected = call(
            functools.partial(late_project_kernel, early, frames),
            late_specs + [whole((3 * width, model))],
            whole((qkv_rows, late * lanes)),
            jax.ShapeDtypeStruct((qkv_rows, late * lanes), BF),
            [
                pltpu.VMEM((late * lanes, width), BF),
                pltpu.VMEM((late * lanes, model), BF),
                pltpu.VMEM((late * lanes, model), BF),
            ],
        )(*far_late[half], *far_hidden, spatial_out_weight, gain_one, qkv_weight)
        back = call(
            functools.partial(temporal_kernel, groups, late, half, lanes),
            [whole((qkv_rows, tokens))] * early + [whole((qkv_rows, late * lanes))],
            [whole(back_shape)] * groups,
            [jax.ShapeDtypeStruct(back_shape, BF)] * groups,
            [pltpu.VMEM((rows // SUB, width, groups * frames * SUB), BF)],
        )(*projected, late_projected)
        home = {
            j: lax.ppermute(back[j], "frame", [(b, a) for a, b in out_pairs(j)])
            for j in reversed(range(1, groups))
        }
        returned.append([back[0]] + [home[j] for j in range(1, groups)])

    late_mixed = call(
        mix_kernel,
        [whole(late_shape)] * (groups * halves)
        + [whole((late, share, model))] * groups
        + [whole((width, model)), whole((1, model))],
        whole((groups, late, share, model)),
        jax.ShapeDtypeStruct((groups, late, share, model), BF),
    )(*[x for some in own_late for x in some], *own_hidden, spatial_out_weight, gain_one)

    order = [0, 1] + list(reversed(range(2, groups))) if groups > 1 else [0]
    tail = max(1, groups // 4)
    calls = [(tuple(order), half) for half in range(halves - 1)]
    calls += [(tuple(js), halves - 1) for js in (order[:-tail], order[-tail:]) if js]
    result = jax.ShapeDtypeStruct((frames, tokens, model), BF)
    out = handed = before = None
    for n, (js, half) in enumerate(calls):
        last = n + 1 == len(calls)
        rows_shape = (len(js), frames, rows, model)
        extra = [] if out is None else [out]
        writes = (len(before[0]) if before else 0) + (len(js) if last else 0)
        in_specs = (
            [smem]
            + [whole(back_shape)] * len(js)
            + [whole((1, share, model))] * (len(js) * early)
            + [whole((groups, late, share, model)), whole((width, model)), whole((1, model))]
            + ([whole(handed.shape)] if before else [])
            + [any_spec] * len(extra)
        )
        outs = ([any_spec], [result]) if before or last else ([], [])
        kept = ([], []) if last else ([whole(rows_shape)], [jax.ShapeDtypeStruct(rows_shape, BF)])
        scratch = [pltpu.VMEM(rows_shape, BF)] * last + [pltpu.SemaphoreType.DMA((writes,))] * bool(writes)
        got = call(
            functools.partial(output_kernel, groups, js, early, half, halves, before, last, len(extra)),
            in_specs,
            outs[0] + kept[0],
            outs[1] + kept[1],
            scratch,
            alias={len(in_specs) - 1: 0} if extra else None,
        )(
            place,
            *[returned[half][j] for j in js],
            *[mixed[f][j] for j in js for f in range(early)],
            late_mixed,
            temporal_out_weight,
            gain_two,
            *([handed] if before else []),
            *extra,
        )
        got = list(got)
        out = got.pop(0) if before or last else None
        handed = None if last else got[0]
        before = (js, half)
    return out


def solution(mesh):
    rows = P(("group", "frame"), "strip", None)
    placed = (rows, rows, rows, rows, P(), P(), P(), P(), P(), rows, P(("group", "frame"), "strip"))

    return jax.shard_map(shards, mesh=mesh, in_specs=placed, out_specs=rows, check_vma=False)
```

```python
import functools
import math

import jax
import jax.numpy as jnp
from jax import lax
from jax.experimental import pallas as pl
from jax.experimental.pallas import tpu as pltpu
from jax.sharding import PartitionSpec as P


HEAD_DIM = 72
TILE = 128
MAXT = 3
SUB = 16
EPS = 1e-06
EXP2_SCALE = HEAD_DIM ** -0.5 * math.log2(math.e)

BF = jnp.bfloat16
F32 = jnp.float32


def peer(i, j, n):
    return i ^ j if n & (n - 1) == 0 else (i + j) % n


def vmem(limit):
    return pltpu.CompilerParams(vmem_limit_bytes=limit << 20)


def whole(shape):
    return pl.BlockSpec(shape, lambda *_: (0,) * len(shape))


def contract(a, b, da, db):
    return lax.dot_general(a, b, (((da,), (db,)), ((), ())), preferred_element_type=F32)


def head_scale(x):
    return lax.rsqrt(jnp.mean(x * x, axis=0, keepdims=True) + EPS)


def head(h, base=0):
    return slice(base + h * HEAD_DIM, base + (h + 1) * HEAD_DIM)


def with_ones(v):
    return jnp.concatenate([v, jnp.ones((8, v.shape[1]), v.dtype)], axis=0)


def averaged(o):
    return o[:HEAD_DIM, :] / o[HEAD_DIM:HEAD_DIM + 1, :]


def pipeline(steps, scores, weigh, gather):
    ahead, behind = scores(*steps[0]), None
    for n, step in enumerate(steps):
        now = ahead
        if n + 1 < len(steps):
            ahead = scores(*steps[n + 1])
        weighed = weigh(now)
        if behind is not None:
            gather(*steps[n - 1], behind)
        behind = weighed
    gather(*steps[-1], behind)


def prep_kernel(place, k_ref, v_ref, *refs):
    n, width, _ = k_ref.shape
    even = place[1] % 2 == 0
    copies = []
    if len(refs) > 2:
        src, (a_ref, b_ref), pieces, sems = refs[0], refs[1:3], refs[3:-1], refs[-1]
        late, share, _ = pieces[0].shape
        for j in reversed(range(len(pieces))):
            start = pl.multiple_of(peer(place[0], j, len(pieces)) * share, SUB)
            part = src.at[pl.ds(src.shape[0] - late, late), pl.ds(start, share), :]
            copies.append(pltpu.make_async_copy(part, pieces[j], sems.at[j]))
            copies[-1].start()
    else:
        a_ref, b_ref = refs

    def fill(first, second):
        for f in range(n):
            for h in range(width // HEAD_DIM):
                x = k_ref[f, head(h), :].astype(F32)
                y = (x * head_scale(x)).astype(BF)
                first[f, head(h), :] = y[:, :TILE]
                second[f, head(h), :] = y[:, TILE:]
            first[f, width:, :] = v_ref[f, :, :TILE]
            second[f, width:, :] = v_ref[f, :, TILE:]

    pl.when(even)(functools.partial(fill, b_ref, a_ref))
    pl.when(jnp.logical_not(even))(functools.partial(fill, a_ref, b_ref))
    for copy in copies:
        copy.wait()


def tile_masks(frame, n, tiles, local, place, counts, lists):
    strip = place[1]
    odd = strip % 2
    first = strip * tiles
    if local:
        spots = (first + 1 - odd, first + odd)
    else:
        spots = (first + 2 - 3 * odd, first - 1 + 3 * odd)
    masks = []
    for f in range(n):
        rows = []
        for spot in spots:
            cells = []
            for t in range(tiles):
                hit = jnp.bool_(False)
                for j in range(MAXT):
                    hit = hit | ((lists[j, t, frame + f] == spot) & (j < counts[t, frame + f]))
                cells.append(jnp.full((SUB, TILE), jnp.where(hit, 1.0, 0.0), F32))
            rows.append(jnp.concatenate(cells, axis=1).astype(BF))
        masks.append(rows)
    return masks


def attend(masks, keys, query, finish):
    n = keys[0].shape[0]
    width = keys[0].shape[1] // 2

    def scores(f, h):
        qn = query(f, h)
        return f, [contract(ref[f, head(h), :], qn, 0, 0) for ref in keys]

    def weigh(scored):
        f, s = scored
        packed = []
        for mask, x in zip(masks[f], s):
            p = jnp.exp2(x * EXP2_SCALE).astype(BF).reshape(TILE // SUB, SUB, x.shape[1])
            packed.append((p * mask).reshape(x.shape))
        return jnp.concatenate(packed, axis=0)

    def gather(f, h, weights):
        v = jnp.concatenate([ref[f, head(h, width), :] for ref in keys], axis=1)
        finish(f, h, contract(with_ones(v), weights, 1, 0))

    pipeline([(f, h) for f in range(n) for h in range(width // HEAD_DIM)], scores, weigh, gather)


def sums(h):
    return slice(h * (HEAD_DIM + 8), (h + 1) * (HEAD_DIM + 8))


def local_kernel(frame, place, counts, lists, q_ref, a_ref, b_ref, qn_ref, sum_ref):
    n, _, tokens = q_ref.shape

    def query(f, h):
        q = q_ref[f, head(h), :].astype(F32)
        qn = (q * head_scale(q)).astype(BF)
        qn_ref[f, head(h), :] = qn
        return qn

    def finish(f, h, o):
        sum_ref[f, sums(h), :] = o

    masks = tile_masks(frame, n, tokens // TILE, True, place, counts, lists)
    attend(masks, (a_ref, b_ref), query, finish)


def remote_attend(frame, place, counts, lists, qn_ref, sum_ref, ra_ref, rb_ref, att, done=None):
    n, width, tokens = qn_ref.shape

    def query(f, h):
        return qn_ref[f, head(h), :]

    def finish(f, h, o):
        att[f, head(h), :] = averaged(o + sum_ref[f, sums(h), :]).astype(att.dtype)
        if done and (h + 1) * HEAD_DIM == width:
            done(f)

    masks = tile_masks(frame, n, tokens // TILE, False, place, counts, lists)
    attend(masks, (ra_ref, rb_ref), query, finish)


def add_normed(blocks):
    ahead = blocks[0][0]()
    for n, (_, finish) in enumerate(blocks):
        proj = ahead
        if n + 1 < len(blocks):
            ahead = blocks[n + 1][0]()
        scale = lax.rsqrt(jnp.mean(proj * proj, axis=-1, keepdims=True) + EPS)
        finish(proj * scale)


def spatial_kernel(frame, n_groups, place, counts, lists, qn_ref, sum_ref, ra_ref, rb_ref, h_ref, w_ref, g_ref, *rest):
    outs, (att, mix) = rest[:n_groups], rest[n_groups:]
    remote_attend(frame, place, counts, lists, qn_ref, sum_ref, ra_ref, rb_ref, att)
    n, tokens, _ = h_ref.shape

    def block(f):
        def finish(normed):
            mix[f] = (h_ref[f].astype(F32) + normed * g_ref[...]).astype(BF)

        return lambda: contract(att[f], w_ref[...], 0, 0), finish

    add_normed([block(f) for f in range(n)])
    share = tokens // n_groups
    for j, out in enumerate(outs):
        group = peer(place[0], j, n_groups)
        for f in range(n):
            out[f] = mix[f, pl.ds(pl.multiple_of(group * share, SUB), share), :]


def late_kernel(frame, n_groups, halves, place, counts, lists, qn_ref, sum_ref, ra_ref, rb_ref, *rest):
    outs, (att, rows) = rest[:n_groups * halves], rest[n_groups * halves:]
    _, width, tokens = qn_ref.shape

    def turn(f):
        rows[:, f * width:(f + 1) * width] = att[f].T

    remote_attend(frame, place, counts, lists, qn_ref, sum_ref, ra_ref, rb_ref, att, turn)
    size = tokens // n_groups // halves
    for half in range(halves):
        for j in range(n_groups):
            start = (peer(place[0], j, n_groups) * halves + half) * size
            outs[half * n_groups + j][...] = rows[pl.ds(pl.multiple_of(start, SUB), size), :]


def mix_kernel(*refs):
    w_ref, g_ref, out = refs[-3:]
    n_groups, n, share, _ = out.shape
    atts, hids = refs[:-3 - n_groups], refs[-3 - n_groups:-3]
    width = w_ref.shape[0]
    rows = atts[0].shape[0]
    halves = share // rows

    def block(js):
        def start():
            x = [
                atts[half * n_groups + j][:, f * width:(f + 1) * width]
                for j in js
                for f in range(n)
                for half in range(halves)
            ]
            return contract(jnp.concatenate(x, axis=0), w_ref[...], 1, 0)

        def finish(normed):
            for i, j in enumerate(js):
                for f in range(n):
                    at = (i * n + f) * share
                    part = normed[at:at + share, :] * g_ref[...]
                    out[j, f] = (hids[j][f].astype(F32) + part).astype(BF)

        return start, finish

    add_normed([block(js) for js in blocks_of(n_groups, n * share)])


def blocks_of(n_groups, rows):
    size = max(1, min(n_groups, 2 * TILE // rows))
    return [range(at, min(at + size, n_groups)) for at in range(0, n_groups, size)]


def paired(chunks, lanes, frames):
    return chunks % 2 == 0 and frames % 2 == 0 and 2 * lanes == TILE


def slot(c, frame, chunks, n_groups, frames):
    return c ^ (frame & 1) if paired(chunks, n_groups * SUB, frames) else c


def project(w_ref, x, out):
    width = w_ref.shape[0] // 3
    cut = w_ref.shape[0] // 2
    heads = width // HEAD_DIM
    parts = [contract(w_ref[i * cut:(i + 1) * cut, :], x, 1, 1) for i in range(2)]
    for h in range(3 * heads):
        i, at = divmod(h * HEAD_DIM, cut)
        y = parts[i][at:at + HEAD_DIM, :]
        if h < 2 * heads:
            y = y * head_scale(y)
        pad = jnp.full((8, y.shape[1]), 0.0 if h < 2 * heads else 1.0, F32)
        out[sums(h), :] = jnp.concatenate([y, pad], axis=0).astype(BF)


def project_kernel(frame, frames, *refs):
    pieces, w_ref, out, x = refs[:-3], refs[-3], refs[-2], refs[-1]
    n_groups = len(pieces)
    chunks = pieces[0].shape[1] // SUB
    for c in range(chunks):
        for j, piece in enumerate(pieces):
            at = (slot(c, frame, chunks, n_groups, frames) * n_groups + j) * SUB
            x[at:at + SUB, :] = piece[0, c * SUB:(c + 1) * SUB, :]
    project(w_ref, x[...], out)


def late_project_kernel(frame, frames, *refs):
    n_groups = (len(refs) - 7) // 2
    atts, hids = refs[:n_groups], refs[n_groups:2 * n_groups]
    w_ref, g_ref, qkv_ref, out, a, b, x = refs[2 * n_groups:]
    width = w_ref.shape[0]
    n = hids[0].shape[0]
    rows = atts[0].shape[0]
    chunks = rows // SUB
    for f in range(n):
        for c in range(chunks):
            for j in range(n_groups):
                at = ((f * chunks + slot(c, frame + f, chunks, n_groups, frames)) * n_groups + j) * SUB
                piece = slice(c * SUB, (c + 1) * SUB)
                a[at:at + SUB, :] = atts[j][piece, f * width:(f + 1) * width]
                b[at:at + SUB, :] = hids[j][f, piece, :]

    def finish(normed):
        x[...] = (b[...].astype(F32) + normed * g_ref[...]).astype(BF)

    add_normed([(lambda: contract(a[...], w_ref[...], 1, 0), finish)])
    project(qkv_ref, x[...], out)


def temporal_kernel(n_groups, late, half, span, *refs):
    early_refs, late_ref = refs[:-n_groups - 2], refs[-n_groups - 2]
    outs, att = refs[-n_groups - 1:-1], refs[-1]
    early = len(early_refs)
    frames = early + late
    ins = [(ref, half * span) for ref in early_refs] + [(late_ref, f * span) for f in range(late)]
    lanes = n_groups * SUB
    chunks = span // lanes
    heads = late_ref.shape[0] // 3 // (HEAD_DIM + 8)
    width = heads * HEAD_DIM
    rows = frames * lanes
    pair = paired(chunks, lanes, frames)
    row_pos = lax.broadcasted_iota(jnp.int32, (rows, rows), 0) % SUB
    col_pos = lax.broadcasted_iota(jnp.int32, (rows, rows), 1) % SUB
    same = jnp.where(row_pos == col_pos, 1.0, 0.0).astype(BF)
    low = lax.broadcasted_iota(jnp.int32, (HEAD_DIM + 8, TILE), 1) < lanes

    def take(c, where):
        if not pair:
            return jnp.concatenate(
                [r[where, at + c * lanes:at + (c + 1) * lanes] for r, at in ins], axis=1
            )
        got = [r[where, at + c // 2 * TILE:at + (c // 2 + 1) * TILE] for r, at in ins]
        return jnp.concatenate(
            [
                jnp.where(low, got[m + (c & 1)], got[m + 1 - (c & 1)])
                for m in range(0, frames, 2)
            ],
            axis=1,
        )

    def scores(c, h):
        return contract(take(c, sums(heads + h)), take(c, sums(h)), 0, 0)

    def weigh(s):
        return jnp.exp2(s * EXP2_SCALE).astype(BF) * same

    def gather(c, h, p):
        att[c, head(h), :] = averaged(contract(take(c, sums(2 * heads + h)), p, 1, 0)).astype(BF)
        if h + 1 == heads:
            turn(c)

    def turn(c):
        turned = att[c].T
        for j, out in enumerate(outs):
            for f in range(frames):
                at = (f ^ (c & 1) if pair else f) * lanes + j * SUB
                out[c * SUB:(c + 1) * SUB, f * width:(f + 1) * width] = turned[at:at + SUB, :]

    steps = [(c, h) for c in range(chunks) for h in range(heads)]
    pipeline(steps, scores, weigh, gather)


def output_kernel(n_groups, js, early, half, halves, before, last, aliased, place, *refs):
    n = len(js)
    atts, pieces = refs[:n], refs[n:n * (1 + early)]
    late_ref, w_ref, g_ref = refs[n * (1 + early):n * (1 + early) + 3]
    rest = list(refs[n * (1 + early) + 3:])
    handed = rest.pop(0) if before else None
    rest = rest[aliased:]
    out = rest.pop(0) if before or last else None
    buf = rest.pop(0)
    late = late_ref.shape[1]
    rows = atts[0].shape[0]
    cut = slice(half * rows, (half + 1) * rows)
    width = w_ref.shape[0]
    frames = early + late
    copies = []

    def write(src, j, some_half):
        group = peer(place[0], j, n_groups)
        at = pl.multiple_of((group * halves + some_half) * rows, SUB)
        copy = pltpu.make_async_copy(src, out.at[:, pl.ds(at, rows), :], rest[0].at[len(copies)])
        copy.start()
        copies.append(copy)

    if before:
        for i, j in enumerate(before[0]):
            write(handed.at[i], j, before[1])

    def block(some):
        def start():
            x = [atts[i][:, f * width:(f + 1) * width] for i in some for f in range(frames)]
            return contract(jnp.concatenate(x, axis=0), w_ref[...], 1, 0)

        def finish(normed):
            for k, i in enumerate(some):
                j = js[i]
                for f in range(frames):
                    mine = pieces[i * early + f][0, cut, :] if f < early else late_ref[j, f - early, cut, :]
                    at = (k * frames + f) * rows
                    part = normed[at:at + rows, :] * g_ref[...]
                    buf[i, f] = (mine.astype(F32) + part).astype(BF)
                if last:
                    write(buf.at[i], j, half)

        return start, finish

    add_normed([block(some) for some in blocks_of(n, frames * rows)])
    for copy in copies:
        copy.wait()


def shards(
    spatial_queries,
    spatial_keys,
    spatial_values,
    hidden,
    spatial_out_weight,
    spatial_gain,
    temporal_qkv_weight,
    temporal_out_weight,
    temporal_gain,
    tile_list,
    tile_count,
):
    frames, tokens, width = spatial_queries.shape
    model = hidden.shape[2]
    groups = lax.axis_size("frame")
    strips = lax.axis_size("strip")
    share = tokens // groups
    halves = 2 if share % (4 * SUB) == 0 else 1
    rows = share // halves
    queries = pltpu.with_memory_space_constraint(jnp.transpose(spatial_queries, (0, 2, 1)), pltpu.HBM)
    keys = pltpu.with_memory_space_constraint(jnp.transpose(spatial_keys, (0, 2, 1)), pltpu.HBM)
    values = pltpu.with_memory_space_constraint(jnp.transpose(spatial_values, (0, 2, 1)), pltpu.HBM)
    hidden_far = pltpu.with_memory_space_constraint(hidden, pltpu.HBM)
    lists = jnp.transpose(tile_list, (2, 1, 0))
    counts = tile_count.T
    qkv_weight = temporal_qkv_weight.T
    gain_one = spatial_gain.reshape(1, model)
    gain_two = temporal_gain.reshape(1, model)
    place = jnp.stack([lax.axis_index("frame"), lax.axis_index("strip")]).astype(jnp.int32)
    near = [(i, i ^ 1) for i in range(strips) if i ^ 1 < strips]
    far = [e for i in range(1, strips - 1, 2) for e in ((i, i + 1), (i + 1, i))]
    edge = jax.ShapeDtypeStruct((2 * width, TILE), BF)
    smem = pl.BlockSpec(memory_space=pltpu.SMEM)
    any_spec = pl.BlockSpec(memory_space=pl.ANY)

    def call(kernel, in_specs, out_specs, out_shape, scratch=(), limit=32, prefetch=0, alias=None):
        return pl.pallas_call(
            kernel,
            grid_spec=pltpu.PrefetchScalarGridSpec(
                num_scalar_prefetch=prefetch,
                grid=(1,),
                in_specs=in_specs,
                out_specs=out_specs,
                scratch_shapes=list(scratch),
            ),
            out_shape=out_shape,
            input_output_aliases=alias or {},
            compiler_params=vmem(limit),
        )

    late = frames // 2
    early = frames - late

    def out_pairs(j):
        return [(i, peer(i, j, groups)) for i in range(groups)]

    def send(parts):
        sent = {}
        for j in range(1, groups):
            sent[j] = lax.ppermute(parts[j], "frame", out_pairs(j))
        return [parts[0]] + [sent[j] for j in range(1, groups)]

    halos = []
    for some in range(2):
        block = pl.BlockSpec((late, width, tokens), lambda *_, some=some: (some, 0, 0))
        split = groups if some == 1 else 0
        a, b, *pieces = call(
            prep_kernel,
            [smem, block, block] + [any_spec] * bool(split),
            [whole((late,) + edge.shape)] * 2 + [any_spec] * split,
            [jax.ShapeDtypeStruct((late,) + edge.shape, BF)] * 2
            + [jax.ShapeDtypeStruct((late, share, model), BF)] * split,
            [pltpu.SemaphoreType.DMA((groups,))] * bool(split),
            limit=16,
        )(place, keys, values, *[hidden_far] * bool(split))
        if split:
            own_hidden = pieces
        halos.append((a, b, lax.ppermute(a, "strip", near), lax.ppermute(b, "strip", far)))
    far_hidden = send(own_hidden)

    padded = width // HEAD_DIM * (HEAD_DIM + 8)
    qkv_rows = 3 * padded
    sum_shape = (late, padded, tokens)
    own_sums = []
    for some in range(2):
        block = pl.BlockSpec((late, width, tokens), lambda *_, some=some: (some, 0, 0))
        own_sums.append(
            call(
                functools.partial(local_kernel, some * late),
                [smem, smem, smem, block] + [whole((late,) + edge.shape)] * 2,
                [whole((late, width, tokens)), whole(sum_shape)],
                [
                    jax.ShapeDtypeStruct((late, width, tokens), BF),
                    jax.ShapeDtypeStruct(sum_shape, F32),
                ],
            )(place, counts, lists, queries, *halos[some][:2])
        )
    sum_specs = [whole((late, width, tokens)), whole(sum_shape)]

    def one(shape, f):
        return pl.BlockSpec((1,) + shape[1:], lambda *_: (f, 0, 0))

    mixed, projected = [], []
    for f in range(early):
        mixed.append(
            call(
                functools.partial(spatial_kernel, f, groups),
                [smem, smem, smem, one((late, width, tokens), f), one(sum_shape, f)]
                + [one((late,) + edge.shape, f)] * 2
                + [one(hidden.shape, f), whole((width, model)), whole((1, model))],
                [whole((1, share, model))] * groups,
                [jax.ShapeDtypeStruct((1, share, model), BF)] * groups,
                [
                    pltpu.VMEM((1, width, tokens), BF),
                    pltpu.VMEM((1, tokens, model), BF),
                ],
            )(place, counts, lists, *own_sums[0], *halos[0][2:], hidden, spatial_out_weight, gain_one)
        )
        arrived = send(mixed[f])
        projected.append(
            call(
                functools.partial(project_kernel, f, frames),
                [whole((1, share, model))] * groups + [whole((3 * width, model))],
                whole((qkv_rows, tokens)),
                jax.ShapeDtypeStruct((qkv_rows, tokens), BF),
                [pltpu.VMEM((tokens, model), BF)],
            )(*arrived, qkv_weight)
        )

    late_shape = (rows, late * width)
    own_late = call(
        functools.partial(late_kernel, early, groups, halves),
        [smem, smem, smem] + sum_specs + [whole((late,) + edge.shape)] * 2,
        [whole(late_shape)] * (groups * halves),
        [jax.ShapeDtypeStruct(late_shape, BF)] * (groups * halves),
        [pltpu.VMEM((late, width, tokens), BF), pltpu.VMEM((tokens, late * width), BF)],
    )(place, counts, lists, *own_sums[1], *halos[1][2:])
    own_late = [own_late[half * groups:(half + 1) * groups] for half in range(halves)]
    far_late = []
    for half in range(halves):
        far_late.append(send(own_late[half]))

    returned = []
    back_shape = (rows, frames * width)
    lanes = tokens // halves
    for half in range(halves):
        hid_block = pl.BlockSpec((late, rows, model), lambda *_, half=half: (0, half, 0))
        late_specs = [whole(late_shape)] * groups + [hid_block] * groups
        late_specs += [whole((width, model)), whole((1, model))]
        late_projected = call(
            functools.partial(late_project_kernel, early, frames),
            late_specs + [whole((3 * width, model))],
            whole((qkv_rows, late * lanes)),
            jax.ShapeDtypeStruct((qkv_rows, late * lanes), BF),
            [
                pltpu.VMEM((late * lanes, width), BF),
                pltpu.VMEM((late * lanes, model), BF),
                pltpu.VMEM((late * lanes, model), BF),
            ],
        )(*far_late[half], *far_hidden, spatial_out_weight, gain_one, qkv_weight)
        back = call(
            functools.partial(temporal_kernel, groups, late, half, lanes),
            [whole((qkv_rows, tokens))] * early + [whole((qkv_rows, late * lanes))],
            [whole(back_shape)] * groups,
            [jax.ShapeDtypeStruct(back_shape, BF)] * groups,
            [pltpu.VMEM((rows // SUB, width, groups * frames * SUB), BF)],
        )(*projected, late_projected)
        home = {}
        for j in range(1, groups):
            home[j] = lax.ppermute(back[j], "frame", [(b, a) for a, b in out_pairs(j)])
        returned.append([back[0]] + [home[j] for j in range(1, groups)])

    late_mixed = call(
        mix_kernel,
        [whole(late_shape)] * (groups * halves)
        + [whole((late, share, model))] * groups
        + [whole((width, model)), whole((1, model))],
        whole((groups, late, share, model)),
        jax.ShapeDtypeStruct((groups, late, share, model), BF),
    )(*[x for some in own_late for x in some], *own_hidden, spatial_out_weight, gain_one)

    tail = max(1, groups // 4)
    order = tuple(range(groups))
    calls = [(order, half) for half in range(halves - 1)]
    calls += [(js, halves - 1) for js in (order[:2], order[2:-tail], order[max(2, groups - tail):]) if js]
    result = jax.ShapeDtypeStruct((frames, tokens, model), BF)
    out = handed = before = None
    for n, (js, half) in enumerate(calls):
        last = n + 1 == len(calls)
        rows_shape = (len(js), frames, rows, model)
        extra = [] if out is None else [out]
        writes = (len(before[0]) if before else 0) + (len(js) if last else 0)
        in_specs = (
            [smem]
            + [whole(back_shape)] * len(js)
            + [whole((1, share, model))] * (len(js) * early)
            + [whole((groups, late, share, model)), whole((width, model)), whole((1, model))]
            + ([whole(handed.shape)] if before else [])
            + [any_spec] * len(extra)
        )
        outs = ([any_spec], [result]) if before or last else ([], [])
        kept = ([], []) if last else ([whole(rows_shape)], [jax.ShapeDtypeStruct(rows_shape, BF)])
        scratch = [pltpu.VMEM(rows_shape, BF)] * last + [pltpu.SemaphoreType.DMA((writes,))] * bool(writes)
        got = call(
            functools.partial(output_kernel, groups, js, early, half, halves, before, last, len(extra)),
            in_specs,
            outs[0] + kept[0],
            outs[1] + kept[1],
            scratch,
            alias={len(in_specs) - 1: 0} if extra else None,
        )(
            place,
            *[returned[half][j] for j in js],
            *[mixed[f][j] for j in js for f in range(early)],
            late_mixed,
            temporal_out_weight,
            gain_two,
            *([handed] if before else []),
            *extra,
        )
        got = list(got)
        out = got.pop(0) if before or last else None
        handed = None if last else got[0]
        before = (js, half)
    return out


def solution(mesh):
    rows = P(("group", "frame"), "strip", None)
    placed = (rows, rows, rows, rows, P(), P(), P(), P(), P(), rows, P(("group", "frame"), "strip"))

    return jax.shard_map(shards, mesh=mesh, in_specs=placed, out_specs=rows, check_vma=False)
```

```python
import functools
import math

import jax
import jax.numpy as jnp
from jax import lax
from jax.experimental import pallas as pl
from jax.experimental.pallas import tpu as pltpu
from jax.sharding import PartitionSpec as P


HEAD_DIM = 72
TILE = 128
MAXT = 3
SUB = 16
EPS = 1e-06
EXP2_SCALE = HEAD_DIM ** -0.5 * math.log2(math.e)

BF = jnp.bfloat16
F32 = jnp.float32


def peer(i, j, n):
    return i ^ j if n & (n - 1) == 0 else (i + j) % n


def vmem(limit):
    return pltpu.CompilerParams(vmem_limit_bytes=limit << 20)


def whole(shape):
    return pl.BlockSpec(shape, lambda *_: (0,) * len(shape))


def contract(a, b, da, db):
    return lax.dot_general(a, b, (((da,), (db,)), ((), ())), preferred_element_type=F32)


def head_scale(x):
    return lax.rsqrt(jnp.mean(x * x, axis=0, keepdims=True) + EPS)


def head(h, base=0):
    return slice(base + h * HEAD_DIM, base + (h + 1) * HEAD_DIM)


def with_ones(v):
    return jnp.concatenate([v, jnp.ones((8, v.shape[1]), v.dtype)], axis=0)


def averaged(o):
    return o[:HEAD_DIM, :] / o[HEAD_DIM:HEAD_DIM + 1, :]


def pipeline(steps, scores, weigh, gather):
    ahead, behind = scores(*steps[0]), None
    for n, step in enumerate(steps):
        now = ahead
        if n + 1 < len(steps):
            ahead = scores(*steps[n + 1])
        weighed = weigh(now)
        if behind is not None:
            gather(*steps[n - 1], behind)
        behind = weighed
    gather(*steps[-1], behind)


def prep_kernel(k_ref, v_ref, *refs):
    n, width, _ = k_ref.shape
    even = lax.axis_index("strip") % 2 == 0
    copies = []
    if len(refs) > 2:
        src, (a_ref, b_ref), pieces, sems = refs[0], refs[1:3], refs[3:-1], refs[-1]
        late, share, _ = pieces[0].shape
        for j in reversed(range(len(pieces))):
            start = pl.multiple_of(peer(lax.axis_index("frame"), j, len(pieces)) * share, SUB)
            part = src.at[pl.ds(src.shape[0] - late, late), pl.ds(start, share), :]
            copies.append(pltpu.make_async_copy(part, pieces[j], sems.at[j]))
            copies[-1].start()
    else:
        a_ref, b_ref = refs

    def fill(first, second):
        for f in range(n):
            for h in range(width // HEAD_DIM):
                x = k_ref[f, head(h), :].astype(F32)
                y = (x * head_scale(x)).astype(BF)
                first[f, head(h), :] = y[:, :TILE]
                second[f, head(h), :] = y[:, TILE:]
            first[f, width:, :] = v_ref[f, :, :TILE]
            second[f, width:, :] = v_ref[f, :, TILE:]

    pl.when(even)(functools.partial(fill, b_ref, a_ref))
    pl.when(jnp.logical_not(even))(functools.partial(fill, a_ref, b_ref))
    for copy in copies:
        copy.wait()


def tile_masks(frame, n, tiles, local, counts, lists):
    strip = lax.axis_index("strip")
    odd = strip % 2
    first = strip * tiles
    if local:
        spots = (first + 1 - odd, first + odd)
    else:
        spots = (first + 2 - 3 * odd, first - 1 + 3 * odd)
    masks = []
    for f in range(n):
        rows = []
        for spot in spots:
            cells = []
            for t in range(tiles):
                hit = jnp.bool_(False)
                for j in range(MAXT):
                    hit = hit | ((lists[j, t, frame + f] == spot) & (j < counts[t, frame + f]))
                cells.append(jnp.full((SUB, TILE), jnp.where(hit, 1.0, 0.0), F32))
            rows.append(jnp.concatenate(cells, axis=1).astype(BF))
        masks.append(rows)
    return masks


def attend(masks, keys, query, finish):
    n = keys[0].shape[0]
    width = keys[0].shape[1] // 2

    def scores(f, h):
        qn = query(f, h)
        return f, [contract(ref[f, head(h), :], qn, 0, 0) for ref in keys]

    def weigh(scored):
        f, s = scored
        packed = []
        for mask, x in zip(masks[f], s):
            p = jnp.exp2(x * EXP2_SCALE).astype(BF).reshape(TILE // SUB, SUB, x.shape[1])
            packed.append((p * mask).reshape(x.shape))
        return jnp.concatenate(packed, axis=0)

    def gather(f, h, weights):
        v = jnp.concatenate([ref[f, head(h, width), :] for ref in keys], axis=1)
        finish(f, h, contract(with_ones(v), weights, 1, 0))

    pipeline([(f, h) for f in range(n) for h in range(width // HEAD_DIM)], scores, weigh, gather)


def sums(h):
    return slice(h * (HEAD_DIM + 8), (h + 1) * (HEAD_DIM + 8))


def local_kernel(frame, counts, lists, q_ref, a_ref, b_ref, qn_ref, sum_ref, mask_ref):
    n, _, tokens = q_ref.shape

    def query(f, h):
        q = q_ref[f, head(h), :].astype(F32)
        qn = (q * head_scale(q)).astype(BF)
        qn_ref[f, head(h), :] = qn
        return qn

    def finish(f, h, o):
        sum_ref[f, sums(h), :] = o

    for f, rows in enumerate(tile_masks(frame, n, tokens // TILE, False, counts, lists)):
        for i, row in enumerate(rows):
            mask_ref[f, i] = row
    masks = tile_masks(frame, n, tokens // TILE, True, counts, lists)
    attend(masks, (a_ref, b_ref), query, finish)


def remote_attend(qn_ref, sum_ref, mask_ref, ra_ref, rb_ref, att, done=None):
    n, width, _ = qn_ref.shape

    def query(f, h):
        return qn_ref[f, head(h), :]

    def finish(f, h, o):
        att[f, head(h), :] = averaged(o + sum_ref[f, sums(h), :]).astype(att.dtype)
        if done and (h + 1) * HEAD_DIM == width:
            done(f)

    masks = [[mask_ref[f, i] for i in range(2)] for f in range(n)]
    attend(masks, (ra_ref, rb_ref), query, finish)


def add_normed(blocks):
    ahead = blocks[0][0]()
    for n, (_, finish) in enumerate(blocks):
        proj = ahead
        if n + 1 < len(blocks):
            ahead = blocks[n + 1][0]()
        scale = lax.rsqrt(jnp.mean(proj * proj, axis=-1, keepdims=True) + EPS)
        finish(proj * scale)


def spatial_kernel(n_groups, qn_ref, sum_ref, mask_ref, ra_ref, rb_ref, h_ref, w_ref, g_ref, *rest):
    outs, (att, mix) = rest[:n_groups], rest[n_groups:]
    remote_attend(qn_ref, sum_ref, mask_ref, ra_ref, rb_ref, att)
    n, tokens, _ = h_ref.shape

    def block(f):
        def finish(normed):
            mix[f] = (h_ref[f].astype(F32) + normed * g_ref[...]).astype(BF)

        return lambda: contract(att[f], w_ref[...], 0, 0), finish

    add_normed([block(f) for f in range(n)])
    share = tokens // n_groups
    for j, out in enumerate(outs):
        group = peer(lax.axis_index("frame"), j, n_groups)
        for f in range(n):
            out[f] = mix[f, pl.ds(pl.multiple_of(group * share, SUB), share), :]


def late_kernel(n_groups, halves, qn_ref, sum_ref, mask_ref, ra_ref, rb_ref, *rest):
    outs, (att, rows) = rest[:n_groups * halves], rest[n_groups * halves:]
    _, width, tokens = qn_ref.shape

    def turn(f):
        rows[:, f * width:(f + 1) * width] = att[f].T

    remote_attend(qn_ref, sum_ref, mask_ref, ra_ref, rb_ref, att, turn)
    size = tokens // n_groups // halves
    for half in range(halves):
        for j in range(n_groups):
            start = (peer(lax.axis_index("frame"), j, n_groups) * halves + half) * size
            outs[half * n_groups + j][...] = rows[pl.ds(pl.multiple_of(start, SUB), size), :]


def mix_kernel(*refs):
    w_ref, g_ref, out = refs[-3:]
    n_groups, n, share, _ = out.shape
    atts, hids = refs[:-3 - n_groups], refs[-3 - n_groups:-3]
    width = w_ref.shape[0]
    rows = atts[0].shape[0]
    halves = share // rows

    def block(js):
        def start():
            x = [
                atts[half * n_groups + j][:, f * width:(f + 1) * width]
                for j in js
                for f in range(n)
                for half in range(halves)
            ]
            return contract(jnp.concatenate(x, axis=0), w_ref[...], 1, 0)

        def finish(normed):
            for i, j in enumerate(js):
                for f in range(n):
                    at = (i * n + f) * share
                    part = normed[at:at + share, :] * g_ref[...]
                    out[j, f] = (hids[j][f].astype(F32) + part).astype(BF)

        return start, finish

    add_normed([block(js) for js in blocks_of(n_groups, n * share)])


def blocks_of(n_groups, rows):
    size = max(1, min(n_groups, 2 * TILE // rows))
    return [range(at, min(at + size, n_groups)) for at in range(0, n_groups, size)]


def paired(chunks, lanes, frames):
    return chunks % 2 == 0 and frames % 2 == 0 and 2 * lanes == TILE


def slot(c, frame, chunks, n_groups, frames):
    return c ^ (frame & 1) if paired(chunks, n_groups * SUB, frames) else c


def project(w_ref, x, out):
    width = w_ref.shape[0] // 3
    cut = w_ref.shape[0] // 2
    heads = width // HEAD_DIM
    parts = [contract(w_ref[i * cut:(i + 1) * cut, :], x, 1, 1) for i in range(2)]
    for h in range(3 * heads):
        i, at = divmod(h * HEAD_DIM, cut)
        y = parts[i][at:at + HEAD_DIM, :]
        if h < 2 * heads:
            y = y * head_scale(y)
        pad = jnp.full((8, y.shape[1]), 0.0 if h < 2 * heads else 1.0, F32)
        out[sums(h), :] = jnp.concatenate([y, pad], axis=0).astype(BF)


def project_kernel(frame, frames, *refs):
    pieces, w_ref, out, x = refs[:-3], refs[-3], refs[-2], refs[-1]
    n_groups = len(pieces)
    chunks = pieces[0].shape[1] // SUB
    for c in range(chunks):
        for j, piece in enumerate(pieces):
            at = (slot(c, frame, chunks, n_groups, frames) * n_groups + j) * SUB
            x[at:at + SUB, :] = piece[0, c * SUB:(c + 1) * SUB, :]
    project(w_ref, x[...], out)


def late_project_kernel(frame, frames, *refs):
    n_groups = (len(refs) - 7) // 2
    atts, hids = refs[:n_groups], refs[n_groups:2 * n_groups]
    w_ref, g_ref, qkv_ref, out, a, b, x = refs[2 * n_groups:]
    width = w_ref.shape[0]
    n = hids[0].shape[0]
    rows = atts[0].shape[0]
    chunks = rows // SUB
    for f in range(n):
        for c in range(chunks):
            for j in range(n_groups):
                at = ((f * chunks + slot(c, frame + f, chunks, n_groups, frames)) * n_groups + j) * SUB
                piece = slice(c * SUB, (c + 1) * SUB)
                a[at:at + SUB, :] = atts[j][piece, f * width:(f + 1) * width]
                b[at:at + SUB, :] = hids[j][f, piece, :]

    def finish(normed):
        x[...] = (b[...].astype(F32) + normed * g_ref[...]).astype(BF)

    add_normed([(lambda: contract(a[...], w_ref[...], 1, 0), finish)])
    project(qkv_ref, x[...], out)


def temporal_kernel(n_groups, late, half, span, *refs):
    early_refs, late_ref = refs[:-n_groups - 2], refs[-n_groups - 2]
    outs, att = refs[-n_groups - 1:-1], refs[-1]
    early = len(early_refs)
    frames = early + late
    ins = [(ref, half * span) for ref in early_refs] + [(late_ref, f * span) for f in range(late)]
    lanes = n_groups * SUB
    chunks = span // lanes
    heads = late_ref.shape[0] // 3 // (HEAD_DIM + 8)
    width = heads * HEAD_DIM
    rows = frames * lanes
    pair = paired(chunks, lanes, frames)
    row_pos = lax.broadcasted_iota(jnp.int32, (rows, rows), 0) % SUB
    col_pos = lax.broadcasted_iota(jnp.int32, (rows, rows), 1) % SUB
    same = jnp.where(row_pos == col_pos, 1.0, 0.0).astype(BF)
    low = lax.broadcasted_iota(jnp.int32, (HEAD_DIM + 8, TILE), 1) < lanes

    def take(c, where):
        if not pair:
            return jnp.concatenate(
                [r[where, at + c * lanes:at + (c + 1) * lanes] for r, at in ins], axis=1
            )
        got = [r[where, at + c // 2 * TILE:at + (c // 2 + 1) * TILE] for r, at in ins]
        return jnp.concatenate(
            [
                jnp.where(low, got[m + (c & 1)], got[m + 1 - (c & 1)])
                for m in range(0, frames, 2)
            ],
            axis=1,
        )

    def scores(c, h):
        return contract(take(c, sums(heads + h)), take(c, sums(h)), 0, 0)

    def weigh(s):
        return jnp.exp2(s * EXP2_SCALE).astype(BF) * same

    def gather(c, h, p):
        att[c, head(h), :] = averaged(contract(take(c, sums(2 * heads + h)), p, 1, 0)).astype(BF)
        if h + 1 == heads:
            turn(c)

    def turn(c):
        turned = att[c].T
        for j, out in enumerate(outs):
            for f in range(frames):
                at = (f ^ (c & 1) if pair else f) * lanes + j * SUB
                out[c * SUB:(c + 1) * SUB, f * width:(f + 1) * width] = turned[at:at + SUB, :]

    steps = [(c, h) for c in range(chunks) for h in range(heads)]
    pipeline(steps, scores, weigh, gather)


def output_kernel(n_groups, js, early, half, halves, before, last, aliased, *refs):
    n = len(js)
    atts, pieces = refs[:n], refs[n:n * (1 + early)]
    late_ref, w_ref, g_ref = refs[n * (1 + early):n * (1 + early) + 3]
    rest = list(refs[n * (1 + early) + 3:])
    handed = rest.pop(0) if before else None
    rest = rest[aliased:]
    out = rest.pop(0) if before or last else None
    buf = rest.pop(0)
    late = late_ref.shape[1]
    rows = atts[0].shape[0]
    cut = slice(half * rows, (half + 1) * rows)
    width = w_ref.shape[0]
    frames = early + late
    copies = []

    def write(src, j, some_half):
        group = peer(lax.axis_index("frame"), j, n_groups)
        at = pl.multiple_of((group * halves + some_half) * rows, SUB)
        copy = pltpu.make_async_copy(src, out.at[:, pl.ds(at, rows), :], rest[0].at[len(copies)])
        copy.start()
        copies.append(copy)

    if before:
        for i, j in enumerate(before[0]):
            write(handed.at[i], j, before[1])

    def block(some):
        def start():
            x = [atts[i][:, f * width:(f + 1) * width] for i in some for f in range(frames)]
            return contract(jnp.concatenate(x, axis=0), w_ref[...], 1, 0)

        def finish(normed):
            for k, i in enumerate(some):
                j = js[i]
                for f in range(frames):
                    mine = pieces[i * early + f][0, cut, :] if f < early else late_ref[j, f - early, cut, :]
                    at = (k * frames + f) * rows
                    part = normed[at:at + rows, :] * g_ref[...]
                    buf[i, f] = (mine.astype(F32) + part).astype(BF)
                if last:
                    write(buf.at[i], j, half)

        return start, finish

    add_normed([block(some) for some in blocks_of(n, frames * rows)])
    for copy in copies:
        copy.wait()


def shards(
    spatial_queries,
    spatial_keys,
    spatial_values,
    hidden,
    spatial_out_weight,
    spatial_gain,
    temporal_qkv_weight,
    temporal_out_weight,
    temporal_gain,
    tile_list,
    tile_count,
):
    frames, tokens, width = spatial_queries.shape
    model = hidden.shape[2]
    groups = lax.axis_size("frame")
    strips = lax.axis_size("strip")
    share = tokens // groups
    halves = 2 if share % (4 * SUB) == 0 else 1
    rows = share // halves
    queries = pltpu.with_memory_space_constraint(jnp.transpose(spatial_queries, (0, 2, 1)), pltpu.HBM)
    keys = pltpu.with_memory_space_constraint(jnp.transpose(spatial_keys, (0, 2, 1)), pltpu.HBM)
    values = pltpu.with_memory_space_constraint(jnp.transpose(spatial_values, (0, 2, 1)), pltpu.HBM)
    hidden_far = pltpu.with_memory_space_constraint(hidden, pltpu.HBM)
    lists = jnp.transpose(tile_list, (2, 1, 0))
    counts = tile_count.T
    qkv_weight = temporal_qkv_weight.T
    gain_one = spatial_gain.reshape(1, model)
    gain_two = temporal_gain.reshape(1, model)
    near = [(i, i ^ 1) for i in range(strips) if i ^ 1 < strips]
    far = [e for i in range(1, strips - 1, 2) for e in ((i, i + 1), (i + 1, i))]
    edge = jax.ShapeDtypeStruct((2 * width, TILE), BF)
    smem = pl.BlockSpec(memory_space=pltpu.SMEM)
    any_spec = pl.BlockSpec(memory_space=pl.ANY)

    def call(kernel, in_specs, out_specs, out_shape, scratch=(), limit=32, prefetch=0, alias=None):
        return pl.pallas_call(
            kernel,
            grid_spec=pltpu.PrefetchScalarGridSpec(
                num_scalar_prefetch=prefetch,
                grid=(1,),
                in_specs=in_specs,
                out_specs=out_specs,
                scratch_shapes=list(scratch),
            ),
            out_shape=out_shape,
            input_output_aliases=alias or {},
            compiler_params=vmem(limit),
        )

    late = frames // 2
    early = frames - late

    def out_pairs(j):
        return [(i, peer(i, j, groups)) for i in range(groups)]

    def send(parts):
        sent = {}
        for j in range(1, groups):
            sent[j] = lax.ppermute(parts[j], "frame", out_pairs(j))
        return [parts[0]] + [sent[j] for j in range(1, groups)]

    halos = []
    for some in range(2):
        block = pl.BlockSpec((late, width, tokens), lambda *_, some=some: (some, 0, 0))
        split = groups if some == 1 else 0
        a, b, *pieces = call(
            prep_kernel,
            [block, block] + [any_spec] * bool(split),
            [whole((late,) + edge.shape)] * 2 + [any_spec] * split,
            [jax.ShapeDtypeStruct((late,) + edge.shape, BF)] * 2
            + [jax.ShapeDtypeStruct((late, share, model), BF)] * split,
            [pltpu.SemaphoreType.DMA((groups,))] * bool(split),
            limit=16,
        )(keys, values, *[hidden_far] * bool(split))
        if split:
            own_hidden = pieces
        halos.append((a, b, lax.ppermute(a, "strip", near), lax.ppermute(b, "strip", far)))
    far_hidden = send(own_hidden)

    padded = width // HEAD_DIM * (HEAD_DIM + 8)
    qkv_rows = 3 * padded
    sum_shape = (late, padded, tokens)
    mask_shape = (late, 2, SUB, tokens)
    own_sums = []
    for some in range(2):
        block = pl.BlockSpec((late, width, tokens), lambda *_, some=some: (some, 0, 0))
        own_sums.append(
            call(
                functools.partial(local_kernel, some * late),
                [smem, smem, block] + [whole((late,) + edge.shape)] * 2,
                [whole((late, width, tokens)), whole(sum_shape), whole(mask_shape)],
                [
                    jax.ShapeDtypeStruct((late, width, tokens), BF),
                    jax.ShapeDtypeStruct(sum_shape, F32),
                    jax.ShapeDtypeStruct(mask_shape, BF),
                ],
            )(counts, lists, queries, *halos[some][:2])
        )
    sum_specs = [whole((late, width, tokens)), whole(sum_shape), whole(mask_shape)]

    def one(shape, f):
        return pl.BlockSpec((1,) + shape[1:], lambda *_: (f,) + (0,) * (len(shape) - 1))

    mixed, projected = [], []
    for f in range(early):
        mixed.append(
            call(
                functools.partial(spatial_kernel, groups),
                [one((late, width, tokens), f), one(sum_shape, f), one(mask_shape, f)]
                + [one((late,) + edge.shape, f)] * 2
                + [one(hidden.shape, f), whole((width, model)), whole((1, model))],
                [whole((1, share, model))] * groups,
                [jax.ShapeDtypeStruct((1, share, model), BF)] * groups,
                [
                    pltpu.VMEM((1, width, tokens), BF),
                    pltpu.VMEM((1, tokens, model), BF),
                ],
            )(*own_sums[0], *halos[0][2:], hidden, spatial_out_weight, gain_one)
        )
        arrived = send(mixed[f])
        projected.append(
            call(
                functools.partial(project_kernel, f, frames),
                [whole((1, share, model))] * groups + [whole((3 * width, model))],
                whole((qkv_rows, tokens)),
                jax.ShapeDtypeStruct((qkv_rows, tokens), BF),
                [pltpu.VMEM((tokens, model), BF)],
            )(*arrived, qkv_weight)
        )

    late_shape = (rows, late * width)
    own_late = call(
        functools.partial(late_kernel, groups, halves),
        sum_specs + [whole((late,) + edge.shape)] * 2,
        [whole(late_shape)] * (groups * halves),
        [jax.ShapeDtypeStruct(late_shape, BF)] * (groups * halves),
        [pltpu.VMEM((late, width, tokens), BF), pltpu.VMEM((tokens, late * width), BF)],
    )(*own_sums[1], *halos[1][2:])
    own_late = [own_late[half * groups:(half + 1) * groups] for half in range(halves)]
    far_late = []
    for half in range(halves):
        far_late.append(send(own_late[half]))

    returned = []
    back_shape = (rows, frames * width)
    lanes = tokens // halves
    for half in range(halves):
        hid_block = pl.BlockSpec((late, rows, model), lambda *_, half=half: (0, half, 0))
        late_specs = [whole(late_shape)] * groups + [hid_block] * groups
        late_specs += [whole((width, model)), whole((1, model))]
        late_projected = call(
            functools.partial(late_project_kernel, early, frames),
            late_specs + [whole((3 * width, model))],
            whole((qkv_rows, late * lanes)),
            jax.ShapeDtypeStruct((qkv_rows, late * lanes), BF),
            [
                pltpu.VMEM((late * lanes, width), BF),
                pltpu.VMEM((late * lanes, model), BF),
                pltpu.VMEM((late * lanes, model), BF),
            ],
        )(*far_late[half], *far_hidden, spatial_out_weight, gain_one, qkv_weight)
        back = call(
            functools.partial(temporal_kernel, groups, late, half, lanes),
            [whole((qkv_rows, tokens))] * early + [whole((qkv_rows, late * lanes))],
            [whole(back_shape)] * groups,
            [jax.ShapeDtypeStruct(back_shape, BF)] * groups,
            [pltpu.VMEM((rows // SUB, width, groups * frames * SUB), BF)],
        )(*projected, late_projected)
        home = {}
        for j in range(1, groups):
            home[j] = lax.ppermute(back[j], "frame", [(b, a) for a, b in out_pairs(j)])
        returned.append([back[0]] + [home[j] for j in range(1, groups)])

    late_mixed = call(
        mix_kernel,
        [whole(late_shape)] * (groups * halves)
        + [whole((late, share, model))] * groups
        + [whole((width, model)), whole((1, model))],
        whole((groups, late, share, model)),
        jax.ShapeDtypeStruct((groups, late, share, model), BF),
    )(*[x for some in own_late for x in some], *own_hidden, spatial_out_weight, gain_one)

    tail = max(1, groups // 4)
    order = tuple(range(groups))
    calls = [(order, half) for half in range(halves - 1)]
    calls += [(js, halves - 1) for js in (order[:2], order[2:-tail], order[max(2, groups - tail):]) if js]
    result = jax.ShapeDtypeStruct((frames, tokens, model), BF)
    out = handed = before = None
    for n, (js, half) in enumerate(calls):
        last = n + 1 == len(calls)
        rows_shape = (len(js), frames, rows, model)
        extra = [] if out is None else [out]
        writes = (len(before[0]) if before else 0) + (len(js) if last else 0)
        in_specs = (
            [whole(back_shape)] * len(js)
            + [whole((1, share, model))] * (len(js) * early)
            + [whole((groups, late, share, model)), whole((width, model)), whole((1, model))]
            + ([whole(handed.shape)] if before else [])
            + [any_spec] * len(extra)
        )
        outs = ([any_spec], [result]) if before or last else ([], [])
        kept = ([], []) if last else ([whole(rows_shape)], [jax.ShapeDtypeStruct(rows_shape, BF)])
        scratch = [pltpu.VMEM(rows_shape, BF)] * last + [pltpu.SemaphoreType.DMA((writes,))] * bool(writes)
        got = call(
            functools.partial(output_kernel, groups, js, early, half, halves, before, last, len(extra)),
            in_specs,
            outs[0] + kept[0],
            outs[1] + kept[1],
            scratch,
            alias={len(in_specs) - 1: 0} if extra else None,
        )(
            *[returned[half][j] for j in js],
            *[mixed[f][j] for j in js for f in range(early)],
            late_mixed,
            temporal_out_weight,
            gain_two,
            *([handed] if before else []),
            *extra,
        )
        got = list(got)
        out = got.pop(0) if before or last else None
        handed = None if last else got[0]
        before = (js, half)
    return out


def solution(mesh):
    rows = P(("group", "frame"), "strip", None)
    placed = (rows, rows, rows, rows, P(), P(), P(), P(), P(), rows, P(("group", "frame"), "strip"))

    return jax.shard_map(shards, mesh=mesh, in_specs=placed, out_specs=rows, check_vma=False)
```
